256 devices in a mesh: group: 32 (over y, z_hi, core), tensor: 8 (over z_lo, x).
Axes of the slice: x: 4, y: 4, z: 8 (z_hi: 4, z_lo: 2; z = z_hi * 2 + z_lo), core: 2. Of those that a mesh axis runs over, the one named last changes fastest.
Arguments:
- span_rows: bfloat16 [49152, 2048], P('group', 'tensor'), may hold values from -80 to 80
- norm_gain: float32 [2048], replicated, may hold values from 0.1 to 1.9
- q_weight: bfloat16 [2048, 2048], P(None, 'tensor'), may hold values from -0.125 to 0.125
- gate_weight: bfloat16 [2048, 2048], P(None, 'tensor'), may hold values from -0.125 to 0.125
- k_weight: bfloat16 [2048, 1024], P(None, 'tensor'), may hold values from -0.125 to 0.125
- v_weight: bfloat16 [2048, 1024], P(None, 'tensor'), may hold values from -0.125 to 0.125
- q_norm_gain: float32 [128], replicated, may hold values from 1 to 150
- k_norm_gain: float32 [128], replicated, may hold values from 1 to 2.5
- o_weight: bfloat16 [2048, 2048], P('tensor'), may hold values from -0.125 to 0.125
- key_cache: bfloat16 [32, 64, 128, 1024], P('group', None, None, 'tensor'), may hold values from -6 to 6
- value_cache: bfloat16 [32, 64, 128, 1024], P('group', None, None, 'tensor'), may hold values from -6 to 6
- holders: int32 [768, 1], replicated, may hold values from 0 to 31; in each aligned block of 24 rows (0 to 23, 24 to 47, ...) at most 2 rows name the same one
- prefix_lengths: int32 [768], replicated, may hold values from 1 to 128, 49152 in all
Outputs:
- attn_out: bfloat16 [49152, 2048], P(('group', 'tensor'))
The draws below stay inside these ranges and needn't reach their ends.
Inputs may be any that keep to these rules, and one draw needn't show every extreme that they name: `holders`: among the 24 requests of one group no holder is named more than 2 times; in some groups one holder is named exactly 2 times. `prefix_lengths`: some request has a prefix of exactly 128 positions.
All inputs are finite; a program needn't handle non-finite values.
Results may differ from the reference program's by a relative error of at most 0.03.
Values may be sent and summed in bfloat16 or wider, within the bound.
No kernel may reach another device: no remote copies, remote signals or barrier semaphores. Data moves between devices by JAX's collectives and lax.ppermute only.
A program may use at most 128 MiB of HBM per device.

```python
import math
import jax
import jax.numpy as jnp
import numpy as np
from jax import lax

D = 2048
HEADS = 16
KV_HEADS = 8
HEAD_DIM = 128
SPAN = 64
CAP = 2
REQ = 24
CLEN = 128
GROUPS = 32
SLOTS = 64
ROWS = 49152
N_TENSOR = 8


def draw_span_rows(key, part):
    column_key = jax.random.fold_in(jax.random.fold_in(key, 11), 1)
    base_key = jax.random.fold_in(jax.random.fold_in(key, 11), 2)
    column_scale = jnp.exp(jax.random.uniform(column_key, (D,), jnp.float32, 0.0, jnp.log(10.0)))
    base_values = jnp.clip(jax.random.normal(base_key, (ROWS, D), jnp.float32), -5.0, 5.0)
    return (base_values * column_scale[None, :]).astype(jnp.bfloat16)


def draw_q_norm_gain(key, part):
    base_values = jnp.exp(jax.random.uniform(jax.random.fold_in(key, 23), (HEAD_DIM,), jnp.float32, 0.0, jnp.log(3.0)))
    return base_values.astype(jnp.float32)


def draw_key_cache(key, part):
    noise_key = jax.random.fold_in(jax.random.fold_in(key, 37), 0)
    full_shape = (GROUPS, SLOTS, CLEN, KV_HEADS, HEAD_DIM)
    base_values = jnp.clip(1.5 * jax.random.normal(noise_key, full_shape, jnp.float32), -6.0, 6.0)
    return base_values.reshape(GROUPS, SLOTS, CLEN, KV_HEADS * HEAD_DIM).astype(jnp.bfloat16)


def shard_levels(rng, extent, shards, low, high):
    gain = 1.0
    for dim, blocks in shards:
        steps = jax.random.uniform(jax.random.fold_in(jax.random.fold_in(rng, 6), dim), (blocks,), jnp.float32, low / len(shards), high / len(shards))
        gain = gain * jnp.repeat(jnp.exp(steps), extent[dim] // blocks).reshape((-1,) + (1,) * (len(extent) - 1 - dim))
    return gain


def profile(amount, total, bound, lean):
    weights = [(1 << 20) // math.isqrt(standing ** lean) + 1 for standing in range(2, amount + 1)]
    rest, holding = total - bound - (amount - 1), [1] * (amount - 1)
    while rest > 0:
        candidates = [i for i in range(amount - 1) if holding[i] < bound]
        pool, remaining = sum([weights[i] for i in candidates]), rest
        for i in candidates:
            extra = min(bound - holding[i], max(1, remaining * weights[i] // pool), rest)
            holding[i] = holding[i] + extra
            rest = rest - extra
    return np.array([bound] + holding)


def uneven_parts(own_key, count, total, most, lean):
    if count == 2:
        one = jax.random.randint(own_key, (), max(1, total - most), min(most, total - 1) + 1)
        return jnp.stack([one, total - one])
    lengths = jnp.asarray(profile(count, total, most, lean), jnp.int32)
    couples = (count - 1) // 2
    donor, taker = lengths[1:1 + 2 * couples:2], lengths[2:2 + 2 * couples:2]
    slack = jnp.minimum(donor - 1, most - taker)
    passed = jax.random.randint(jax.random.fold_in(own_key, 1), (couples,), 0, 1 << 20) % (slack + 1)
    lengths = lengths.at[1:1 + 2 * couples:2].set(donor - passed).at[2:2 + 2 * couples:2].set(taker + passed)
    return lengths[jax.random.permutation(jax.random.fold_in(own_key, 2), count)]


def shared_out(own_key, own, number, rows, number_of, top, limit, slope):
    sequence = jax.random.permutation(own_key, number_of)
    heavy_load, common = load_shares(number_of, rows * top, limit, slope, True), load_shares(number_of, rows * top, limit, slope, False)
    places = jnp.arange(number_of)

    def named(sizes, rotation):
        used = int((sizes > 0).sum())
        fixed = max(1, used // 4)
        shifted = fixed + (places - fixed + rotation * (used - fixed)) % max(1, number_of - fixed)
        return jnp.zeros((number_of,), jnp.int32).at[sequence[jnp.where(places < fixed, places, shifted)]].set(jnp.asarray(sizes, jnp.int32))

    sizes = jnp.where(number % 4 == 0, named(heavy_load, number // 4), named(common, number - number // 4 - 1))
    mixed = jax.random.permutation(jax.random.fold_in(own, 3), number_of)
    donor, receiver = mixed[0:number_of // 2 * 2:2], mixed[1:number_of // 2 * 2:2]
    margin = jnp.minimum(sizes[donor] - 1, limit - sizes[receiver]) // 2
    margin = jnp.where((donor == sequence[0]) | (receiver == sequence[0]) | (sizes[receiver] == 0), 0, jnp.maximum(margin, 0))
    shifted = jax.random.randint(jax.random.fold_in(own, 4), (number_of // 2,), 0, 1 << 20) % (margin + 1)
    sizes = sizes.at[donor].add(-shifted).at[receiver].add(shifted)
    members = jnp.searchsorted(jnp.cumsum(sizes), jnp.arange(rows * top), side="right").astype(jnp.int32)
    table = members.reshape(top, rows).T
    table = table[jax.random.permutation(jax.random.fold_in(own, 1), rows)]
    rotation = jax.random.randint(jax.random.fold_in(own, 2), (rows, 1), 0, top)
    return jnp.take_along_axis(table, (jnp.arange(top)[None, :] + rotation) % top, axis=1)


def load_shares(number_of, total, reach, skew, full):
    loads = [(1 << 20) // math.isqrt(grade ** skew) + 1 for grade in range(1, number_of + 1)]
    largest = reach if full else min(reach, max(-(-total // number_of), total * loads[0] // sum(loads)))
    least = 1 if total - largest >= number_of - 1 else 0
    holding, surplus = [largest] + [least] * (number_of - 1), total - largest - least * (number_of - 1)
    while surplus > 0:
        free = [i for i in range(1, number_of) if holding[i] < largest] or [i for i in range(1, number_of) if holding[i] < reach]
        whole, budget = sum([loads[i] for i in free]), surplus
        for i in free:
            addition = min(reach - holding[i], max(1, budget * loads[i] // whole), surplus)
            holding[i] = holding[i] + addition
            surplus = surplus - addition
    return np.array(holding)


def normal_values(stream_key, shape, spread, limit, shards=(), kind=jnp.bfloat16):
    entries = jax.random.normal(stream_key, shape, jnp.float32) * spread
    if len(shards) > 0:
        entries = shard_levels(stream_key, shape, shards, -0.22, 0.18) * entries
    return jnp.clip(entries, min=-limit, max=limit).astype(kind)


def setup_inputs(seed: int = 0) -> dict:
    keys = jax.random.split(jax.random.key(seed), 14)
    span_rows = draw_span_rows(jax.random.fold_in(keys[13], 71), 0)
    norm_gain = jnp.clip(1.0 + 0.18 * jax.random.normal(keys[1], (D,), jnp.float32), 0.1, 1.9)
    q_weight = normal_values(keys[2], (D, HEADS * HEAD_DIM), D ** -0.5, 0.125, ((1, 8),))
    gate_weight = normal_values(keys[3], (D, HEADS * HEAD_DIM), D ** -0.5, 0.125, ((1, 8),))
    k_weight = normal_values(keys[4], (D, KV_HEADS * HEAD_DIM), D ** -0.5, 0.125, ((1, 8),))
    v_weight = normal_values(keys[5], (D, KV_HEADS * HEAD_DIM), D ** -0.5, 0.125, ((1, 8),))
    q_norm_gain = draw_q_norm_gain(jax.random.fold_in(keys[13], 71), 0)
    k_norm_gain = jnp.clip(jnp.exp(jax.random.uniform(keys[7], (HEAD_DIM,), jnp.float32, math.log(1.0), math.log(2.5))), 1.0, 2.5)
    o_weight = normal_values(keys[8], (HEADS * HEAD_DIM, D), (HEADS * HEAD_DIM) ** -0.5, 0.125, ((0, 8),))
    key_cache = draw_key_cache(jax.random.fold_in(keys[13], 71), 0)
    value_cache = normal_values(keys[10], (GROUPS, SLOTS, CLEN, KV_HEADS * HEAD_DIM), 1.0, 6.0, ((0, 32), (3, 8)))
    holders_keys = jax.random.split(jax.random.fold_in(keys[11], 1), (GROUPS * REQ) // REQ)
    holders_turns = jax.random.permutation(jax.random.fold_in(keys[11], 3), (GROUPS * REQ) // REQ)
    holders = jax.vmap(lambda own, number: shared_out(jax.random.fold_in(keys[11], 2), own, number, REQ, GROUPS, 1, CAP, 2))(holders_keys, holders_turns).reshape((GROUPS * REQ, 1))
    prefix_lengths = uneven_parts(keys[12], GROUPS * REQ, GROUPS * REQ * CLEN // 2, CLEN, 2).astype(jnp.int32)
    return {"span_rows": span_rows, "norm_gain": norm_gain, "q_weight": q_weight, "gate_weight": gate_weight, "k_weight": k_weight, "v_weight": v_weight, "q_norm_gain": q_norm_gain, "k_norm_gain": k_norm_gain, "o_weight": o_weight, "key_cache": key_cache, "value_cache": value_cache, "holders": holders, "prefix_lengths": prefix_lengths}


EPSILON = 1e-06
ROPE_BASE = 1000000.0

def rms_scale(values, gain_vector):
    mean_sq = lax.optimization_barrier(jnp.mean(values * values, axis=-1, keepdims=True))
    return values * lax.rsqrt(mean_sq + EPSILON) * gain_vector

def rotate(values, positions):
    half_dim = values.shape[-1] // 2
    frequency = ROPE_BASE ** (-jnp.arange(half_dim, dtype=jnp.float32) * 2.0 / values.shape[-1])
    angles = positions.astype(jnp.float32)[:, :, None, None] * frequency
    cosine = jnp.cos(angles)
    sine_part = jnp.sin(angles)
    front_half = values[..., :half_dim]
    back_half = values[..., half_dim:]
    return jnp.concatenate([front_half * cosine - back_half * sine_part, back_half * cosine + front_half * sine_part], axis=-1)

def reference(span_rows, norm_gain, q_weight, gate_weight, k_weight, v_weight, q_norm_gain, k_norm_gain, o_weight, key_cache, value_cache, holders, prefix_lengths):
    requests = GROUPS * REQ
    all_holders = holders.reshape(GROUPS, REQ).astype(jnp.int32)
    same_holder = all_holders[:, :, None] == all_holders[:, None, :]
    request_order = jnp.arange(REQ)
    earlier = request_order[None, :] < request_order[:, None]
    all_ranks = lax.optimization_barrier(jnp.sum(jnp.logical_and(same_holder, earlier[None]), axis=2)).astype(jnp.int32)
    group_ids = (jnp.arange(requests) // REQ).astype(jnp.int32)
    slot_index = (group_ids * CAP + all_ranks.reshape(-1)).astype(jnp.int32)
    flat_holders = all_holders.reshape(-1).astype(jnp.int32)
    positions = prefix_lengths.astype(jnp.int32)[:, None] + jnp.arange(SPAN, dtype=jnp.int32)[None, :]
    normed = rms_scale(span_rows.astype(jnp.float32), norm_gain.astype(jnp.float32)).astype(jnp.bfloat16)
    queries = jnp.dot(normed, q_weight, preferred_element_type=jnp.float32).reshape(requests, SPAN, HEADS, HEAD_DIM)
    queries = rotate(rms_scale(queries, q_norm_gain.astype(jnp.float32)), positions).astype(jnp.bfloat16)
    new_keys = jnp.dot(normed, k_weight, preferred_element_type=jnp.float32).reshape(requests, SPAN, KV_HEADS, HEAD_DIM)
    new_keys = rotate(rms_scale(new_keys, k_norm_gain.astype(jnp.float32)), positions).astype(jnp.bfloat16)
    new_values = jnp.dot(normed, v_weight, preferred_element_type=jnp.float32).astype(jnp.bfloat16).reshape(requests, SPAN, KV_HEADS, HEAD_DIM)
    gate_logits = jnp.dot(normed, gate_weight, preferred_element_type=jnp.float32)
    queries, new_keys, new_values = lax.optimization_barrier((queries, new_keys, new_values))
    score_scale = 1.0 / math.sqrt(HEAD_DIM)
    group_share = HEADS // KV_HEADS

    def attend_request(request_item):
        request_query, request_keys, request_values, holder_id, slot_id, length_now = request_item
        prefix_keys = key_cache[holder_id, slot_id].reshape(CLEN, KV_HEADS, HEAD_DIM)
        prefix_values = value_cache[holder_id, slot_id].reshape(CLEN, KV_HEADS, HEAD_DIM)
        all_keys = jnp.concatenate([prefix_keys, request_keys], axis=0).astype(jnp.float32)
        all_values = jnp.concatenate([prefix_values, request_values], axis=0).astype(jnp.float32)
        grouped = request_query.reshape(SPAN, KV_HEADS, group_share, HEAD_DIM).astype(jnp.float32)
        scores = jnp.einsum('qkgd,lkd->kgql', grouped, all_keys) * score_scale
        key_index = jnp.arange(CLEN + SPAN)[None, :]
        query_index = jnp.arange(SPAN)[:, None]
        valid_keys = jnp.where(key_index < CLEN, key_index < length_now, key_index - CLEN <= query_index)
        scores = jnp.where(valid_keys, scores, -jnp.inf)
        row_max = lax.optimization_barrier(jnp.max(scores, axis=-1, keepdims=True))
        raw_weights = jnp.exp(scores - row_max)
        row_total = lax.optimization_barrier(jnp.sum(raw_weights, axis=-1, keepdims=True))
        weights = lax.optimization_barrier(raw_weights.astype(jnp.bfloat16)).astype(jnp.float32)
        mixed_heads = jnp.einsum('kgql,lkd->kgqd', weights, all_values) / row_total
        return jnp.transpose(mixed_heads, (2, 0, 1, 3)).reshape(SPAN, HEADS * HEAD_DIM)
    mixed_heads = lax.map(attend_request, (queries, new_keys, new_values, flat_holders, slot_index, prefix_lengths.astype(jnp.int32)))
    attended = (mixed_heads.reshape(requests * SPAN, HEADS * HEAD_DIM) * jax.nn.sigmoid(gate_logits)).astype(jnp.bfloat16)
    block_cols = HEADS * HEAD_DIM // N_TENSOR
    summed = jnp.zeros((requests * SPAN, D), jnp.float32)
    for part_index in range(N_TENSOR):
        partial_out = jnp.dot(attended[:, part_index * block_cols:(part_index + 1) * block_cols], o_weight[part_index * block_cols:(part_index + 1) * block_cols], preferred_element_type=jnp.float32).astype(jnp.bfloat16)
        partial_out = lax.optimization_barrier(partial_out)
        summed = summed + partial_out.astype(jnp.float32)
    return summed.astype(jnp.bfloat16)
```

```python
import functools
import math

import jax
import jax.numpy as jnp
from jax import lax
from jax.experimental import pallas as pl
from jax.experimental.pallas import tpu as pltpu
from jax.sharding import Mesh
from jax.sharding import PartitionSpec as P

EPSILON = 1e-06
ROPE_BASE = 1000000.0
GROUP = ("y", "zh", "c")
TENSOR = ("zl", "x")
ROW_TILE = 256
BATCH = 4


def ring(size, step):
    return [(i, (i + step) % size) for i in range(size)]


def shift(value, axis, step):
    return lax.ppermute(value, axis, ring(lax.axis_size(axis), step))


def spread(block):
    twin = shift(block, "zl", 1)
    below, above = shift(block, "x", 1), shift(block, "x", -1)
    twin_below, twin_above = shift(twin, "x", 1), shift(twin, "x", -1)
    far = shift(below, "x", 1)
    twin_far = shift(twin_above, "x", -1)
    return [block, twin, below, above, twin_below, twin_above, far, twin_far]


def block_ids():
    zl, x = lax.axis_index("zl"), lax.axis_index("x")
    pairs = [(0, 0), (1, 0), (0, 3), (0, 1), (1, 3), (1, 1), (0, 2), (1, 2)]
    return jnp.stack([((zl + dz) % 2) * 4 + (x + dx) % 4 for dz, dx in pairs]).astype(jnp.int32)


def head_norm_rotate(values, gain, cosine, sine):
    scale = lax.rsqrt(jnp.mean(values * values, axis=-1, keepdims=True) + EPSILON)
    scaled = values * scale * gain
    half = values.shape[-1] // 2
    return scaled * cosine + pltpu.roll(scaled, half, 1) * sine


def project_kernel(ids, *refs):
    pieces, rest = refs[:8], refs[8:]
    (gain, wq, wg, wk, wv, q_gain, k_gain, cosine, sine, q_out, g_out, k_out, v_out, normed) = rest
    width = pieces[0].shape[1]
    head = wk.shape[1]
    total = jnp.zeros((pieces[0].shape[0], 1), jnp.float32)
    for piece in pieces:
        value = piece[...].astype(jnp.float32)
        total = total + jnp.sum(value * value, axis=-1, keepdims=True)
    scale = lax.rsqrt(total / (8 * width) + EPSILON)
    for j, piece in enumerate(pieces):
        block = ids[j]
        value = piece[...].astype(jnp.float32) * scale * gain[pl.ds(block, 1), :]
        normed[:, pl.ds(pl.multiple_of(block * width, width), width)] = value.astype(jnp.bfloat16)
    x = normed[...]
    cos, sin = cosine[...], sine[...]
    q = jnp.dot(x, wq[...], preferred_element_type=jnp.float32)
    for h in range(q.shape[1] // head):
        part = head_norm_rotate(q[:, h * head : (h + 1) * head], q_gain[...], cos, sin)
        q_out[:, h * head : (h + 1) * head] = part.astype(jnp.bfloat16)
    k = jnp.dot(x, wk[...], preferred_element_type=jnp.float32)
    k_out[...] = head_norm_rotate(k, k_gain[...], cos, sin).astype(jnp.bfloat16)
    v_out[...] = jnp.dot(x, wv[...], preferred_element_type=jnp.float32).astype(jnp.bfloat16)
    gate = jnp.dot(x, wg[...], preferred_element_type=jnp.float32)
    g_out[...] = jax.nn.sigmoid(gate)


def project(ids, pieces, gain, wq, wg, wk, wv, q_gain, k_gain, cosine, sine):
    rows, width = pieces[0].shape
    depth = gain.shape[0]
    head = q_gain.shape[0]
    tile = lambda columns: pl.BlockSpec((ROW_TILE, columns), lambda i, _: (i, 0))
    whole = lambda a: pl.BlockSpec(a.shape, lambda i, _: (0, 0))
    gain = gain.reshape(depth // width, width)
    q_gain, k_gain = q_gain.reshape(1, head), k_gain.reshape(1, head)
    constants = (gain, wq, wg, wk, wv, q_gain, k_gain)
    return pl.pallas_call(
        project_kernel,
        out_shape=(
            jax.ShapeDtypeStruct((rows, wq.shape[1]), jnp.bfloat16),
            jax.ShapeDtypeStruct((rows, wg.shape[1]), jnp.float32),
            jax.ShapeDtypeStruct((rows, head), jnp.bfloat16),
            jax.ShapeDtypeStruct((rows, head), jnp.bfloat16),
        ),
        grid_spec=pltpu.PrefetchScalarGridSpec(
            num_scalar_prefetch=1,
            grid=(rows // ROW_TILE,),
            in_specs=[tile(width)] * 8 + [whole(a) for a in constants] + [tile(head)] * 2,
            out_specs=[tile(wq.shape[1]), tile(wg.shape[1]), tile(head), tile(head)],
            scratch_shapes=[pltpu.VMEM((ROW_TILE, depth), jnp.bfloat16)],
        ),
        compiler_params=pltpu.CompilerParams(vmem_limit_bytes=40 << 20),
        cost_estimate=pl.CostEstimate(
            flops=2 * rows * depth * 6 * head, bytes_accessed=14 << 20, transcendentals=rows * 256
        ),
        name="project",
    )(ids, *pieces, *constants, cosine, sine)


def attend_kernel(starts, lengths, q, g, k, v, keys, values, out):
    head = k.shape[1]
    span = q.shape[0] // BATCH
    window = 128
    shares = q.shape[1] // head
    score_scale = 1.0 / math.sqrt(head)
    contract = (((1,), (1,)), ((), ()))
    column = lax.broadcasted_iota(jnp.int32, (shares * span, window), 1)
    old_row = lax.broadcasted_iota(jnp.int32, (window, head), 0)
    token = lax.broadcasted_iota(jnp.int32, (shares, span, span), 1).reshape(shares * span, span)
    causal = lax.broadcasted_iota(jnp.int32, (shares * span, span), 1) <= token
    for b in range(BATCH):
        r = pl.program_id(0) * BATCH + b
        length = lengths[r]
        rows = slice(b * span, (b + 1) * span)
        query = jnp.concatenate([q[rows, s * head : (s + 1) * head] for s in range(shares)], axis=0)
        place = pl.ds(pl.multiple_of(starts[r], 16), window)
        old_keys, old_values = keys[place, :], values[place, :]
        old_values = jnp.where(old_row < length, old_values, jnp.zeros_like(old_values))
        old = lax.dot_general(query, old_keys, contract, preferred_element_type=jnp.float32)
        new = lax.dot_general(query, k[rows, :], contract, preferred_element_type=jnp.float32)
        old = jnp.where(column < length, old * score_scale, -jnp.inf)
        new = jnp.where(causal, new * score_scale, -jnp.inf)
        row_max = jnp.maximum(
            jnp.max(old, axis=-1, keepdims=True), jnp.max(new, axis=-1, keepdims=True)
        )
        old, new = jnp.exp(old - row_max), jnp.exp(new - row_max)
        row_total = jnp.sum(old, axis=-1, keepdims=True) + jnp.sum(new, axis=-1, keepdims=True)
        mixed = jnp.dot(old.astype(jnp.bfloat16), old_values, preferred_element_type=jnp.float32)
        mixed += jnp.dot(new.astype(jnp.bfloat16), v[rows, :], preferred_element_type=jnp.float32)
        mixed = mixed / row_total
        for s in range(shares):
            columns = slice(s * head, (s + 1) * head)
            part = mixed[s * span : (s + 1) * span] * g[rows, columns]
            out[rows, columns] = part.astype(jnp.bfloat16)


def attend(starts, lengths, q, g, k, v, keys, values):
    rows, columns = q.shape
    head = k.shape[1]
    step = rows // lengths.shape[0] * BATCH
    tile = lambda width: pl.BlockSpec((step, width), lambda i, *_: (i, 0))
    whole = lambda a: pl.BlockSpec(a.shape, lambda i, *_: (0, 0))
    return pl.pallas_call(
        attend_kernel,
        out_shape=jax.ShapeDtypeStruct((rows, columns), jnp.bfloat16),
        grid_spec=pltpu.PrefetchScalarGridSpec(
            num_scalar_prefetch=2,
            grid=(rows // step,),
            in_specs=[tile(columns)] * 2 + [tile(head)] * 2 + [whole(keys), whole(values)],
            out_specs=tile(columns),
        ),
        compiler_params=pltpu.CompilerParams(vmem_limit_bytes=40 << 20),
        cost_estimate=pl.CostEstimate(
            flops=4 * rows * columns * 192, bytes_accessed=8 << 20, transcendentals=rows * 2 * 192
        ),
        name="attend",
    )(starts, lengths, q, g, k, v, keys, values)


def assemble_kernel(places, *refs):
    pieces, out, sems = refs[:-2], refs[-2], refs[-1]
    depth = pieces[0].shape[0]
    copies = []
    for j, piece in enumerate(pieces):
        start = pl.multiple_of(places[j] * depth, depth)
        copies.append(pltpu.make_async_copy(piece, out.at[pl.ds(start, depth)], sems.at[j]))
    for copy in copies:
        copy.start()
    for copy in copies:
        copy.wait()


def assemble(places, pieces):
    depth, columns = pieces[0].shape
    count = len(pieces)
    return pl.pallas_call(
        assemble_kernel,
        out_shape=jax.ShapeDtypeStruct((depth * count, columns), pieces[0].dtype),
        grid_spec=pltpu.PrefetchScalarGridSpec(
            num_scalar_prefetch=1,
            grid=(1,),
            in_specs=[pl.BlockSpec(memory_space=pl.ANY)] * count,
            out_specs=pl.BlockSpec(memory_space=pl.ANY),
            scratch_shapes=[pltpu.SemaphoreType.DMA((count,))],
        ),
        cost_estimate=pl.CostEstimate(flops=0, bytes_accessed=16 << 20, transcendentals=0),
        name="assemble",
    )(places, *pieces)


def output_kernel(heads, weight, out, joined):
    width = heads.shape[2]

    @pl.when(pl.program_id(0) == 0)
    def _():
        for j in range(heads.shape[0]):
            joined[:, j * width : (j + 1) * width] = heads[j]

    total = jnp.dot(joined[...], weight[...], preferred_element_type=jnp.float32)
    out[...] = total.astype(jnp.bfloat16)


def project_out(heads, weight):
    blocks, rows, width = heads.shape
    depth, columns = weight.shape
    tile = 512
    return pl.pallas_call(
        output_kernel,
        out_shape=jax.ShapeDtypeStruct((rows, columns), jnp.bfloat16),
        grid=(columns // tile,),
        in_specs=[
            pl.BlockSpec(heads.shape, lambda i: (0, 0, 0)),
            pl.BlockSpec((depth, tile), lambda i: (0, i)),
        ],
        out_specs=pl.BlockSpec((rows, tile), lambda i: (0, i)),
        scratch_shapes=[pltpu.VMEM((rows, depth), jnp.bfloat16)],
        compiler_params=pltpu.CompilerParams(vmem_limit_bytes=30 << 20),
        cost_estimate=pl.CostEstimate(
            flops=2 * rows * depth * columns, bytes_accessed=10 << 20, transcendentals=0
        ),
        name="project_out",
    )(heads, weight)


def local(
    span_rows,
    norm_gain,
    q_weight,
    gate_weight,
    k_weight,
    v_weight,
    q_norm_gain,
    k_norm_gain,
    o_weight,
    key_cache,
    value_cache,
    holders,
    prefix_lengths,
):
    groups = 32
    group_id = lax.axis_index(GROUP)
    requests = prefix_lengths.shape[0] // groups
    rows = span_rows.shape[0]
    span_len = rows // requests
    head_dim = q_norm_gain.shape[0]
    capacity = key_cache.shape[1] // groups
    window = key_cache.shape[2]
    blocks = lax.axis_size(TENSOR)

    all_holders = holders.reshape(groups, requests)
    my_holders = lax.dynamic_index_in_dim(all_holders, group_id, 0, keepdims=False)
    my_lengths = lax.dynamic_index_in_dim(
        prefix_lengths.reshape(groups, requests), group_id, 0, keepdims=False
    )
    order = jnp.arange(requests)
    earlier = order[None, :] < order[:, None]
    my_ranks = jnp.sum((my_holders[:, None] == my_holders[None, :]) & earlier, axis=1)
    starts = ((my_holders * capacity + my_ranks) * window).astype(jnp.int32)

    positions = my_lengths[:, None] + jnp.arange(span_len, dtype=jnp.int32)[None, :]
    half = head_dim // 2
    frequency = ROPE_BASE ** (-jnp.arange(half, dtype=jnp.float32) * 2.0 / head_dim)
    angles = positions.reshape(-1).astype(jnp.float32)[:, None] * frequency
    cosine, sine = jnp.cos(angles), jnp.sin(angles)
    cosine = jnp.concatenate([cosine, cosine], axis=-1)
    sine = jnp.concatenate([-sine, sine], axis=-1)

    ids = block_ids()
    pieces = spread(span_rows)

    local_keys = key_cache.reshape(groups, capacity * window, head_dim)
    local_values = value_cache.reshape(groups, capacity * window, head_dim)
    keys = lax.all_to_all(local_keys, GROUP, 0, 0, tiled=True).reshape(-1, head_dim)
    values = lax.all_to_all(local_values, GROUP, 0, 0, tiled=True).reshape(-1, head_dim)

    q, g, k, v = project(
        ids, pieces, norm_gain, q_weight, gate_weight, k_weight, v_weight,
        q_norm_gain, k_norm_gain, cosine, sine,
    )

    core = lax.axis_index("c")
    depth = o_weight.shape[0] // 2
    mine = lax.dynamic_slice_in_dim(o_weight, core * depth, depth, 0)
    half_pieces = spread(mine)
    other_pieces = [shift(p, "c", 1) for p in half_pieces]
    places = jnp.concatenate([ids * 2 + core, ids * 2 + 1 - core]).astype(jnp.int32)
    whole_weight = assemble(places, half_pieces + other_pieces)

    attended = attend(starts, my_lengths, q, g, k, v, keys, values)
    heads = lax.all_to_all(
        attended.reshape(blocks, rows // blocks, attended.shape[1]), TENSOR, 0, 0, tiled=True
    )
    return project_out(heads, whole_weight)


def solution(mesh):
    mesh = Mesh(mesh.devices.reshape(4, 4, 2, 2, 4), GROUP + TENSOR)
    placed = (
        P(GROUP, TENSOR),
        P(),
        P(None, TENSOR),
        P(None, TENSOR),
        P(None, TENSOR),
        P(None, TENSOR),
        P(),
        P(),
        P(TENSOR, None),
        P(GROUP, None, None, TENSOR),
        P(GROUP, None, None, TENSOR),
        P(),
        P(),
    )
    return jax.shard_map(
        local, mesh=mesh, in_specs=placed, out_specs=P(GROUP + TENSOR, None), check_vma=False
    )
```

```python
import functools
import math

import jax
import jax.numpy as jnp
from jax import lax
from jax.experimental import pallas as pl
from jax.experimental.pallas import tpu as pltpu
from jax.sharding import Mesh
from jax.sharding import PartitionSpec as P

EPSILON = 1e-06
ROPE_BASE = 1000000.0
GROUP = ("y", "zh", "c")
TENSOR = ("zl", "x")
ROW_TILE = 256
BATCH = 4
UNIT = 16
PACKED = 72 * UNIT


def ring(size, step):
    return [(i, (i + step) % size) for i in range(size)]


def shift(value, axis, step):
    return lax.ppermute(value, axis, ring(lax.axis_size(axis), step))


def spread(block):
    twin = shift(block, "zl", 1)
    below, above = shift(block, "x", 1), shift(block, "x", -1)
    twin_below, twin_above = shift(twin, "x", 1), shift(twin, "x", -1)
    far = shift(below, "x", 1)
    twin_far = shift(twin_above, "x", -1)
    return [block, twin, below, above, twin_below, twin_above, far, twin_far]


def block_ids():
    zl, x = lax.axis_index("zl"), lax.axis_index("x")
    pairs = [(0, 0), (1, 0), (0, 3), (0, 1), (1, 3), (1, 1), (0, 2), (1, 2)]
    return jnp.stack([((zl + dz) % 2) * 4 + (x + dx) % 4 for dz, dx in pairs]).astype(jnp.int32)


def head_norm_rotate(values, gain, cosine, sine):
    scale = lax.rsqrt(jnp.mean(values * values, axis=-1, keepdims=True) + EPSILON)
    scaled = values * scale * gain
    half = values.shape[-1] // 2
    return scaled * cosine + pltpu.roll(scaled, half, 1) * sine


def project_kernel(ids, *refs):
    pieces, rest = refs[:8], refs[8:]
    (gain, wq, wg, wk, wv, q_gain, k_gain, cosine, sine, q_out, g_out, k_out, v_out, normed) = rest
    width = pieces[0].shape[1]
    head = wk.shape[1]
    total = jnp.zeros((pieces[0].shape[0], 1), jnp.float32)
    for piece in pieces:
        value = piece[...].astype(jnp.float32)
        total = total + jnp.sum(value * value, axis=-1, keepdims=True)
    scale = lax.rsqrt(total / (8 * width) + EPSILON)
    for j, piece in enumerate(pieces):
        block = ids[j]
        value = piece[...].astype(jnp.float32) * scale * gain[pl.ds(block, 1), :]
        normed[:, pl.ds(pl.multiple_of(block * width, width), width)] = value.astype(jnp.bfloat16)
    x = normed[...]
    cos, sin = cosine[...], sine[...]
    q = jnp.dot(x, wq[...], preferred_element_type=jnp.float32)
    for h in range(q.shape[1] // head):
        part = head_norm_rotate(q[:, h * head : (h + 1) * head], q_gain[...], cos, sin)
        q_out[:, h * head : (h + 1) * head] = part.astype(jnp.bfloat16)
    k = jnp.dot(x, wk[...], preferred_element_type=jnp.float32)
    k_out[...] = head_norm_rotate(k, k_gain[...], cos, sin).astype(jnp.bfloat16)
    v_out[...] = jnp.dot(x, wv[...], preferred_element_type=jnp.float32).astype(jnp.bfloat16)
    gate = jnp.dot(x, wg[...], preferred_element_type=jnp.float32)
    g_out[...] = jax.nn.sigmoid(gate)


def project(ids, pieces, gain, wq, wg, wk, wv, q_gain, k_gain, cosine, sine):
    rows, width = pieces[0].shape
    depth = gain.shape[0]
    head = q_gain.shape[0]
    tile = lambda columns: pl.BlockSpec((ROW_TILE, columns), lambda i, _: (i, 0))
    whole = lambda a: pl.BlockSpec(a.shape, lambda i, _: (0, 0))
    gain = gain.reshape(depth // width, width)
    q_gain, k_gain = q_gain.reshape(1, head), k_gain.reshape(1, head)
    constants = (gain, wq, wg, wk, wv, q_gain, k_gain)
    return pl.pallas_call(
        project_kernel,
        out_shape=(
            jax.ShapeDtypeStruct((rows, wq.shape[1]), jnp.bfloat16),
            jax.ShapeDtypeStruct((rows, wg.shape[1]), jnp.float32),
            jax.ShapeDtypeStruct((rows, head), jnp.bfloat16),
            jax.ShapeDtypeStruct((rows, head), jnp.bfloat16),
        ),
        grid_spec=pltpu.PrefetchScalarGridSpec(
            num_scalar_prefetch=1,
            grid=(rows // ROW_TILE,),
            in_specs=[tile(width)] * 8 + [whole(a) for a in constants] + [tile(head)] * 2,
            out_specs=[tile(wq.shape[1]), tile(wg.shape[1]), tile(head), tile(head)],
            scratch_shapes=[pltpu.VMEM((ROW_TILE, depth), jnp.bfloat16)],
        ),
        compiler_params=pltpu.CompilerParams(vmem_limit_bytes=40 << 20),
        cost_estimate=pl.CostEstimate(
            flops=2 * rows * depth * 6 * head, bytes_accessed=14 << 20, transcendentals=rows * 256
        ),
        name="project",
    )(ids, *pieces, *constants, cosine, sine)


def attend_kernel(starts, lengths, q, g, k, v, *refs):
    key_parts, value_parts = refs[:4], refs[4:8]
    out, keys, values = refs[8:]
    head = k.shape[1]
    span = q.shape[0] // BATCH
    shares = q.shape[1] // head
    size = key_parts[0].shape[0]
    window = keys.shape[0] - 4 * size
    score_scale = 1.0 / math.sqrt(head)
    contract = (((1,), (1,)), ((), ()))

    @pl.when(pl.program_id(0) == 0)
    def _():
        for j in range(4):
            keys[j * size : (j + 1) * size, :] = key_parts[j][...]
            values[j * size : (j + 1) * size, :] = value_parts[j][...]
        keys[4 * size :, :] = jnp.zeros((window, head), keys.dtype)
        values[4 * size :, :] = jnp.zeros((window, head), values.dtype)

    column = lax.broadcasted_iota(jnp.int32, (shares * span, window), 1)
    old_row = lax.broadcasted_iota(jnp.int32, (window, head), 0)
    token = lax.broadcasted_iota(jnp.int32, (shares, span, span), 1).reshape(shares * span, span)
    causal = lax.broadcasted_iota(jnp.int32, (shares * span, span), 1) <= token
    for b in range(BATCH):
        r = pl.program_id(0) * BATCH + b
        length = lengths[r]
        rows = slice(b * span, (b + 1) * span)
        query = jnp.concatenate([q[rows, s * head : (s + 1) * head] for s in range(shares)], axis=0)
        place = pl.ds(pl.multiple_of(starts[r], UNIT), window)
        old_keys, old_values = keys[place, :], values[place, :]
        old_values = jnp.where(old_row < length, old_values, jnp.zeros_like(old_values))
        old = lax.dot_general(query, old_keys, contract, preferred_element_type=jnp.float32)
        new = lax.dot_general(query, k[rows, :], contract, preferred_element_type=jnp.float32)
        old = jnp.where(column < length, old * score_scale, -jnp.inf)
        new = jnp.where(causal, new * score_scale, -jnp.inf)
        row_max = jnp.maximum(
            jnp.max(old, axis=-1, keepdims=True), jnp.max(new, axis=-1, keepdims=True)
        )
        old, new = jnp.exp(old - row_max), jnp.exp(new - row_max)
        row_total = jnp.sum(old, axis=-1, keepdims=True) + jnp.sum(new, axis=-1, keepdims=True)
        mixed = jnp.dot(old.astype(jnp.bfloat16), old_values, preferred_element_type=jnp.float32)
        mixed += jnp.dot(new.astype(jnp.bfloat16), v[rows, :], preferred_element_type=jnp.float32)
        mixed = mixed / row_total
        for s in range(shares):
            columns = slice(s * head, (s + 1) * head)
            part = mixed[s * span : (s + 1) * span] * g[rows, columns]
            out[rows, columns] = part.astype(jnp.bfloat16)


def attend(starts, lengths, q, g, k, v, keys, values, window):
    rows, columns = q.shape
    head = k.shape[1]
    step = rows // lengths.shape[0] * BATCH
    tile = lambda width: pl.BlockSpec((step, width), lambda i, *_: (i, 0))
    whole = lambda a: pl.BlockSpec(a.shape, lambda i, *_: (0, 0))
    store = pltpu.VMEM((4 * keys[0].shape[0] + window, head), keys[0].dtype)
    return pl.pallas_call(
        attend_kernel,
        out_shape=jax.ShapeDtypeStruct((rows, columns), jnp.bfloat16),
        grid_spec=pltpu.PrefetchScalarGridSpec(
            num_scalar_prefetch=2,
            grid=(rows // step,),
            in_specs=[tile(columns)] * 2 + [tile(head)] * 2 + [whole(a) for a in keys + values],
            out_specs=tile(columns),
            scratch_shapes=[store, store],
        ),
        compiler_params=pltpu.CompilerParams(vmem_limit_bytes=40 << 20),
        cost_estimate=pl.CostEstimate(
            flops=4 * rows * columns * 192, bytes_accessed=8 << 20, transcendentals=rows * 2 * 192
        ),
        name="attend",
    )(starts, lengths, q, g, k, v, *keys, *values)


def pack_kernel(offsets, *refs):
    pieces, outs, store = refs[:4], refs[4:8], refs[8]
    slots, window = pieces[0].shape[2], pieces[0].shape[3]
    size = outs[0].shape[0]
    for k, out in enumerate(outs):
        for j in range(4 * 2 * slots):
            p, q, rank = j // (2 * slots), j // slots % 2, j % slots
            block = offsets[4 * 4 * 2 * slots + k]
            place = pl.multiple_of(offsets[k * 4 * 2 * slots + j], UNIT)
            store[pl.ds(place, window), :] = pieces[p][q, block, rank]
        out[...] = store[:size, :]


def pack(offsets, pieces, size):
    window, head = pieces[0].shape[3:]
    return pl.pallas_call(
        pack_kernel,
        out_shape=[jax.ShapeDtypeStruct((size, head), pieces[0].dtype)] * 4,
        grid_spec=pltpu.PrefetchScalarGridSpec(
            num_scalar_prefetch=1,
            grid=(1,),
            in_specs=[pl.BlockSpec(a.shape, lambda i, _: (0,) * 5) for a in pieces],
            out_specs=[pl.BlockSpec((size, head), lambda i, _: (0, 0))] * 4,
            scratch_shapes=[pltpu.VMEM((size + window, head), pieces[0].dtype)],
        ),
        compiler_params=pltpu.CompilerParams(vmem_limit_bytes=30 << 20),
        cost_estimate=pl.CostEstimate(flops=0, bytes_accessed=4 << 20, transcendentals=0),
        name="pack",
    )(offsets, *pieces)


def output_kernel(places, heads, mine, other, out, joined):
    count, depth = mine.shape[:2]

    @pl.when(pl.program_id(0) == 0)
    def _():
        for j in range(count):
            for h in range(2):
                first = pl.multiple_of((places[count] + h) % 2 * depth, depth)
                columns = slice((2 * j + h) * depth, (2 * j + h + 1) * depth)
                joined[:, columns] = heads[places[j], :, pl.ds(first, depth)]

    total = jnp.zeros(out.shape, jnp.float32)
    for j in range(count):
        weight = jnp.concatenate([mine[j], other[j]], axis=0)
        part = joined[:, 2 * j * depth : 2 * (j + 1) * depth]
        total = total + jnp.dot(part, weight, preferred_element_type=jnp.float32)
    out[...] = total.astype(jnp.bfloat16)


def project_out(places, heads, mine, other):
    blocks, rows, width = heads.shape
    depth, columns = mine.shape[1:]
    tile = 512
    half = pl.BlockSpec((blocks, depth, tile), lambda i, _: (0, 0, i))
    return pl.pallas_call(
        output_kernel,
        out_shape=jax.ShapeDtypeStruct((rows, columns), jnp.bfloat16),
        grid_spec=pltpu.PrefetchScalarGridSpec(
            num_scalar_prefetch=1,
            grid=(columns // tile,),
            in_specs=[pl.BlockSpec(heads.shape, lambda i, _: (0, 0, 0)), half, half],
            out_specs=pl.BlockSpec((rows, tile), lambda i, _: (0, i)),
            scratch_shapes=[pltpu.VMEM((rows, blocks * width), jnp.bfloat16)],
        ),
        compiler_params=pltpu.CompilerParams(vmem_limit_bytes=30 << 20),
        cost_estimate=pl.CostEstimate(
            flops=2 * rows * blocks * width * columns, bytes_accessed=10 << 20, transcendentals=0
        ),
        name="project_out",
    )(places, heads, mine, other)


def take(array, index):
    return lax.dynamic_index_in_dim(array, index, 0, keepdims=False)


def across_y(cache, groups, capacity):
    window, head = cache.shape[1:]
    y, c = lax.axis_index("y"), lax.axis_index("c")
    sides = cache.reshape(4, 4, 2, capacity, window, head)
    own = lax.dynamic_index_in_dim(sides, c, 2, keepdims=False)
    twin = shift(lax.dynamic_index_in_dim(sides, 1 - c, 2, keepdims=False), "c", 1)
    parts = [jnp.stack([take(own, (y + k) % 4), take(twin, (y + k) % 4)]) for k in range(4)]
    return [parts[0]] + [shift(parts[k], "y", k) for k in (1, 3, 2)]


def across_z(parts):
    return [parts[0]] + [shift(parts[k], "zh", k) for k in range(1, 4)]


def local(
    span_rows,
    norm_gain,
    q_weight,
    gate_weight,
    k_weight,
    v_weight,
    q_norm_gain,
    k_norm_gain,
    o_weight,
    key_cache,
    value_cache,
    holders,
    prefix_lengths,
):
    groups = lax.axis_size(GROUP)
    group_id = lax.axis_index(GROUP)
    requests = prefix_lengths.shape[0] // groups
    rows = span_rows.shape[0]
    span_len = rows // requests
    head_dim = q_norm_gain.shape[0]
    capacity = key_cache.shape[1] // groups
    window = key_cache.shape[2]
    blocks = lax.axis_size(TENSOR)

    y, zh, core = lax.axis_index("y"), lax.axis_index("zh"), lax.axis_index("c")
    all_holders = holders.reshape(groups, requests)
    all_lengths = prefix_lengths.reshape(groups, requests)
    order = jnp.arange(requests)
    earlier = order[None, :] < order[:, None]
    same = all_holders[:, :, None] == all_holders[:, None, :]
    all_ranks = jnp.sum(same & earlier[None], axis=2)
    all_units = (all_lengths + UNIT - 1) // UNIT
    plane = all_holders // 2 % 4
    per_plane = jnp.sum(
        jnp.where(plane[:, :, None] == jnp.arange(4), all_units[:, :, None], 0), axis=1
    )
    fits = jnp.max(per_plane) * UNIT <= PACKED

    seen_y, seen_c = jnp.array([0, 3, 1, 2]), jnp.array([0, 1])
    slot_y = (y + seen_y[:, None, None]) % 4
    slot_c = (core + seen_c[None, :, None]) % 2
    slot_rank = jnp.arange(capacity)[None, None, :]
    z_ids = (zh + jnp.arange(4)) % 4
    served = (y * 4 + z_ids) * 2 + core
    slot_holder = (slot_y * 4 + zh) * 2 + slot_c
    slot_key = (slot_holder * capacity + slot_rank).reshape(-1)
    served_key = (all_holders * capacity + all_ranks)[served]
    hit = served_key[:, :, None] == slot_key[None, None, :]
    slot_units = jnp.sum(jnp.where(hit, all_units[served][:, :, None], 0), axis=1)
    offsets = (jnp.cumsum(slot_units, axis=1) - slot_units) * UNIT
    z_ids = z_ids.astype(jnp.int32)

    mine = lambda a: lax.dynamic_index_in_dim(a, group_id, 0, keepdims=False)
    my_holders, my_ranks, my_lengths, my_units = map(
        mine, (all_holders, all_ranks, all_lengths, all_units)
    )
    from_y = (my_holders // 8 - y) % 4
    from_y = jnp.where(from_y == 3, 1, jnp.where(from_y == 1, 2, jnp.where(from_y == 2, 3, 0)))
    from_z = (zh - my_holders // 2 % 4) % 4
    from_c = (my_holders - core) % 2
    my_order = (from_y * 2 + from_c) * capacity + my_ranks
    ahead = (from_z[:, None] == from_z[None, :]) & (my_order[None, :] < my_order[:, None])
    my_start = jnp.sum(jnp.where(ahead, my_units[None, :], 0), axis=1) * UNIT

    def packing(size):
        limit = jnp.minimum(offsets, size).reshape(-1)
        places = jnp.concatenate([limit, z_ids]).astype(jnp.int32)
        starts = jnp.minimum(from_z * size + my_start, 4 * size)
        return places, starts.astype(jnp.int32)

    positions = my_lengths[:, None] + jnp.arange(span_len, dtype=jnp.int32)[None, :]
    half = head_dim // 2
    frequency = ROPE_BASE ** (-jnp.arange(half, dtype=jnp.float32) * 2.0 / head_dim)
    angles = positions.reshape(-1).astype(jnp.float32)[:, None] * frequency
    cosine, sine = jnp.cos(angles), jnp.sin(angles)
    cosine = jnp.concatenate([cosine, cosine], axis=-1)
    sine = jnp.concatenate([-sine, sine], axis=-1)

    ids = block_ids()
    pieces = spread(span_rows)

    key_parts = across_y(key_cache[0], groups, capacity)
    value_parts = across_y(value_cache[0], groups, capacity)
    places, starts = packing(PACKED)
    keys = across_z(pack(places, key_parts, PACKED))
    values = across_z(pack(places, value_parts, PACKED))

    depth = o_weight.shape[0] // 2
    half, pieces[6], pieces[7] = lax.optimization_barrier(
        (lax.dynamic_slice_in_dim(o_weight, core * depth, depth, 0), pieces[6], pieces[7])
    )
    pair = jnp.stack([half, shift(half, "zl", 1)])
    below, above = shift(pair, "x", 1), shift(pair, "x", -1)
    far, twin_far = shift(below[0], "x", 1), shift(above[1], "x", -1)
    halves = jnp.stack(
        [pair[0], pair[1], below[0], above[0], below[1], above[1], far, twin_far]
    )
    other_halves = shift(halves, "c", 1)

    q, g, k, v = project(
        ids, pieces, norm_gain, q_weight, gate_weight, k_weight, v_weight,
        q_norm_gain, k_norm_gain, cosine, sine,
    )

    def packed(keys, values, key_parts, value_parts, q, g, k, v):
        return attend(starts, my_lengths, q, g, k, v, keys, values, window)

    def full(keys, values, key_parts, value_parts, q, g, k, v):
        size = 8 * capacity * window
        places, starts = packing(size)
        keys, values = (across_z(pack(places, a, size)) for a in (key_parts, value_parts))
        return attend(starts, my_lengths, q, g, k, v, keys, values, window)

    attended = lax.cond(fits, packed, full, keys, values, key_parts, value_parts, q, g, k, v)
    heads = lax.all_to_all(
        attended.reshape(blocks, rows // blocks, attended.shape[1]), TENSOR, 0, 0, tiled=True
    )
    out_places = jnp.concatenate([ids, core[None]]).astype(jnp.int32)
    return project_out(out_places, heads, halves, other_halves)


def solution(mesh):
    mesh = Mesh(mesh.devices.reshape(4, 4, 2, 2, 4), GROUP + TENSOR)
    placed = (
        P(GROUP, TENSOR),
        P(),
        P(None, TENSOR),
        P(None, TENSOR),
        P(None, TENSOR),
        P(None, TENSOR),
        P(),
        P(),
        P(TENSOR, None),
        P(GROUP, None, None, TENSOR),
        P(GROUP, None, None, TENSOR),
        P(),
        P(),
    )
    return jax.shard_map(
        local, mesh=mesh, in_specs=placed, out_specs=P(GROUP + TENSOR, None), check_vma=False
    )
```

```python
import functools
import math

import jax
import jax.numpy as jnp
from jax import lax
from jax.experimental import pallas as pl
from jax.experimental.pallas import tpu as pltpu
from jax.sharding import Mesh
from jax.sharding import PartitionSpec as P

EPSILON = 1e-06
ROPE_BASE = 1000000.0
GROUP = ("y", "zh", "c")
TENSOR = ("zl", "x")
ROW_TILE = 256
BATCH = 4
UNIT = 16
PACKED = 72 * UNIT
COST = pl.CostEstimate(flops=1 << 20, bytes_accessed=1 << 20, transcendentals=0)


def ring(size, step):
    return [(i, (i + step) % size) for i in range(size)]


def shift(value, axis, step):
    return lax.ppermute(value, axis, ring(lax.axis_size(axis), step))


def spread(block):
    twin = shift(block, "zl", 1)
    below, above = shift(block, "x", 1), shift(block, "x", -1)
    twin_below, twin_above = shift(twin, "x", 1), shift(twin, "x", -1)
    far = shift(below, "x", 1)
    twin_far = shift(twin_above, "x", -1)
    return [block, twin, below, above, twin_below, twin_above, far, twin_far]


def block_ids():
    zl, x = lax.axis_index("zl"), lax.axis_index("x")
    pairs = [(0, 0), (1, 0), (0, 3), (0, 1), (1, 3), (1, 1), (0, 2), (1, 2)]
    return jnp.stack([((zl + dz) % 2) * 4 + (x + dx) % 4 for dz, dx in pairs]).astype(jnp.int32)


def head_norm_rotate(values, gain, cosine, sine):
    scale = lax.rsqrt(jnp.mean(values * values, axis=-1, keepdims=True) + EPSILON)
    scaled = values * scale * gain
    half = values.shape[-1] // 2
    return scaled * cosine + pltpu.roll(scaled, half, 1) * sine


def project_kernel(ids, *refs):
    pieces, rest = refs[:8], refs[8:]
    (gain, wq, wg, wk, wv, q_gain, k_gain, cosine, sine, q_out, g_out, k_out, v_out, scaled) = rest
    rows, width = pieces[0].shape
    head = wk.shape[1]
    edges = [0]
    for w in (wq, wg, wk, wv):
        edges.append(edges[-1] + w.shape[1])

    @pl.when(pl.program_id(0) == 0)
    def _():
        for j in range(8):
            block = pl.multiple_of(ids[j] * width, width)
            here = pl.ds(block, width)
            for w, first, last in zip((wq, wg, wk, wv), edges, edges[1:]):
                part = w[here, :].astype(jnp.float32) * gain[here, :]
                scaled[j * width : (j + 1) * width, first:last] = part.astype(jnp.bfloat16)

    total = jnp.zeros((rows, 128), jnp.float32)
    product = jnp.zeros((rows, edges[-1]), jnp.float32)
    for j, piece in enumerate(pieces):
        value = piece[...]
        product = product + jnp.dot(
            value, scaled[j * width : (j + 1) * width, :], preferred_element_type=jnp.float32
        )
        value = value.astype(jnp.float32)
        square = value * value
        for first in range(0, width, 128):
            total = total + square[:, first : first + 128]
    total = jnp.sum(total, axis=-1, keepdims=True)
    product = product * lax.rsqrt(total / (8 * width) + EPSILON)
    cos, sin = cosine[...], sine[...]
    for h in range(edges[1] // head):
        here = slice(h * head, (h + 1) * head)
        part = head_norm_rotate(product[:, here], q_gain[...], cos, sin)
        q_out[:, here] = part.astype(jnp.bfloat16)
    g_out[...] = jax.nn.sigmoid(product[:, edges[1] : edges[2]])
    k = head_norm_rotate(product[:, edges[2] : edges[3]], k_gain[...], cos, sin)
    k_out[...] = k.astype(jnp.bfloat16)
    v_out[...] = product[:, edges[3] : edges[4]].astype(jnp.bfloat16)


def project(ids, pieces, gain, wq, wg, wk, wv, q_gain, k_gain, cosine, sine):
    rows, width = pieces[0].shape
    depth = gain.shape[0]
    head = q_gain.shape[0]
    tile = lambda columns: pl.BlockSpec((ROW_TILE, columns), lambda i, _: (i, 0))
    whole = lambda a: pl.BlockSpec(a.shape, lambda i, _: (0, 0))
    q_gain, k_gain = q_gain.reshape(1, head), k_gain.reshape(1, head)
    constants = (gain.reshape(depth, 1), wq, wg, wk, wv, q_gain, k_gain)
    columns = sum(w.shape[1] for w in (wq, wg, wk, wv))
    return pl.pallas_call(
        project_kernel,
        out_shape=(
            jax.ShapeDtypeStruct((rows, wq.shape[1]), jnp.bfloat16),
            jax.ShapeDtypeStruct((rows, wg.shape[1]), jnp.float32),
            jax.ShapeDtypeStruct((rows, head), jnp.bfloat16),
            jax.ShapeDtypeStruct((rows, head), jnp.bfloat16),
        ),
        grid_spec=pltpu.PrefetchScalarGridSpec(
            num_scalar_prefetch=1,
            grid=(rows // ROW_TILE,),
            in_specs=[tile(width)] * 8 + [whole(a) for a in constants] + [tile(head)] * 2,
            out_specs=[tile(wq.shape[1]), tile(wg.shape[1]), tile(head), tile(head)],
            scratch_shapes=[pltpu.VMEM((depth, columns), jnp.bfloat16)],
        ),
        compiler_params=pltpu.CompilerParams(vmem_limit_bytes=40 << 20),
        cost_estimate=COST,
        name="project",
    )(ids, *pieces, *constants, cosine, sine)


def attend_kernel(starts, lengths, q, g, k, v, *refs):
    key_parts, value_parts = refs[:4], refs[4:8]
    out, keys, values = refs[8:]
    head = k.shape[1]
    span = q.shape[0] // BATCH
    shares = q.shape[1] // head
    size = key_parts[0].shape[0]
    window = keys.shape[0] - 4 * size
    score_scale = 1.0 / math.sqrt(head)
    contract = (((1,), (1,)), ((), ()))

    @pl.when(pl.program_id(0) == 0)
    def _():
        for j in range(4):
            keys[j * size : (j + 1) * size, :] = key_parts[j][...]
            values[j * size : (j + 1) * size, :] = value_parts[j][...]
        keys[4 * size :, :] = jnp.zeros((window, head), keys.dtype)
        values[4 * size :, :] = jnp.zeros((window, head), values.dtype)

    column = lax.broadcasted_iota(jnp.int32, (shares * span, window), 1)
    old_row = lax.broadcasted_iota(jnp.int32, (window, head), 0)
    token = lax.broadcasted_iota(jnp.int32, (shares, span, window), 1)
    token = token.reshape(shares * span, window)
    together = window // span
    for b in range(BATCH):
        r = pl.program_id(0) * BATCH + b
        length = lengths[r]
        rows = slice(b * span, (b + 1) * span)
        first = b // together * together
        both = slice(first * span, (first + together) * span)
        own = column - (b - first) * span
        query = jnp.concatenate([q[rows, s * head : (s + 1) * head] for s in range(shares)], axis=0)
        place = pl.ds(pl.multiple_of(starts[r], UNIT), window)
        old_keys, old_values = keys[place, :], values[place, :]
        old_values = jnp.where(old_row < length, old_values, jnp.zeros_like(old_values))
        old = lax.dot_general(query, old_keys, contract, preferred_element_type=jnp.float32)
        new = lax.dot_general(query, k[both, :], contract, preferred_element_type=jnp.float32)
        old = jnp.where(column < length, old * score_scale, -jnp.inf)
        new = jnp.where((own >= 0) & (own <= token), new * score_scale, -jnp.inf)
        row_max = jnp.max(jnp.maximum(old, new), axis=-1, keepdims=True)
        old, new = jnp.exp(old - row_max), jnp.exp(new - row_max)
        row_total = jnp.sum(old + new, axis=-1, keepdims=True)
        mixed = jnp.dot(old.astype(jnp.bfloat16), old_values, preferred_element_type=jnp.float32)
        mixed += jnp.dot(new.astype(jnp.bfloat16), v[both, :], preferred_element_type=jnp.float32)
        mixed = mixed / row_total
        for s in range(shares):
            columns = slice(s * head, (s + 1) * head)
            part = mixed[s * span : (s + 1) * span] * g[rows, columns]
            out[rows, columns] = part.astype(jnp.bfloat16)


def attend(starts, lengths, q, g, k, v, keys, values, window):
    rows, columns = q.shape
    head = k.shape[1]
    step = rows // lengths.shape[0] * BATCH
    tile = lambda width: pl.BlockSpec((step, width), lambda i, *_: (i, 0))
    whole = lambda a: pl.BlockSpec(a.shape, lambda i, *_: (0, 0))
    store = pltpu.VMEM((4 * keys[0].shape[0] + window, head), keys[0].dtype)
    return pl.pallas_call(
        attend_kernel,
        out_shape=jax.ShapeDtypeStruct((rows, columns), jnp.bfloat16),
        grid_spec=pltpu.PrefetchScalarGridSpec(
            num_scalar_prefetch=2,
            grid=(rows // step,),
            in_specs=[tile(columns)] * 2 + [tile(head)] * 2 + [whole(a) for a in keys + values],
            out_specs=tile(columns),
            scratch_shapes=[store, store],
        ),
        compiler_params=pltpu.CompilerParams(vmem_limit_bytes=40 << 20),
        cost_estimate=COST,
        name="attend",
    )(starts, lengths, q, g, k, v, *keys, *values)


def pack_kernel(offsets, own, twin, *refs):
    received, outs, store = refs[:3], refs[3:7], refs[7]
    window, head = own.shape[4:]
    slots = own.shape[3]
    size = outs[0].shape[0]
    for k, out in enumerate(outs):
        block = offsets[k]
        for j in range(4 * 2 * slots):
            p, side, rank = j // (2 * slots), j // slots % 2, j % slots
            place = pl.multiple_of(offsets[6 + k * 4 * 2 * slots + j], UNIT)
            if p > 0:
                value = received[p - 1][side, block, rank]
            elif side > 0:
                value = twin[0, block, rank]
            else:
                value = own[0, block, 0, rank]
            store[pl.ds(place, window), :] = value
        out[...] = store[:size, :]


def pack(offsets, cache, twin, received, size):
    capacity, window, head = cache.shape[3:]
    return pl.pallas_call(
        pack_kernel,
        out_shape=[jax.ShapeDtypeStruct((size, head), cache.dtype)] * 4,
        grid_spec=pltpu.PrefetchScalarGridSpec(
            num_scalar_prefetch=1,
            grid=(1,),
            in_specs=[
                pl.BlockSpec((1, 4, 1, capacity, window, head), lambda i, o: (o[4], 0, o[5], 0, 0, 0)),
                pl.BlockSpec((1, 4, capacity, window, head), lambda i, o: (o[4], 0, 0, 0, 0)),
            ]
            + [pl.BlockSpec(a.shape, lambda i, _: (0,) * 5) for a in received],
            out_specs=[pl.BlockSpec((size, head), lambda i, _: (0, 0))] * 4,
            scratch_shapes=[pltpu.VMEM((size + window, head), cache.dtype)],
        ),
        compiler_params=pltpu.CompilerParams(vmem_limit_bytes=30 << 20),
        cost_estimate=COST,
        name="pack",
    )(offsets, cache, twin, *received)


def copy_kernel(_, *refs):
    for source, target in zip(refs, refs[len(refs) // 2 :]):
        target[...] = source[...].reshape(target.shape)


def for_twin(place, caches):
    _, _, _, capacity, window, head = caches[0].shape
    return pl.pallas_call(
        copy_kernel,
        out_shape=[jax.ShapeDtypeStruct((4, 4, capacity, window, head), caches[0].dtype)] * 2,
        grid_spec=pltpu.PrefetchScalarGridSpec(
            num_scalar_prefetch=1,
            grid=(4,),
            in_specs=[
                pl.BlockSpec((1, 4, 1, capacity, window, head), lambda i, o: (i, 0, 1 - o[1], 0, 0, 0))
            ]
            * 2,
            out_specs=[pl.BlockSpec((1, 4, capacity, window, head), lambda i, _: (i, 0, 0, 0, 0))] * 2,
        ),
        cost_estimate=COST,
        name="for_twin",
    )(place, *caches)


def arrange_kernel(_, *refs):
    for own, twin, out in zip(refs[:3], refs[3:6], refs[6:]):
        out[0] = own[0, :, 0]
        out[1] = twin[0]


def arrange(place, cache, twin):
    capacity, window, head = cache.shape[3:]
    own = lambda k: pl.BlockSpec(
        (1, 4, 1, capacity, window, head), lambda i, o: ((o[0] + k) % 4, 0, o[1], 0, 0, 0)
    )
    other = lambda k: pl.BlockSpec(
        (1, 4, capacity, window, head), lambda i, o: ((o[0] + k) % 4, 0, 0, 0, 0)
    )
    shape = (2, 4, capacity, window, head)
    return pl.pallas_call(
        arrange_kernel,
        out_shape=[jax.ShapeDtypeStruct(shape, cache.dtype)] * 3,
        grid_spec=pltpu.PrefetchScalarGridSpec(
            num_scalar_prefetch=1,
            grid=(1,),
            in_specs=[own(k) for k in (1, 3, 2)] + [other(k) for k in (1, 3, 2)],
            out_specs=[pl.BlockSpec(shape, lambda i, _: (0,) * 5)] * 3,
        ),
        compiler_params=pltpu.CompilerParams(vmem_limit_bytes=20 << 20),
        cost_estimate=COST,
        name="arrange",
    )(place, cache, cache, cache, twin, twin, twin)


def output_kernel(place, heads, mine, other, out, joined):
    count, depth = mine.shape[:2]

    @pl.when(pl.program_id(0) == 0)
    def _():
        for j in range(count):
            for h in range(2):
                first = pl.multiple_of((place[1] + h) % 2 * depth, depth)
                columns = slice((2 * j + h) * depth, (2 * j + h + 1) * depth)
                joined[:, columns] = heads[j, :, pl.ds(first, depth)]

    total = jnp.zeros(out.shape, jnp.float32)
    for j in range(count):
        weight = jnp.concatenate([mine[j], other[j]], axis=0)
        part = joined[:, 2 * j * depth : 2 * (j + 1) * depth]
        total = total + jnp.dot(part, weight, preferred_element_type=jnp.float32)
    out[...] = total.astype(jnp.bfloat16)


def project_out(place, heads, mine, other):
    blocks, rows, width = heads.shape
    depth, columns = mine.shape[1:]
    tile = 512
    half = pl.BlockSpec((blocks, depth, tile), lambda i, _: (0, 0, i))
    return pl.pallas_call(
        output_kernel,
        out_shape=jax.ShapeDtypeStruct((rows, columns), jnp.bfloat16),
        grid_spec=pltpu.PrefetchScalarGridSpec(
            num_scalar_prefetch=1,
            grid=(columns // tile,),
            in_specs=[pl.BlockSpec(heads.shape, lambda i, _: (0, 0, 0)), half, half],
            out_specs=pl.BlockSpec((rows, tile), lambda i, _: (0, i)),
            scratch_shapes=[pltpu.VMEM((rows, blocks * width), jnp.bfloat16)],
        ),
        compiler_params=pltpu.CompilerParams(vmem_limit_bytes=30 << 20),
        cost_estimate=COST,
        name="project_out",
    )(place, heads, mine, other)


def across_y(place, cache, twin):
    return [shift(a, "y", k) for a, k in zip(arrange(place, cache, twin), (1, 3, 2))]


def across_z(parts):
    return [parts[0]] + [shift(parts[k], "zh", k) for k in range(1, 4)]


def local(
    span_rows,
    norm_gain,
    q_weight,
    gate_weight,
    k_weight,
    v_weight,
    q_norm_gain,
    k_norm_gain,
    o_weight,
    key_cache,
    value_cache,
    holders,
    prefix_lengths,
):
    groups = lax.axis_size(GROUP)
    group_id = lax.axis_index(GROUP)
    requests = prefix_lengths.shape[0] // groups
    rows = span_rows.shape[0]
    span_len = rows // requests
    head_dim = q_norm_gain.shape[0]
    capacity = key_cache.shape[1] // groups
    window = key_cache.shape[2]
    blocks = lax.axis_size(TENSOR)

    y, zh, core = lax.axis_index("y"), lax.axis_index("zh"), lax.axis_index("c")
    all_holders = holders.reshape(groups, requests)
    all_lengths = prefix_lengths.reshape(groups, requests)
    order = jnp.arange(requests)
    earlier = order[None, :] < order[:, None]
    same = all_holders[:, :, None] == all_holders[:, None, :]
    all_ranks = jnp.sum(same & earlier[None], axis=2)
    all_units = (all_lengths + UNIT - 1) // UNIT
    plane = all_holders // 2 % 4
    per_plane = jnp.sum(
        jnp.where(plane[:, :, None] == jnp.arange(4), all_units[:, :, None], 0), axis=1
    )
    fits = jnp.max(per_plane) * UNIT <= PACKED

    seen_y, seen_c = jnp.array([0, 3, 1, 2]), jnp.array([0, 1])
    slot_y = (y + seen_y[:, None, None]) % 4
    slot_c = (core + seen_c[None, :, None]) % 2
    slot_rank = jnp.arange(capacity)[None, None, :]
    z_ids = (zh + jnp.arange(4)) % 4
    served = (y * 4 + z_ids) * 2 + core
    slot_holder = (slot_y * 4 + zh) * 2 + slot_c
    slot_key = (slot_holder * capacity + slot_rank).reshape(-1)
    served_key = (all_holders * capacity + all_ranks)[served]
    hit = served_key[:, :, None] == slot_key[None, None, :]
    slot_units = jnp.sum(jnp.where(hit, all_units[served][:, :, None], 0), axis=1)
    offsets = (jnp.cumsum(slot_units, axis=1) - slot_units) * UNIT
    place = jnp.stack([y, core]).astype(jnp.int32)

    mine = lambda a: lax.dynamic_index_in_dim(a, group_id, 0, keepdims=False)
    my_holders, my_ranks, my_lengths, my_units = map(
        mine, (all_holders, all_ranks, all_lengths, all_units)
    )
    from_y = (my_holders // 8 - y) % 4
    from_y = jnp.where(from_y == 3, 1, jnp.where(from_y == 1, 2, jnp.where(from_y == 2, 3, 0)))
    from_z = (zh - my_holders // 2 % 4) % 4
    from_c = (my_holders - core) % 2
    my_order = (from_y * 2 + from_c) * capacity + my_ranks
    ahead = (from_z[:, None] == from_z[None, :]) & (my_order[None, :] < my_order[:, None])
    my_start = jnp.sum(jnp.where(ahead, my_units[None, :], 0), axis=1) * UNIT

    def packing(size):
        limit = jnp.minimum(offsets, size).reshape(-1)
        places = jnp.concatenate([z_ids, place, limit]).astype(jnp.int32)
        starts = jnp.minimum(from_z * size + my_start, 4 * size)
        return places, starts.astype(jnp.int32)

    positions = my_lengths[:, None] + jnp.arange(span_len, dtype=jnp.int32)[None, :]
    half = head_dim // 2
    frequency = ROPE_BASE ** (-jnp.arange(half, dtype=jnp.float32) * 2.0 / head_dim)
    angles = positions.reshape(-1).astype(jnp.float32)[:, None] * frequency
    cosine, sine = jnp.cos(angles), jnp.sin(angles)
    cosine = jnp.concatenate([cosine, cosine], axis=-1)
    sine = jnp.concatenate([-sine, sine], axis=-1)

    ids = block_ids()
    sides = (4, 4, 2, capacity, window, head_dim)
    caches = [key_cache.reshape(sides), value_cache.reshape(sides)]
    twins = [shift(a, "c", 1) for a in for_twin(place, caches)]
    places, starts = packing(PACKED)
    pieces = spread(span_rows)

    key_parts = across_y(place, caches[0], twins[0])
    value_parts = across_y(place, caches[1], twins[1])
    keys = across_z(pack(places, caches[0], twins[0], key_parts, PACKED))
    values = across_z(pack(places, caches[1], twins[1], value_parts, PACKED))

    depth = o_weight.shape[0] // 2
    half = lax.dynamic_slice_in_dim(o_weight, core * depth, depth, 0)
    halves = lax.all_gather(half, TENSOR)
    other_halves = shift(halves, "c", 1)

    q, g, k, v = project(
        ids, pieces, norm_gain, q_weight, gate_weight, k_weight, v_weight,
        q_norm_gain, k_norm_gain, cosine, sine,
    )

    def packed(keys, values, twins, key_parts, value_parts, q, g, k, v):
        return attend(starts, my_lengths, q, g, k, v, keys, values, window)

    def full(keys, values, twins, key_parts, value_parts, q, g, k, v):
        size = 8 * capacity * window
        places, starts = packing(size)
        keys = across_z(pack(places, caches[0], twins[0], key_parts, size))
        values = across_z(pack(places, caches[1], twins[1], value_parts, size))
        return attend(starts, my_lengths, q, g, k, v, keys, values, window)

    q, other_halves = lax.optimization_barrier((q, other_halves))
    attended = lax.cond(fits, packed, full, keys, values, twins, key_parts, value_parts, q, g, k, v)
    heads = lax.all_to_all(
        attended.reshape(blocks, rows // blocks, attended.shape[1]), TENSOR, 0, 0, tiled=True
    )
    return project_out(place, heads, halves, other_halves)


def solution(mesh):
    mesh = Mesh(mesh.devices.reshape(4, 4, 2, 2, 4), GROUP + TENSOR)
    placed = (
        P(GROUP, TENSOR),
        P(),
        P(None, TENSOR),
        P(None, TENSOR),
        P(None, TENSOR),
        P(None, TENSOR),
        P(),
        P(),
        P(TENSOR, None),
        P(GROUP, None, None, TENSOR),
        P(GROUP, None, None, TENSOR),
        P(),
        P(),
    )
    return jax.shard_map(
        local, mesh=mesh, in_specs=placed, out_specs=P(GROUP + TENSOR, None), check_vma=False
    )
```

```python
import functools
import math

import jax
import jax.numpy as jnp
from jax import lax
from jax.experimental import pallas as pl
from jax.experimental.pallas import tpu as pltpu
from jax.sharding import Mesh
from jax.sharding import PartitionSpec as P

EPSILON = 1e-06
ROPE_BASE = 1000000.0
GROUP = ("y", "zh", "c")
TENSOR = ("zl", "x")
ROW_TILE = 256
BATCH = 4
UNIT = 16
PACKED = 72 * UNIT
COST = pl.CostEstimate(flops=1 << 20, bytes_accessed=1 << 20, transcendentals=0)


def ring(size, step):
    return [(i, (i + step) % size) for i in range(size)]


def shift(value, axis, step):
    return lax.ppermute(value, axis, ring(lax.axis_size(axis), step))


def spread(block):
    twin = shift(block, "zl", 1)
    below, above = shift(block, "x", 1), shift(block, "x", -1)
    twin_below, twin_above = shift(twin, "x", 1), shift(twin, "x", -1)
    far = shift(below, "x", 1)
    twin_far = shift(twin_above, "x", -1)
    return [block, twin, below, above, twin_below, twin_above, far, twin_far]


def block_ids():
    zl, x = lax.axis_index("zl"), lax.axis_index("x")
    pairs = [(0, 0), (1, 0), (0, 3), (0, 1), (1, 3), (1, 1), (0, 2), (1, 2)]
    return jnp.stack([((zl + dz) % 2) * 4 + (x + dx) % 4 for dz, dx in pairs]).astype(jnp.int32)


def head_norm_rotate(values, gain, cosine, sine):
    scale = lax.rsqrt(jnp.mean(values * values, axis=-1, keepdims=True) + EPSILON)
    scaled = values * scale * gain
    half = values.shape[-1] // 2
    return scaled * cosine + pltpu.roll(scaled, half, 1) * sine


def project_kernel(ids, *refs):
    pieces, rest = refs[:8], refs[8:]
    (gain, wq, wg, wk, wv, q_gain, k_gain, cosine, sine, q_out, g_out, k_out, v_out, scaled) = rest
    rows, width = pieces[0].shape
    head = wk.shape[1]
    edges = [0]
    for w in (wq, wg, wk, wv):
        edges.append(edges[-1] + w.shape[1])

    @pl.when(pl.program_id(0) == 0)
    def _():
        for j in range(8):
            block = pl.multiple_of(ids[j] * width, width)
            here = pl.ds(block, width)
            for w, first, last in zip((wq, wg, wk, wv), edges, edges[1:]):
                part = w[here, :].astype(jnp.float32) * gain[here, :]
                scaled[j * width : (j + 1) * width, first:last] = part.astype(jnp.bfloat16)

    total = jnp.zeros((rows, 128), jnp.float32)
    product = jnp.zeros((rows, edges[-1]), jnp.float32)
    for j, piece in enumerate(pieces):
        value = piece[...]
        product = product + jnp.dot(
            value, scaled[j * width : (j + 1) * width, :], preferred_element_type=jnp.float32
        )
        value = value.astype(jnp.float32)
        square = value * value
        for first in range(0, width, 128):
            total = total + square[:, first : first + 128]
    total = jnp.sum(total, axis=-1, keepdims=True)
    product = product * lax.rsqrt(total / (8 * width) + EPSILON)
    cos, sin = cosine[...], sine[...]
    for h in range(edges[1] // head):
        here = slice(h * head, (h + 1) * head)
        part = head_norm_rotate(product[:, here], q_gain[...], cos, sin)
        q_out[:, here] = part.astype(jnp.bfloat16)
    g_out[...] = jax.nn.sigmoid(product[:, edges[1] : edges[2]])
    k = head_norm_rotate(product[:, edges[2] : edges[3]], k_gain[...], cos, sin)
    k_out[...] = k.astype(jnp.bfloat16)
    v_out[...] = product[:, edges[3] : edges[4]].astype(jnp.bfloat16)


def project(ids, pieces, gain, wq, wg, wk, wv, q_gain, k_gain, cosine, sine):
    rows, width = pieces[0].shape
    depth = gain.shape[0]
    head = q_gain.shape[0]
    tile = lambda columns: pl.BlockSpec((ROW_TILE, columns), lambda i, _: (i, 0))
    whole = lambda a: pl.BlockSpec(a.shape, lambda i, _: (0, 0))
    q_gain, k_gain = q_gain.reshape(1, head), k_gain.reshape(1, head)
    constants = (gain.reshape(depth, 1), wq, wg, wk, wv, q_gain, k_gain)
    columns = sum(w.shape[1] for w in (wq, wg, wk, wv))
    return pl.pallas_call(
        project_kernel,
        out_shape=(
            jax.ShapeDtypeStruct((rows, wq.shape[1]), jnp.bfloat16),
            jax.ShapeDtypeStruct((rows, wg.shape[1]), jnp.float32),
            jax.ShapeDtypeStruct((rows, head), jnp.bfloat16),
            jax.ShapeDtypeStruct((rows, head), jnp.bfloat16),
        ),
        grid_spec=pltpu.PrefetchScalarGridSpec(
            num_scalar_prefetch=1,
            grid=(rows // ROW_TILE,),
            in_specs=[tile(width)] * 8 + [whole(a) for a in constants] + [tile(head)] * 2,
            out_specs=[tile(wq.shape[1]), tile(wg.shape[1]), tile(head), tile(head)],
            scratch_shapes=[pltpu.VMEM((depth, columns), jnp.bfloat16)],
        ),
        compiler_params=pltpu.CompilerParams(vmem_limit_bytes=40 << 20),
        cost_estimate=COST,
        name="project",
    )(ids, *pieces, *constants, cosine, sine)


def attend_kernel(starts, lengths, q, g, k, v, *refs):
    key_parts, value_parts = refs[:4], refs[4:8]
    out, keys, values = refs[8:]
    head = k.shape[1]
    span = q.shape[0] // BATCH
    shares = q.shape[1] // head
    size = key_parts[0].shape[0]
    window = keys.shape[0] - 4 * size
    score_scale = 1.0 / math.sqrt(head)
    contract = (((1,), (1,)), ((), ()))

    @pl.when(pl.program_id(0) == 0)
    def _():
        for j in range(4):
            keys[j * size : (j + 1) * size, :] = key_parts[j][...]
            values[j * size : (j + 1) * size, :] = value_parts[j][...]
        keys[4 * size :, :] = jnp.zeros((window, head), keys.dtype)
        values[4 * size :, :] = jnp.zeros((window, head), values.dtype)

    column = lax.broadcasted_iota(jnp.int32, (shares * span, window), 1)
    old_row = lax.broadcasted_iota(jnp.int32, (window, head), 0)
    token = lax.broadcasted_iota(jnp.int32, (shares, span, window), 1)
    token = token.reshape(shares * span, window)
    together = window // span
    for b in range(BATCH):
        r = pl.program_id(0) * BATCH + b
        length = lengths[r]
        rows = slice(b * span, (b + 1) * span)
        first = b // together * together
        both = slice(first * span, (first + together) * span)
        own = column - (b - first) * span
        query = jnp.concatenate([q[rows, s * head : (s + 1) * head] for s in range(shares)], axis=0)
        place = pl.ds(pl.multiple_of(starts[r], UNIT), window)
        old_keys, old_values = keys[place, :], values[place, :]
        old_values = jnp.where(old_row < length, old_values, jnp.zeros_like(old_values))
        old = lax.dot_general(query, old_keys, contract, preferred_element_type=jnp.float32)
        new = lax.dot_general(query, k[both, :], contract, preferred_element_type=jnp.float32)
        old = jnp.where(column < length, old * score_scale, -jnp.inf)
        new = jnp.where((own >= 0) & (own <= token), new * score_scale, -jnp.inf)
        row_max = jnp.max(jnp.maximum(old, new), axis=-1, keepdims=True)
        old, new = jnp.exp(old - row_max), jnp.exp(new - row_max)
        row_total = jnp.sum(old + new, axis=-1, keepdims=True)
        mixed = jnp.dot(old.astype(jnp.bfloat16), old_values, preferred_element_type=jnp.float32)
        mixed += jnp.dot(new.astype(jnp.bfloat16), v[both, :], preferred_element_type=jnp.float32)
        mixed = mixed / row_total
        for s in range(shares):
            columns = slice(s * head, (s + 1) * head)
            part = mixed[s * span : (s + 1) * span] * g[rows, columns]
            out[rows, columns] = part.astype(jnp.bfloat16)


def attend(starts, lengths, q, g, k, v, keys, values, window):
    rows, columns = q.shape
    head = k.shape[1]
    step = rows // lengths.shape[0] * BATCH
    tile = lambda width: pl.BlockSpec((step, width), lambda i, *_: (i, 0))
    whole = lambda a: pl.BlockSpec(a.shape, lambda i, *_: (0, 0))
    store = pltpu.VMEM((4 * keys[0].shape[0] + window, head), keys[0].dtype)
    return pl.pallas_call(
        attend_kernel,
        out_shape=jax.ShapeDtypeStruct((rows, columns), jnp.bfloat16),
        grid_spec=pltpu.PrefetchScalarGridSpec(
            num_scalar_prefetch=2,
            grid=(rows // step,),
            in_specs=[tile(columns)] * 2 + [tile(head)] * 2 + [whole(a) for a in keys + values],
            out_specs=tile(columns),
            scratch_shapes=[store, store],
        ),
        compiler_params=pltpu.CompilerParams(vmem_limit_bytes=40 << 20),
        cost_estimate=COST,
        name="attend",
    )(starts, lengths, q, g, k, v, *keys, *values)


def pack_kernel(offsets, cache, *refs):
    outs, store = refs[:4], refs[4]
    sources, _, slots, window, head = cache.shape
    size = outs[0].shape[0]
    for k, out in enumerate(outs):
        for j in range(sources * slots):
            place = pl.multiple_of(offsets[4 + k * sources * slots + j], UNIT)
            store[pl.ds(place, window), :] = cache[j // slots, offsets[k], j % slots]
        out[...] = store[:size, :]


def pack(offsets, cache, size):
    window, head = cache.shape[3:]
    return pl.pallas_call(
        pack_kernel,
        out_shape=[jax.ShapeDtypeStruct((size, head), cache.dtype)] * 4,
        grid_spec=pltpu.PrefetchScalarGridSpec(
            num_scalar_prefetch=1,
            grid=(1,),
            in_specs=[pl.BlockSpec(cache.shape, lambda i, _: (0,) * 5)],
            out_specs=[pl.BlockSpec((size, head), lambda i, _: (0, 0))] * 4,
            scratch_shapes=[pltpu.VMEM((size + window, head), cache.dtype)],
        ),
        compiler_params=pltpu.CompilerParams(vmem_limit_bytes=30 << 20),
        cost_estimate=COST,
        name="pack",
    )(offsets, cache)


def by_target_kernel(source, target):
    for c in range(2):
        target[0, c] = source[0, :, c]


def by_target(cache):
    ny, nz, nc, capacity, window, head = cache.shape
    return pl.pallas_call(
        by_target_kernel,
        out_shape=jax.ShapeDtypeStruct((ny, nc, nz, capacity, window, head), cache.dtype),
        grid=(ny,),
        in_specs=[pl.BlockSpec((1, nz, nc, capacity, window, head), lambda i: (i, 0, 0, 0, 0, 0))],
        out_specs=pl.BlockSpec((1, nc, nz, capacity, window, head), lambda i: (i, 0, 0, 0, 0, 0)),
        cost_estimate=COST,
        name="by_target",
    )(cache)


def output_kernel(heads, weight, out, joined):
    width = heads.shape[2]

    @pl.when(pl.program_id(0) == 0)
    def _():
        for j in range(heads.shape[0]):
            joined[:, j * width : (j + 1) * width] = heads[j]

    total = jnp.dot(joined[...], weight[...], preferred_element_type=jnp.float32)
    out[...] = total.astype(jnp.bfloat16)


def project_out(heads, weight):
    blocks, rows, width = heads.shape
    depth, columns = weight.shape
    tile = 512
    return pl.pallas_call(
        output_kernel,
        out_shape=jax.ShapeDtypeStruct((rows, columns), jnp.bfloat16),
        grid=(columns // tile,),
        in_specs=[
            pl.BlockSpec(heads.shape, lambda i: (0, 0, 0)),
            pl.BlockSpec((depth, tile), lambda i: (0, i)),
        ],
        out_specs=pl.BlockSpec((rows, tile), lambda i: (0, i)),
        scratch_shapes=[pltpu.VMEM((rows, depth), jnp.bfloat16)],
        compiler_params=pltpu.CompilerParams(vmem_limit_bytes=30 << 20),
        cost_estimate=COST,
        name="project_out",
    )(heads, weight)


def across_y(cache):
    _, nz, _, capacity, window, head = cache.shape
    flat = by_target(cache).reshape(8, nz * capacity * window, head)
    return lax.all_to_all(flat, ("y", "c"), 0, 0, tiled=True).reshape(8, nz, capacity, window, head)


def across_z(parts):
    return [parts[0]] + [shift(parts[k], "zh", k) for k in range(1, 4)]


def local(
    span_rows,
    norm_gain,
    q_weight,
    gate_weight,
    k_weight,
    v_weight,
    q_norm_gain,
    k_norm_gain,
    o_weight,
    key_cache,
    value_cache,
    holders,
    prefix_lengths,
):
    groups = lax.axis_size(GROUP)
    group_id = lax.axis_index(GROUP)
    requests = prefix_lengths.shape[0] // groups
    rows = span_rows.shape[0]
    span_len = rows // requests
    head_dim = q_norm_gain.shape[0]
    capacity = key_cache.shape[1] // groups
    window = key_cache.shape[2]
    blocks = lax.axis_size(TENSOR)

    y, zh, core = lax.axis_index("y"), lax.axis_index("zh"), lax.axis_index("c")
    all_holders = holders.reshape(groups, requests)
    all_lengths = prefix_lengths.reshape(groups, requests)
    order = jnp.arange(requests)
    earlier = order[None, :] < order[:, None]
    same = all_holders[:, :, None] == all_holders[:, None, :]
    all_ranks = jnp.sum(same & earlier[None], axis=2)
    all_units = (all_lengths + UNIT - 1) // UNIT
    plane = all_holders // 2 % 4
    per_plane = jnp.sum(
        jnp.where(plane[:, :, None] == jnp.arange(4), all_units[:, :, None], 0), axis=1
    )
    fits = jnp.max(per_plane) * UNIT <= PACKED

    slot_y = jnp.arange(4)[:, None, None]
    slot_c = jnp.arange(2)[None, :, None]
    slot_rank = jnp.arange(capacity)[None, None, :]
    z_ids = (zh + jnp.arange(4)) % 4
    served = (y * 4 + z_ids) * 2 + core
    slot_holder = (slot_y * 4 + zh) * 2 + slot_c
    slot_key = (slot_holder * capacity + slot_rank).reshape(-1)
    served_key = (all_holders * capacity + all_ranks)[served]
    hit = served_key[:, :, None] == slot_key[None, None, :]
    slot_units = jnp.sum(jnp.where(hit, all_units[served][:, :, None], 0), axis=1)
    offsets = (jnp.cumsum(slot_units, axis=1) - slot_units) * UNIT

    mine = lambda a: lax.dynamic_index_in_dim(a, group_id, 0, keepdims=False)
    my_holders, my_ranks, my_lengths, my_units = map(
        mine, (all_holders, all_ranks, all_lengths, all_units)
    )
    from_z = (zh - my_holders // 2 % 4) % 4
    my_order = (my_holders // 8 * 2 + my_holders % 2) * capacity + my_ranks
    ahead = (from_z[:, None] == from_z[None, :]) & (my_order[None, :] < my_order[:, None])
    my_start = jnp.sum(jnp.where(ahead, my_units[None, :], 0), axis=1) * UNIT

    def packing(size):
        limit = jnp.minimum(offsets, size).reshape(-1)
        places = jnp.concatenate([z_ids, limit]).astype(jnp.int32)
        starts = jnp.minimum(from_z * size + my_start, 4 * size)
        return places, starts.astype(jnp.int32)

    positions = my_lengths[:, None] + jnp.arange(span_len, dtype=jnp.int32)[None, :]
    channel = jnp.arange(head_dim)
    half = head_dim // 2
    frequency = ROPE_BASE ** (-(channel % half).astype(jnp.float32) * 2.0 / head_dim)
    angles = positions.reshape(-1).astype(jnp.float32)[:, None] * frequency
    cosine = jnp.cos(angles)
    sine = jnp.sin(angles) * jnp.where(channel < half, -1.0, 1.0)

    ids = block_ids()
    sides = (4, 4, 2, capacity, window, head_dim)
    places, starts = packing(PACKED)
    whole_weight = lax.all_gather(o_weight, TENSOR, axis=0, tiled=True)
    pieces = spread(span_rows)
    key_part, value_part = across_y(key_cache.reshape(sides)), across_y(value_cache.reshape(sides))
    keys = across_z(pack(places, key_part, PACKED))
    values = across_z(pack(places, value_part, PACKED))

    q, g, k, v = project(
        ids, pieces, norm_gain, q_weight, gate_weight, k_weight, v_weight,
        q_norm_gain, k_norm_gain, cosine, sine,
    )

    def packed(keys, values, key_part, value_part, q, g, k, v):
        return attend(starts, my_lengths, q, g, k, v, keys, values, window)

    def full(keys, values, key_part, value_part, q, g, k, v):
        size = 8 * capacity * window
        places, starts = packing(size)
        keys, values = (across_z(pack(places, a, size)) for a in (key_part, value_part))
        return attend(starts, my_lengths, q, g, k, v, keys, values, window)

    attended = lax.cond(fits, packed, full, keys, values, key_part, value_part, q, g, k, v)
    heads = lax.all_to_all(
        attended.reshape(blocks, rows // blocks, attended.shape[1]), TENSOR, 0, 0, tiled=True
    )
    return project_out(heads, whole_weight)


def solution(mesh):
    mesh = Mesh(mesh.devices.reshape(4, 4, 2, 2, 4), GROUP + TENSOR)
    placed = (
        P(GROUP, TENSOR),
        P(),
        P(None, TENSOR),
        P(None, TENSOR),
        P(None, TENSOR),
        P(None, TENSOR),
        P(),
        P(),
        P(TENSOR, None),
        P(GROUP, None, None, TENSOR),
        P(GROUP, None, None, TENSOR),
        P(),
        P(),
    )
    return jax.shard_map(
        local, mesh=mesh, in_specs=placed, out_specs=P(GROUP + TENSOR, None), check_vma=False
    )
```

```python
import functools
import math

import jax
import jax.numpy as jnp
from jax import lax
from jax.experimental import pallas as pl
from jax.experimental.pallas import tpu as pltpu
from jax.sharding import Mesh
from jax.sharding import PartitionSpec as P

EPSILON = 1e-06
ROPE_BASE = 1000000.0
GROUP = ("y", "zh", "c")
TENSOR = ("zl", "x")
ROW_TILE = 256
BATCH = 4
UNIT = 16
PACKED = 72 * UNIT
COST = pl.CostEstimate(flops=1 << 20, bytes_accessed=1 << 20, transcendentals=0)


def ring(size, step):
    return [(i, (i + step) % size) for i in range(size)]


def shift(value, axis, step):
    return lax.ppermute(value, axis, ring(lax.axis_size(axis), step))


def spread(block):
    twin = shift(block, "zl", 1)
    below, above = shift(block, "x", 1), shift(block, "x", -1)
    twin_below, twin_above = shift(twin, "x", 1), shift(twin, "x", -1)
    far = shift(below, "x", 1)
    twin_far = shift(twin_above, "x", -1)
    return [block, twin, below, above, twin_below, twin_above, far, twin_far]


def block_ids():
    zl, x = lax.axis_index("zl"), lax.axis_index("x")
    pairs = [(0, 0), (1, 0), (0, 3), (0, 1), (1, 3), (1, 1), (0, 2), (1, 2)]
    return jnp.stack([((zl + dz) % 2) * 4 + (x + dx) % 4 for dz, dx in pairs]).astype(jnp.int32)


def head_norm_rotate(values, gain, cosine, sine):
    scale = lax.rsqrt(jnp.mean(values * values, axis=-1, keepdims=True) + EPSILON)
    scaled = values * scale * gain
    half = values.shape[-1] // 2
    return scaled * cosine + pltpu.roll(scaled, half, 1) * sine


def project_kernel(ids, *refs):
    pieces, rest = refs[:8], refs[8:]
    (gain, wq, wg, wk, wv, q_gain, k_gain, cosine, sine, q_out, g_out, k_out, v_out, scaled) = rest
    rows, width = pieces[0].shape
    head = wk.shape[1]
    edges = [0]
    for w in (wq, wg, wk, wv):
        edges.append(edges[-1] + w.shape[1])

    @pl.when(pl.program_id(0) == 0)
    def _():
        for j in range(8):
            block = pl.multiple_of(ids[j] * width, width)
            here = pl.ds(block, width)
            for w, first, last in zip((wq, wg, wk, wv), edges, edges[1:]):
                part = w[here, :].astype(jnp.float32) * gain[here, :]
                scaled[j * width : (j + 1) * width, first:last] = part.astype(jnp.bfloat16)

    total = jnp.zeros((rows, 128), jnp.float32)
    product = jnp.zeros((rows, edges[-1]), jnp.float32)
    for j, piece in enumerate(pieces):
        value = piece[...]
        product = product + jnp.dot(
            value, scaled[j * width : (j + 1) * width, :], preferred_element_type=jnp.float32
        )
        value = value.astype(jnp.float32)
        square = value * value
        for first in range(0, width, 128):
            total = total + square[:, first : first + 128]
    total = jnp.sum(total, axis=-1, keepdims=True)
    product = product * lax.rsqrt(total / (8 * width) + EPSILON)
    cos, sin = cosine[...], sine[...]
    for h in range(edges[1] // head):
        here = slice(h * head, (h + 1) * head)
        part = head_norm_rotate(product[:, here], q_gain[...], cos, sin)
        q_out[:, here] = part.astype(jnp.bfloat16)
    g_out[...] = jax.nn.sigmoid(product[:, edges[1] : edges[2]])
    k = head_norm_rotate(product[:, edges[2] : edges[3]], k_gain[...], cos, sin)
    k_out[...] = k.astype(jnp.bfloat16)
    v_out[...] = product[:, edges[3] : edges[4]].astype(jnp.bfloat16)


def project(ids, pieces, gain, wq, wg, wk, wv, q_gain, k_gain, cosine, sine):
    rows, width = pieces[0].shape
    depth = gain.shape[0]
    head = q_gain.shape[0]
    tile = lambda columns: pl.BlockSpec((ROW_TILE, columns), lambda i, _: (i, 0))
    whole = lambda a: pl.BlockSpec(a.shape, lambda i, _: (0, 0))
    q_gain, k_gain = q_gain.reshape(1, head), k_gain.reshape(1, head)
    constants = (gain.reshape(depth, 1), wq, wg, wk, wv, q_gain, k_gain)
    columns = sum(w.shape[1] for w in (wq, wg, wk, wv))
    return pl.pallas_call(
        project_kernel,
        out_shape=(
            jax.ShapeDtypeStruct((rows, wq.shape[1]), jnp.bfloat16),
            jax.ShapeDtypeStruct((rows, wg.shape[1]), jnp.float32),
            jax.ShapeDtypeStruct((rows, head), jnp.bfloat16),
            jax.ShapeDtypeStruct((rows, head), jnp.bfloat16),
        ),
        grid_spec=pltpu.PrefetchScalarGridSpec(
            num_scalar_prefetch=1,
            grid=(rows // ROW_TILE,),
            in_specs=[tile(width)] * 8 + [whole(a) for a in constants] + [tile(head)] * 2,
            out_specs=[tile(wq.shape[1]), tile(wg.shape[1]), tile(head), tile(head)],
            scratch_shapes=[pltpu.VMEM((depth, columns), jnp.bfloat16)],
        ),
        compiler_params=pltpu.CompilerParams(vmem_limit_bytes=40 << 20),
        cost_estimate=COST,
        name="project",
    )(ids, *pieces, *constants, cosine, sine)


def attend_kernel(starts, lengths, q, g, k, v, *refs):
    key_parts, value_parts = refs[:4], refs[4:8]
    out, keys, values = refs[8:]
    head = k.shape[1]
    span = q.shape[0] // BATCH
    shares = q.shape[1] // head
    size = key_parts[0].shape[0]
    window = keys.shape[0] - 4 * size
    score_scale = 1.0 / math.sqrt(head)
    contract = (((1,), (1,)), ((), ()))

    @pl.when(pl.program_id(0) == 0)
    def _():
        for j in range(4):
            keys[j * size : (j + 1) * size, :] = key_parts[j][...]
            values[j * size : (j + 1) * size, :] = value_parts[j][...]
        keys[4 * size :, :] = jnp.zeros((window, head), keys.dtype)
        values[4 * size :, :] = jnp.zeros((window, head), values.dtype)

    column = lax.broadcasted_iota(jnp.int32, (shares * span, window), 1)
    old_row = lax.broadcasted_iota(jnp.int32, (window, head), 0)
    token = lax.broadcasted_iota(jnp.int32, (shares, span, window), 1)
    token = token.reshape(shares * span, window)
    together = window // span
    for b in range(BATCH):
        r = pl.program_id(0) * BATCH + b
        length = lengths[r]
        rows = slice(b * span, (b + 1) * span)
        first = b // together * together
        both = slice(first * span, (first + together) * span)
        own = column - (b - first) * span
        query = jnp.concatenate([q[rows, s * head : (s + 1) * head] for s in range(shares)], axis=0)
        place = pl.ds(pl.multiple_of(starts[r], UNIT), window)
        old_keys, old_values = keys[place, :], values[place, :]
        old_values = jnp.where(old_row < length, old_values, jnp.zeros_like(old_values))
        old = lax.dot_general(query, old_keys, contract, preferred_element_type=jnp.float32)
        new = lax.dot_general(query, k[both, :], contract, preferred_element_type=jnp.float32)
        old = jnp.where(column < length, old * score_scale, -jnp.inf)
        new = jnp.where((own >= 0) & (own <= token), new * score_scale, -jnp.inf)
        row_max = jnp.max(jnp.maximum(old, new), axis=-1, keepdims=True)
        old, new = jnp.exp(old - row_max), jnp.exp(new - row_max)
        row_total = jnp.sum(old + new, axis=-1, keepdims=True)
        mixed = jnp.dot(old.astype(jnp.bfloat16), old_values, preferred_element_type=jnp.float32)
        mixed += jnp.dot(new.astype(jnp.bfloat16), v[both, :], preferred_element_type=jnp.float32)
        mixed = mixed / row_total
        for s in range(shares):
            columns = slice(s * head, (s + 1) * head)
            part = mixed[s * span : (s + 1) * span] * g[rows, columns]
            out[rows, columns] = part.astype(jnp.bfloat16)


def attend(starts, lengths, q, g, k, v, keys, values, window):
    rows, columns = q.shape
    head = k.shape[1]
    step = rows // lengths.shape[0] * BATCH
    tile = lambda width: pl.BlockSpec((step, width), lambda i, *_: (i, 0))
    whole = lambda a: pl.BlockSpec(a.shape, lambda i, *_: (0, 0))
    store = pltpu.VMEM((4 * keys[0].shape[0] + window, head), keys[0].dtype)
    return pl.pallas_call(
        attend_kernel,
        out_shape=jax.ShapeDtypeStruct((rows, columns), jnp.bfloat16),
        grid_spec=pltpu.PrefetchScalarGridSpec(
            num_scalar_prefetch=2,
            grid=(rows // step,),
            in_specs=[tile(columns)] * 2 + [tile(head)] * 2 + [whole(a) for a in keys + values],
            out_specs=tile(columns),
            scratch_shapes=[store, store],
        ),
        compiler_params=pltpu.CompilerParams(vmem_limit_bytes=40 << 20),
        cost_estimate=COST,
        name="attend",
    )(starts, lengths, q, g, k, v, *keys, *values)


def pack_kernel(offsets, cache, *refs):
    outs, store = refs[:4], refs[4]
    sources, _, slots, window, head = cache.shape
    size = outs[0].shape[0]
    for k, out in enumerate(outs):
        for j in range(sources * slots):
            place = pl.multiple_of(offsets[4 + k * sources * slots + j], UNIT)
            store[pl.ds(place, window), :] = cache[j // slots, offsets[k], j % slots]
        out[...] = store[:size, :]


def pack(offsets, cache, size):
    window, head = cache.shape[3:]
    return pl.pallas_call(
        pack_kernel,
        out_shape=[jax.ShapeDtypeStruct((size, head), cache.dtype)] * 4,
        grid_spec=pltpu.PrefetchScalarGridSpec(
            num_scalar_prefetch=1,
            grid=(1,),
            in_specs=[pl.BlockSpec(cache.shape, lambda i, _: (0,) * 5)],
            out_specs=[pl.BlockSpec((size, head), lambda i, _: (0, 0))] * 4,
            scratch_shapes=[pltpu.VMEM((size + window, head), cache.dtype)],
        ),
        compiler_params=pltpu.CompilerParams(vmem_limit_bytes=30 << 20),
        cost_estimate=COST,
        name="pack",
    )(offsets, cache)


def by_target_kernel(source, target):
    for c in range(2):
        target[0, c] = source[0, :, c]


def by_target(cache):
    ny, nz, nc, capacity, window, head = cache.shape
    return pl.pallas_call(
        by_target_kernel,
        out_shape=jax.ShapeDtypeStruct((ny, nc, nz, capacity, window, head), cache.dtype),
        grid=(ny,),
        in_specs=[pl.BlockSpec((1, nz, nc, capacity, window, head), lambda i: (i, 0, 0, 0, 0, 0))],
        out_specs=pl.BlockSpec((1, nc, nz, capacity, window, head), lambda i: (i, 0, 0, 0, 0, 0)),
        cost_estimate=COST,
        name="by_target",
    )(cache)


def output_kernel(place, heads, mine, other, out, joined):
    count, depth = mine.shape[:2]

    @pl.when(pl.program_id(0) == 0)
    def _():
        for j in range(count):
            for h in range(2):
                first = pl.multiple_of((place[1] + h) % 2 * depth, depth)
                columns = slice((2 * j + h) * depth, (2 * j + h + 1) * depth)
                joined[:, columns] = heads[j, :, pl.ds(first, depth)]

    total = jnp.zeros(out.shape, jnp.float32)
    for j in range(count):
        weight = jnp.concatenate([mine[j], other[j]], axis=0)
        part = joined[:, 2 * j * depth : 2 * (j + 1) * depth]
        total = total + jnp.dot(part, weight, preferred_element_type=jnp.float32)
    out[...] = total.astype(jnp.bfloat16)


def project_out(place, heads, mine, other):
    blocks, rows, width = heads.shape
    depth, columns = mine.shape[1:]
    tile = 512
    half = pl.BlockSpec((blocks, depth, tile), lambda i, _: (0, 0, i))
    return pl.pallas_call(
        output_kernel,
        out_shape=jax.ShapeDtypeStruct((rows, columns), jnp.bfloat16),
        grid_spec=pltpu.PrefetchScalarGridSpec(
            num_scalar_prefetch=1,
            grid=(columns // tile,),
            in_specs=[pl.BlockSpec(heads.shape, lambda i, _: (0, 0, 0)), half, half],
            out_specs=pl.BlockSpec((rows, tile), lambda i, _: (0, i)),
            scratch_shapes=[pltpu.VMEM((rows, blocks * width), jnp.bfloat16)],
        ),
        compiler_params=pltpu.CompilerParams(vmem_limit_bytes=30 << 20),
        cost_estimate=COST,
        name="project_out",
    )(place, heads, mine, other)


def across_y(slots):
    ny, nc, nz, capacity, window, head = slots.shape
    flat = slots.reshape(ny * nc, nz * capacity * window, head)
    flat = lax.all_to_all(flat, ("y", "c"), 0, 0, tiled=True)
    return flat.reshape(ny * nc, nz, capacity, window, head)


def across_z(parts):
    return [parts[0]] + [shift(parts[k], "zh", k) for k in range(1, 4)]


def local(
    span_rows,
    norm_gain,
    q_weight,
    gate_weight,
    k_weight,
    v_weight,
    q_norm_gain,
    k_norm_gain,
    o_weight,
    key_cache,
    value_cache,
    holders,
    prefix_lengths,
):
    groups = lax.axis_size(GROUP)
    group_id = lax.axis_index(GROUP)
    requests = prefix_lengths.shape[0] // groups
    rows = span_rows.shape[0]
    span_len = rows // requests
    head_dim = q_norm_gain.shape[0]
    capacity = key_cache.shape[1] // groups
    window = key_cache.shape[2]
    blocks = lax.axis_size(TENSOR)

    y, zh, core = lax.axis_index("y"), lax.axis_index("zh"), lax.axis_index("c")
    all_holders = holders.reshape(groups, requests)
    all_lengths = prefix_lengths.reshape(groups, requests)
    order = jnp.arange(requests)
    earlier = order[None, :] < order[:, None]
    same = all_holders[:, :, None] == all_holders[:, None, :]
    all_ranks = jnp.sum(same & earlier[None], axis=2)
    all_units = (all_lengths + UNIT - 1) // UNIT
    plane = all_holders // 2 % 4
    per_plane = jnp.sum(
        jnp.where(plane[:, :, None] == jnp.arange(4), all_units[:, :, None], 0), axis=1
    )
    fits = jnp.max(per_plane) * UNIT <= PACKED

    slot_y = jnp.arange(4)[:, None, None]
    slot_c = jnp.arange(2)[None, :, None]
    slot_rank = jnp.arange(capacity)[None, None, :]
    z_ids = (zh + jnp.arange(4)) % 4
    served = (y * 4 + z_ids) * 2 + core
    slot_holder = (slot_y * 4 + zh) * 2 + slot_c
    slot_key = (slot_holder * capacity + slot_rank).reshape(-1)
    served_key = (all_holders * capacity + all_ranks)[served]
    hit = served_key[:, :, None] == slot_key[None, None, :]
    slot_units = jnp.sum(jnp.where(hit, all_units[served][:, :, None], 0), axis=1)
    offsets = (jnp.cumsum(slot_units, axis=1) - slot_units) * UNIT

    mine = lambda a: lax.dynamic_index_in_dim(a, group_id, 0, keepdims=False)
    my_holders, my_ranks, my_lengths, my_units = map(
        mine, (all_holders, all_ranks, all_lengths, all_units)
    )
    from_z = (zh - my_holders // 2 % 4) % 4
    my_order = (my_holders // 8 * 2 + my_holders % 2) * capacity + my_ranks
    ahead = (from_z[:, None] == from_z[None, :]) & (my_order[None, :] < my_order[:, None])
    my_start = jnp.sum(jnp.where(ahead, my_units[None, :], 0), axis=1) * UNIT

    def packing(size):
        limit = jnp.minimum(offsets, size).reshape(-1)
        places = jnp.concatenate([z_ids, limit]).astype(jnp.int32)
        starts = jnp.minimum(from_z * size + my_start, 4 * size)
        return places, starts.astype(jnp.int32)

    positions = my_lengths[:, None] + jnp.arange(span_len, dtype=jnp.int32)[None, :]
    channel = jnp.arange(head_dim)
    half = head_dim // 2
    frequency = ROPE_BASE ** (-(channel % half).astype(jnp.float32) * 2.0 / head_dim)
    angles = positions.reshape(-1).astype(jnp.float32)[:, None] * frequency
    cosine = jnp.cos(angles)
    sine = jnp.sin(angles) * jnp.where(channel < half, -1.0, 1.0)

    ids = block_ids()
    sides = (4, 4, 2, capacity, window, head_dim)
    places, starts = packing(PACKED)
    pieces = spread(span_rows)
    key_part = across_y(by_target(key_cache.reshape(sides)))
    value_slots, key_part, pieces[1:4] = lax.optimization_barrier(
        (by_target(value_cache.reshape(sides)), key_part, pieces[1:4])
    )
    value_part = across_y(value_slots)
    keys = across_z(pack(places, key_part, PACKED))

    depth = o_weight.shape[0] // 2
    half = lax.dynamic_slice_in_dim(o_weight, core * depth, depth, 0)
    half, value_part, keys, pieces[4:] = lax.optimization_barrier(
        (half, value_part, keys, pieces[4:])
    )
    copies = jnp.broadcast_to(half, (blocks,) + half.shape)
    halves = lax.all_to_all(copies, TENSOR, 0, 0, tiled=True)
    other_halves = shift(halves, "c", 1)

    values = across_z(pack(places, value_part, PACKED))

    q, g, k, v = project(
        ids, pieces, norm_gain, q_weight, gate_weight, k_weight, v_weight,
        q_norm_gain, k_norm_gain, cosine, sine,
    )

    def packed(keys, values, key_part, value_part, q, g, k, v):
        return attend(starts, my_lengths, q, g, k, v, keys, values, window)

    def full(keys, values, key_part, value_part, q, g, k, v):
        size = 8 * capacity * window
        places, starts = packing(size)
        keys, values = (across_z(pack(places, a, size)) for a in (key_part, value_part))
        return attend(starts, my_lengths, q, g, k, v, keys, values, window)

    attended = lax.cond(fits, packed, full, keys, values, key_part, value_part, q, g, k, v)
    heads = lax.all_to_all(
        attended.reshape(blocks, rows // blocks, attended.shape[1]), TENSOR, 0, 0, tiled=True
    )
    place = jnp.stack([y, core]).astype(jnp.int32)
    return project_out(place, heads, halves, other_halves)


def solution(mesh):
    mesh = Mesh(mesh.devices.reshape(4, 4, 2, 2, 4), GROUP + TENSOR)
    placed = (
        P(GROUP, TENSOR),
        P(),
        P(None, TENSOR),
        P(None, TENSOR),
        P(None, TENSOR),
        P(None, TENSOR),
        P(),
        P(),
        P(TENSOR, None),
        P(GROUP, None, None, TENSOR),
        P(GROUP, None, None, TENSOR),
        P(),
        P(),
    )
    return jax.shard_map(
        local, mesh=mesh, in_specs=placed, out_specs=P(GROUP + TENSOR, None), check_vma=False
    )
```

```python
import functools
import math

import jax
import jax.numpy as jnp
from jax import lax
from jax.experimental import pallas as pl
from jax.experimental.pallas import tpu as pltpu
from jax.sharding import Mesh
from jax.sharding import PartitionSpec as P

EPSILON = 1e-06
ROPE_BASE = 1000000.0
GROUP = ("y", "zh", "c")
TENSOR = ("zl", "x")
ROW_TILE = 256
BATCH = 4
UNIT = 16
PACKED = 72 * UNIT
COST = pl.CostEstimate(flops=1 << 20, bytes_accessed=1 << 20, transcendentals=0)


def ring(size, step):
    return [(i, (i + step) % size) for i in range(size)]


def shift(value, axis, step):
    return lax.ppermute(value, axis, ring(lax.axis_size(axis), step))


def spread(block):
    twin = shift(block, "zl", 1)
    below, above = shift(block, "x", 1), shift(block, "x", -1)
    twin_below, twin_above = shift(twin, "x", 1), shift(twin, "x", -1)
    far = shift(below, "x", 1)
    twin_far = shift(twin_above, "x", -1)
    return [block, twin, below, above, twin_below, twin_above, far, twin_far]


def block_ids():
    zl, x = lax.axis_index("zl"), lax.axis_index("x")
    pairs = [(0, 0), (1, 0), (0, 3), (0, 1), (1, 3), (1, 1), (0, 2), (1, 2)]
    return jnp.stack([((zl + dz) % 2) * 4 + (x + dx) % 4 for dz, dx in pairs]).astype(jnp.int32)


def head_norm_rotate(values, gain, cosine, sine):
    scale = lax.rsqrt(jnp.mean(values * values, axis=-1, keepdims=True) + EPSILON)
    scaled = values * scale * gain
    half = values.shape[-1] // 2
    return scaled * cosine + pltpu.roll(scaled, half, 1) * sine


def project_kernel(ids, *refs):
    pieces, rest = refs[:8], refs[8:]
    (gain, wq, wg, wk, wv, q_gain, k_gain, cosine, sine, q_out, g_out, k_out, v_out, scaled) = rest
    rows, width = pieces[0].shape
    head = wk.shape[1]
    edges = [0]
    for w in (wq, wg, wk, wv):
        edges.append(edges[-1] + w.shape[1])

    @pl.when(pl.program_id(0) == 0)
    def _():
        for j in range(8):
            block = pl.multiple_of(ids[j] * width, width)
            here = pl.ds(block, width)
            for w, first, last in zip((wq, wg, wk, wv), edges, edges[1:]):
                part = w[here, :].astype(jnp.float32) * gain[here, :]
                scaled[j * width : (j + 1) * width, first:last] = part.astype(jnp.bfloat16)

    total = jnp.zeros((rows, 128), jnp.float32)
    product = jnp.zeros((rows, edges[-1]), jnp.float32)
    for j, piece in enumerate(pieces):
        value = piece[...]
        product = product + jnp.dot(
            value, scaled[j * width : (j + 1) * width, :], preferred_element_type=jnp.float32
        )
        value = value.astype(jnp.float32)
        square = value * value
        for first in range(0, width, 128):
            total = total + square[:, first : first + 128]
    total = jnp.sum(total, axis=-1, keepdims=True)
    product = product * lax.rsqrt(total / (8 * width) + EPSILON)
    cos, sin = cosine[...], sine[...]
    for h in range(edges[1] // head):
        here = slice(h * head, (h + 1) * head)
        part = head_norm_rotate(product[:, here], q_gain[...], cos, sin)
        q_out[:, here] = part.astype(jnp.bfloat16)
    g_out[...] = jax.nn.sigmoid(product[:, edges[1] : edges[2]])
    k = head_norm_rotate(product[:, edges[2] : edges[3]], k_gain[...], cos, sin)
    k_out[...] = k.astype(jnp.bfloat16)
    v_out[...] = product[:, edges[3] : edges[4]].astype(jnp.bfloat16)


def project(ids, pieces, gain, wq, wg, wk, wv, q_gain, k_gain, cosine, sine):
    rows, width = pieces[0].shape
    depth = gain.shape[0]
    head = q_gain.shape[0]
    tile = lambda columns: pl.BlockSpec((ROW_TILE, columns), lambda i, _: (i, 0))
    whole = lambda a: pl.BlockSpec(a.shape, lambda i, _: (0, 0))
    q_gain, k_gain = q_gain.reshape(1, head), k_gain.reshape(1, head)
    constants = (gain.reshape(depth, 1), wq, wg, wk, wv, q_gain, k_gain)
    columns = sum(w.shape[1] for w in (wq, wg, wk, wv))
    return pl.pallas_call(
        project_kernel,
        out_shape=(
            jax.ShapeDtypeStruct((rows, wq.shape[1]), jnp.bfloat16),
            jax.ShapeDtypeStruct((rows, wg.shape[1]), jnp.float32),
            jax.ShapeDtypeStruct((rows, head), jnp.bfloat16),
            jax.ShapeDtypeStruct((rows, head), jnp.bfloat16),
        ),
        grid_spec=pltpu.PrefetchScalarGridSpec(
            num_scalar_prefetch=1,
            grid=(rows // ROW_TILE,),
            in_specs=[tile(width)] * 8 + [whole(a) for a in constants] + [tile(head)] * 2,
            out_specs=[tile(wq.shape[1]), tile(wg.shape[1]), tile(head), tile(head)],
            scratch_shapes=[pltpu.VMEM((depth, columns), jnp.bfloat16)],
        ),
        compiler_params=pltpu.CompilerParams(vmem_limit_bytes=40 << 20),
        cost_estimate=COST,
        name="project",
    )(ids, *pieces, *constants, cosine, sine)


def attend_kernel(starts, lengths, q, g, k, v, *refs):
    key_parts, value_parts = refs[:4], refs[4:8]
    out, keys, values = refs[8:]
    head = k.shape[1]
    span = q.shape[0] // BATCH
    shares = q.shape[1] // head
    size = key_parts[0].shape[0]
    window = keys.shape[0] - 4 * size
    score_scale = 1.0 / math.sqrt(head)
    contract = (((1,), (1,)), ((), ()))

    @pl.when(pl.program_id(0) == 0)
    def _():
        for j in range(4):
            keys[j * size : (j + 1) * size, :] = key_parts[j][...]
            values[j * size : (j + 1) * size, :] = value_parts[j][...]
        keys[4 * size :, :] = jnp.zeros((window, head), keys.dtype)
        values[4 * size :, :] = jnp.zeros((window, head), values.dtype)

    column = lax.broadcasted_iota(jnp.int32, (shares * span, window), 1)
    old_row = lax.broadcasted_iota(jnp.int32, (window, head), 0)
    token = lax.broadcasted_iota(jnp.int32, (shares, span, window), 1)
    token = token.reshape(shares * span, window)
    together = window // span
    for b in range(BATCH):
        r = pl.program_id(0) * BATCH + b
        length = lengths[r]
        rows = slice(b * span, (b + 1) * span)
        first = b // together * together
        both = slice(first * span, (first + together) * span)
        own = column - (b - first) * span
        query = jnp.concatenate([q[rows, s * head : (s + 1) * head] for s in range(shares)], axis=0)
        place = pl.ds(pl.multiple_of(starts[r], UNIT), window)
        old_keys, old_values = keys[place, :], values[place, :]
        old_values = jnp.where(old_row < length, old_values, jnp.zeros_like(old_values))
        old = lax.dot_general(query, old_keys, contract, preferred_element_type=jnp.float32)
        new = lax.dot_general(query, k[both, :], contract, preferred_element_type=jnp.float32)
        old = jnp.where(column < length, old * score_scale, -jnp.inf)
        new = jnp.where((own >= 0) & (own <= token), new * score_scale, -jnp.inf)
        row_max = jnp.max(jnp.maximum(old, new), axis=-1, keepdims=True)
        old, new = jnp.exp(old - row_max), jnp.exp(new - row_max)
        row_total = jnp.sum(old + new, axis=-1, keepdims=True)
        mixed = jnp.dot(old.astype(jnp.bfloat16), old_values, preferred_element_type=jnp.float32)
        mixed += jnp.dot(new.astype(jnp.bfloat16), v[both, :], preferred_element_type=jnp.float32)
        mixed = mixed / row_total
        for s in range(shares):
            columns = slice(s * head, (s + 1) * head)
            part = mixed[s * span : (s + 1) * span] * g[rows, columns]
            out[rows, columns] = part.astype(jnp.bfloat16)


def attend(starts, lengths, q, g, k, v, keys, values, window):
    rows, columns = q.shape
    head = k.shape[1]
    step = rows // lengths.shape[0] * BATCH
    tile = lambda width: pl.BlockSpec((step, width), lambda i, *_: (i, 0))
    whole = lambda a: pl.BlockSpec(a.shape, lambda i, *_: (0, 0))
    store = pltpu.VMEM((4 * keys[0].shape[0] + window, head), keys[0].dtype)
    return pl.pallas_call(
        attend_kernel,
        out_shape=jax.ShapeDtypeStruct((rows, columns), jnp.bfloat16),
        grid_spec=pltpu.PrefetchScalarGridSpec(
            num_scalar_prefetch=2,
            grid=(rows // step,),
            in_specs=[tile(columns)] * 2 + [tile(head)] * 2 + [whole(a) for a in keys + values],
            out_specs=tile(columns),
            scratch_shapes=[store, store],
        ),
        compiler_params=pltpu.CompilerParams(vmem_limit_bytes=40 << 20),
        cost_estimate=COST,
        name="attend",
    )(starts, lengths, q, g, k, v, *keys, *values)


def pack_kernel(offsets, cache, *refs):
    outs, store = refs[:4], refs[4]
    sources, _, slots, window, head = cache.shape
    size = outs[0].shape[0]
    for k, out in enumerate(outs):
        for j in range(sources * slots):
            place = pl.multiple_of(offsets[4 + k * sources * slots + j], UNIT)
            store[pl.ds(place, window), :] = cache[j // slots, offsets[k], j % slots]
        out[...] = store[:size, :]


def pack(offsets, cache, size):
    window, head = cache.shape[3:]
    return pl.pallas_call(
        pack_kernel,
        out_shape=[jax.ShapeDtypeStruct((size, head), cache.dtype)] * 4,
        grid_spec=pltpu.PrefetchScalarGridSpec(
            num_scalar_prefetch=1,
            grid=(1,),
            in_specs=[pl.BlockSpec(cache.shape, lambda i, _: (0,) * 5)],
            out_specs=[pl.BlockSpec((size, head), lambda i, _: (0, 0))] * 4,
            scratch_shapes=[pltpu.VMEM((size + window, head), cache.dtype)],
        ),
        compiler_params=pltpu.CompilerParams(vmem_limit_bytes=30 << 20),
        cost_estimate=COST,
        name="pack",
    )(offsets, cache)


def by_target_kernel(source, target):
    for c in range(2):
        target[0, c] = source[0, :, c]


def by_target(cache):
    ny, nz, nc, capacity, window, head = cache.shape
    return pl.pallas_call(
        by_target_kernel,
        out_shape=jax.ShapeDtypeStruct((ny, nc, nz, capacity, window, head), cache.dtype),
        grid=(ny,),
        in_specs=[pl.BlockSpec((1, nz, nc, capacity, window, head), lambda i: (i, 0, 0, 0, 0, 0))],
        out_specs=pl.BlockSpec((1, nc, nz, capacity, window, head), lambda i: (i, 0, 0, 0, 0, 0)),
        cost_estimate=COST,
        name="by_target",
    )(cache)


def copies_kernel(half, twin, out):
    out[0, 0], out[0, 1] = half[...], twin[...]


def copies(half, twin):
    depth, columns = half.shape
    whole = pl.BlockSpec((depth, columns), lambda i: (0, 0))
    return pl.pallas_call(
        copies_kernel,
        out_shape=jax.ShapeDtypeStruct((4, 2, depth, columns), half.dtype),
        grid=(4,),
        in_specs=[whole, whole],
        out_specs=pl.BlockSpec((1, 2, depth, columns), lambda i: (i, 0, 0, 0)),
        cost_estimate=COST,
        name="copies",
    )(half, twin)


def output_kernel(places, heads, mine, other, out, joined):
    count, depth = mine.shape[:2]

    @pl.when(pl.program_id(0) == 0)
    def _():
        for j in range(count):
            for h in range(2):
                first = pl.multiple_of((places[count] + h) % 2 * depth, depth)
                columns = slice((2 * j + h) * depth, (2 * j + h + 1) * depth)
                joined[:, columns] = heads[places[j], :, pl.ds(first, depth)]

    total = jnp.zeros(out.shape, jnp.float32)
    for j in range(count):
        weight = jnp.concatenate([mine[j], other[j]], axis=0)
        part = joined[:, 2 * j * depth : 2 * (j + 1) * depth]
        total = total + jnp.dot(part, weight, preferred_element_type=jnp.float32)
    out[...] = total.astype(jnp.bfloat16)


def project_out(places, heads, mine, other):
    blocks, rows, width = heads.shape
    depth, columns = mine.shape[1:]
    tile = 512
    half = pl.BlockSpec((blocks, depth, tile), lambda i, _: (0, 0, i))
    return pl.pallas_call(
        output_kernel,
        out_shape=jax.ShapeDtypeStruct((rows, columns), jnp.bfloat16),
        grid_spec=pltpu.PrefetchScalarGridSpec(
            num_scalar_prefetch=1,
            grid=(columns // tile,),
            in_specs=[pl.BlockSpec(heads.shape, lambda i, _: (0, 0, 0)), half, half],
            out_specs=pl.BlockSpec((rows, tile), lambda i, _: (0, i)),
            scratch_shapes=[pltpu.VMEM((rows, blocks * width), jnp.bfloat16)],
        ),
        compiler_params=pltpu.CompilerParams(vmem_limit_bytes=30 << 20),
        cost_estimate=COST,
        name="project_out",
    )(places, heads, mine, other)


def across_y(slots):
    ny, nc, nz, capacity, window, head = slots.shape
    flat = slots.reshape(ny * nc, nz * capacity * window, head)
    flat = lax.all_to_all(flat, ("y", "c"), 0, 0, tiled=True)
    return flat.reshape(ny * nc, nz, capacity, window, head)


def across_z(parts):
    return [parts[0]] + [shift(parts[k], "zh", k) for k in range(1, 4)]


def local(
    span_rows,
    norm_gain,
    q_weight,
    gate_weight,
    k_weight,
    v_weight,
    q_norm_gain,
    k_norm_gain,
    o_weight,
    key_cache,
    value_cache,
    holders,
    prefix_lengths,
):
    groups = lax.axis_size(GROUP)
    group_id = lax.axis_index(GROUP)
    requests = prefix_lengths.shape[0] // groups
    rows = span_rows.shape[0]
    span_len = rows // requests
    head_dim = q_norm_gain.shape[0]
    capacity = key_cache.shape[1] // groups
    window = key_cache.shape[2]
    blocks = lax.axis_size(TENSOR)

    y, zh, core = lax.axis_index("y"), lax.axis_index("zh"), lax.axis_index("c")
    all_holders = holders.reshape(groups, requests)
    all_lengths = prefix_lengths.reshape(groups, requests)
    order = jnp.arange(requests)
    earlier = order[None, :] < order[:, None]
    same = all_holders[:, :, None] == all_holders[:, None, :]
    all_ranks = jnp.sum(same & earlier[None], axis=2)
    all_units = (all_lengths + UNIT - 1) // UNIT
    plane = all_holders // 2 % 4
    per_plane = jnp.sum(
        jnp.where(plane[:, :, None] == jnp.arange(4), all_units[:, :, None], 0), axis=1
    )
    fits = jnp.max(per_plane) * UNIT <= PACKED

    slot_y = jnp.arange(4)[:, None, None]
    slot_c = jnp.arange(2)[None, :, None]
    slot_rank = jnp.arange(capacity)[None, None, :]
    z_ids = (zh + jnp.arange(4)) % 4
    served = (y * 4 + z_ids) * 2 + core
    slot_holder = (slot_y * 4 + zh) * 2 + slot_c
    slot_key = (slot_holder * capacity + slot_rank).reshape(-1)
    served_key = (all_holders * capacity + all_ranks)[served]
    hit = served_key[:, :, None] == slot_key[None, None, :]
    slot_units = jnp.sum(jnp.where(hit, all_units[served][:, :, None], 0), axis=1)
    offsets = (jnp.cumsum(slot_units, axis=1) - slot_units) * UNIT

    mine = lambda a: lax.dynamic_index_in_dim(a, group_id, 0, keepdims=False)
    my_holders, my_ranks, my_lengths, my_units = map(
        mine, (all_holders, all_ranks, all_lengths, all_units)
    )
    from_z = (zh - my_holders // 2 % 4) % 4
    my_order = (my_holders // 8 * 2 + my_holders % 2) * capacity + my_ranks
    ahead = (from_z[:, None] == from_z[None, :]) & (my_order[None, :] < my_order[:, None])
    my_start = jnp.sum(jnp.where(ahead, my_units[None, :], 0), axis=1) * UNIT

    def packing(size):
        limit = jnp.minimum(offsets, size).reshape(-1)
        places = jnp.concatenate([z_ids, limit]).astype(jnp.int32)
        starts = jnp.minimum(from_z * size + my_start, 4 * size)
        return places, starts.astype(jnp.int32)

    positions = my_lengths[:, None] + jnp.arange(span_len, dtype=jnp.int32)[None, :]
    channel = jnp.arange(head_dim)
    half = head_dim // 2
    frequency = ROPE_BASE ** (-(channel % half).astype(jnp.float32) * 2.0 / head_dim)
    angles = positions.reshape(-1).astype(jnp.float32)[:, None] * frequency
    cosine = jnp.cos(angles)
    sine = jnp.sin(angles) * jnp.where(channel < half, -1.0, 1.0)

    ids = block_ids()
    sides = (4, 4, 2, capacity, window, head_dim)
    places, starts = packing(PACKED)
    pieces = spread(span_rows)
    depth = o_weight.shape[0] // 2
    half = lax.dynamic_slice_in_dim(o_weight, core * depth, depth, 0)
    half, pieces[1] = lax.optimization_barrier((half, pieces[1]))
    twin_half = shift(half, "zl", 1)

    key_part = across_y(by_target(key_cache.reshape(sides)))
    value_slots, key_part, pieces[1:6], twin_half = lax.optimization_barrier(
        (by_target(value_cache.reshape(sides)), key_part, pieces[1:6], twin_half)
    )
    value_part = across_y(value_slots)
    keys = across_z(pack(places, key_part, PACKED))
    repeated, value_part, keys, pieces[6:] = lax.optimization_barrier(
        (copies(half, twin_half), value_part, keys, pieces[6:])
    )
    packed_values = pack(places, value_part, PACKED)
    repeated, packed_values = lax.optimization_barrier((repeated, packed_values))
    halves = lax.all_to_all(repeated, "x", 0, 0, tiled=True)
    halves = halves.reshape((blocks,) + half.shape)
    other_halves = shift(halves, "c", 1)

    values = across_z(packed_values)

    q, g, k, v = project(
        ids, pieces, norm_gain, q_weight, gate_weight, k_weight, v_weight,
        q_norm_gain, k_norm_gain, cosine, sine,
    )

    def packed(keys, values, key_part, value_part, q, g, k, v):
        return attend(starts, my_lengths, q, g, k, v, keys, values, window)

    def full(keys, values, key_part, value_part, q, g, k, v):
        size = 8 * capacity * window
        places, starts = packing(size)
        keys, values = (across_z(pack(places, a, size)) for a in (key_part, value_part))
        return attend(starts, my_lengths, q, g, k, v, keys, values, window)

    attended = lax.cond(fits, packed, full, keys, values, key_part, value_part, q, g, k, v)
    heads = lax.all_to_all(
        attended.reshape(blocks, rows // blocks, attended.shape[1]), TENSOR, 0, 0, tiled=True
    )
    x_ids, zl_ids = jnp.arange(blocks) // 2, (lax.axis_index("zl") + jnp.arange(blocks)) % 2
    out_places = jnp.concatenate([zl_ids * 4 + x_ids, core[None]]).astype(jnp.int32)
    return project_out(out_places, heads, halves, other_halves)


def solution(mesh):
    mesh = Mesh(mesh.devices.reshape(4, 4, 2, 2, 4), GROUP + TENSOR)
    placed = (
        P(GROUP, TENSOR),
        P(),
        P(None, TENSOR),
        P(None, TENSOR),
        P(None, TENSOR),
        P(None, TENSOR),
        P(),
        P(),
        P(TENSOR, None),
        P(GROUP, None, None, TENSOR),
        P(GROUP, None, None, TENSOR),
        P(),
        P(),
    )
    return jax.shard_map(
        local, mesh=mesh, in_specs=placed, out_specs=P(GROUP + TENSOR, None), check_vma=False
    )
```

```python
import functools
import math

import jax
import jax.numpy as jnp
from jax import lax
from jax.experimental import pallas as pl
from jax.experimental.pallas import tpu as pltpu
from jax.sharding import Mesh
from jax.sharding import PartitionSpec as P

EPSILON = 1e-06
ROPE_BASE = 1000000.0
GROUP = ("y", "zh", "c")
TENSOR = ("zl", "x")
ROW_TILE = 256
BATCH = 4
UNIT = 16
PACKED = 72 * UNIT
COST = pl.CostEstimate(flops=1 << 20, bytes_accessed=1 << 20, transcendentals=0)


def ring(size, step):
    return [(i, (i + step) % size) for i in range(size)]


def shift(value, axis, step):
    return lax.ppermute(value, axis, ring(lax.axis_size(axis), step))


def spread(block):
    twin = shift(block, "zl", 1)
    below, above = shift(block, "x", 1), shift(block, "x", -1)
    twin_below, twin_above = shift(twin, "x", 1), shift(twin, "x", -1)
    far = shift(below, "x", 1)
    twin_far = shift(twin_above, "x", -1)
    return [block, twin, below, above, twin_below, twin_above, far, twin_far]


def block_ids():
    zl, x = lax.axis_index("zl"), lax.axis_index("x")
    pairs = [(0, 0), (1, 0), (0, 3), (0, 1), (1, 3), (1, 1), (0, 2), (1, 2)]
    return jnp.stack([((zl + dz) % 2) * 4 + (x + dx) % 4 for dz, dx in pairs]).astype(jnp.int32)


def head_norm_rotate(values, gain, cosine, sine):
    scale = lax.rsqrt(jnp.mean(values * values, axis=-1, keepdims=True) + EPSILON)
    scaled = values * scale * gain
    half = values.shape[-1] // 2
    return scaled * cosine + pltpu.roll(scaled, half, 1) * sine


def project_kernel(ids, *refs):
    pieces, rest = refs[:8], refs[8:]
    (gain, wq, wg, wk, wv, q_gain, k_gain, cosine, sine, q_out, g_out, k_out, v_out, scaled) = rest
    rows, width = pieces[0].shape
    head = wk.shape[1]
    edges = [0]
    for w in (wq, wg, wk, wv):
        edges.append(edges[-1] + w.shape[1])

    @pl.when(pl.program_id(0) == 0)
    def _():
        for j in range(8):
            block = pl.multiple_of(ids[j] * width, width)
            here = pl.ds(block, width)
            for w, first, last in zip((wq, wg, wk, wv), edges, edges[1:]):
                part = w[here, :].astype(jnp.float32) * gain[here, :]
                scaled[j * width : (j + 1) * width, first:last] = part.astype(jnp.bfloat16)

    total = jnp.zeros((rows, 128), jnp.float32)
    product = jnp.zeros((rows, edges[-1]), jnp.float32)
    for j, piece in enumerate(pieces):
        value = piece[...]
        product = product + jnp.dot(
            value, scaled[j * width : (j + 1) * width, :], preferred_element_type=jnp.float32
        )
        value = value.astype(jnp.float32)
        square = value * value
        for first in range(0, width, 128):
            total = total + square[:, first : first + 128]
    total = jnp.sum(total, axis=-1, keepdims=True)
    product = product * lax.rsqrt(total / (8 * width) + EPSILON)
    cos, sin = cosine[...], sine[...]
    for h in range(edges[1] // head):
        here = slice(h * head, (h + 1) * head)
        part = head_norm_rotate(product[:, here], q_gain[...], cos, sin)
        q_out[:, here] = part.astype(jnp.bfloat16)
    g_out[...] = jax.nn.sigmoid(product[:, edges[1] : edges[2]])
    k = head_norm_rotate(product[:, edges[2] : edges[3]], k_gain[...], cos, sin)
    k_out[...] = k.astype(jnp.bfloat16)
    v_out[...] = product[:, edges[3] : edges[4]].astype(jnp.bfloat16)


def project(ids, pieces, gain, wq, wg, wk, wv, q_gain, k_gain, cosine, sine):
    rows, width = pieces[0].shape
    depth = gain.shape[0]
    head = q_gain.shape[0]
    tile = lambda columns: pl.BlockSpec((ROW_TILE, columns), lambda i, _: (i, 0))
    whole = lambda a: pl.BlockSpec(a.shape, lambda i, _: (0, 0))
    q_gain, k_gain = q_gain.reshape(1, head), k_gain.reshape(1, head)
    constants = (gain.reshape(depth, 1), wq, wg, wk, wv, q_gain, k_gain)
    columns = sum(w.shape[1] for w in (wq, wg, wk, wv))
    return pl.pallas_call(
        project_kernel,
        out_shape=(
            jax.ShapeDtypeStruct((rows, wq.shape[1]), jnp.bfloat16),
            jax.ShapeDtypeStruct((rows, wg.shape[1]), jnp.float32),
            jax.ShapeDtypeStruct((rows, head), jnp.bfloat16),
            jax.ShapeDtypeStruct((rows, head), jnp.bfloat16),
        ),
        grid_spec=pltpu.PrefetchScalarGridSpec(
            num_scalar_prefetch=1,
            grid=(rows // ROW_TILE,),
            in_specs=[tile(width)] * 8 + [whole(a) for a in constants] + [tile(head)] * 2,
            out_specs=[tile(wq.shape[1]), tile(wg.shape[1]), tile(head), tile(head)],
            scratch_shapes=[pltpu.VMEM((depth, columns), jnp.bfloat16)],
        ),
        cost_estimate=COST,
        name="project",
    )(ids, *pieces, *constants, cosine, sine)


def attend_kernel(starts, lengths, q, g, k, v, *refs):
    key_parts, value_parts = refs[:4], refs[4:8]
    out, keys, values = refs[8:]
    head = k.shape[1]
    span = q.shape[0] // BATCH
    shares = q.shape[1] // head
    size = key_parts[0].shape[0]
    window = keys.shape[0] - 4 * size
    score_scale = 1.0 / math.sqrt(head)
    contract = (((1,), (1,)), ((), ()))

    @pl.when(pl.program_id(0) == 0)
    def _():
        for j in range(4):
            keys[j * size : (j + 1) * size, :] = key_parts[j][...]
            values[j * size : (j + 1) * size, :] = value_parts[j][...]
        keys[4 * size :, :] = jnp.zeros((window, head), keys.dtype)
        values[4 * size :, :] = jnp.zeros((window, head), values.dtype)

    column = lax.broadcasted_iota(jnp.int32, (shares * span, window), 1)
    old_row = lax.broadcasted_iota(jnp.int32, (window, head), 0)
    token = lax.broadcasted_iota(jnp.int32, (shares, span, window), 1)
    token = token.reshape(shares * span, window)
    together = window // span
    for b in range(BATCH):
        r = pl.program_id(0) * BATCH + b
        length = lengths[r]
        rows = slice(b * span, (b + 1) * span)
        first = b // together * together
        both = slice(first * span, (first + together) * span)
        own = column - (b - first) * span
        query = jnp.concatenate([q[rows, s * head : (s + 1) * head] for s in range(shares)], axis=0)
        place = pl.ds(pl.multiple_of(starts[r], UNIT), window)
        old_keys, old_values = keys[place, :], values[place, :]
        old_values = jnp.where(old_row < length, old_values, jnp.zeros_like(old_values))
        old = lax.dot_general(query, old_keys, contract, preferred_element_type=jnp.float32)
        new = lax.dot_general(query, k[both, :], contract, preferred_element_type=jnp.float32)
        old = jnp.where(column < length, old * score_scale, -jnp.inf)
        new = jnp.where((own >= 0) & (own <= token), new * score_scale, -jnp.inf)
        row_max = jnp.max(jnp.maximum(old, new), axis=-1, keepdims=True)
        old, new = jnp.exp(old - row_max), jnp.exp(new - row_max)
        row_total = jnp.sum(old + new, axis=-1, keepdims=True)
        mixed = jnp.dot(old.astype(jnp.bfloat16), old_values, preferred_element_type=jnp.float32)
        mixed += jnp.dot(new.astype(jnp.bfloat16), v[both, :], preferred_element_type=jnp.float32)
        mixed = mixed / row_total
        for s in range(shares):
            columns = slice(s * head, (s + 1) * head)
            part = mixed[s * span : (s + 1) * span] * g[rows, columns]
            out[rows, columns] = part.astype(jnp.bfloat16)


def attend(starts, lengths, q, g, k, v, keys, values, window):
    rows, columns = q.shape
    head = k.shape[1]
    step = rows // lengths.shape[0] * BATCH
    tile = lambda width: pl.BlockSpec((step, width), lambda i, *_: (i, 0))
    whole = lambda a: pl.BlockSpec(a.shape, lambda i, *_: (0, 0))
    store = pltpu.VMEM((4 * keys[0].shape[0] + window, head), keys[0].dtype)
    return pl.pallas_call(
        attend_kernel,
        out_shape=jax.ShapeDtypeStruct((rows, columns), jnp.bfloat16),
        grid_spec=pltpu.PrefetchScalarGridSpec(
            num_scalar_prefetch=2,
            grid=(rows // step,),
            in_specs=[tile(columns)] * 2 + [tile(head)] * 2 + [whole(a) for a in keys + values],
            out_specs=tile(columns),
            scratch_shapes=[store, store],
        ),
        cost_estimate=COST,
        name="attend",
    )(starts, lengths, q, g, k, v, *keys, *values)


def pack_kernel(offsets, cache, *refs):
    outs, store = refs[:4], refs[4]
    sources, _, slots, window, head = cache.shape
    size = outs[0].shape[0]
    for k, out in enumerate(outs):
        for j in range(sources * slots):
            place = pl.multiple_of(offsets[4 + k * sources * slots + j], UNIT)
            store[pl.ds(place, window), :] = cache[j // slots, offsets[k], j % slots]
        out[...] = store[:size, :]


def pack(offsets, cache, size):
    window, head = cache.shape[3:]
    return pl.pallas_call(
        pack_kernel,
        out_shape=[jax.ShapeDtypeStruct((size, head), cache.dtype)] * 4,
        grid_spec=pltpu.PrefetchScalarGridSpec(
            num_scalar_prefetch=1,
            grid=(1,),
            in_specs=[pl.BlockSpec(cache.shape, lambda i, _: (0,) * 5)],
            out_specs=[pl.BlockSpec((size, head), lambda i, _: (0, 0))] * 4,
            scratch_shapes=[pltpu.VMEM((size + window, head), cache.dtype)],
        ),
        cost_estimate=COST,
        name="pack",
    )(offsets, cache)


def by_target_kernel(source, target):
    for c in range(2):
        target[0, c] = source[0, :, c]


def by_target(cache):
    ny, nz, nc, capacity, window, head = cache.shape
    return pl.pallas_call(
        by_target_kernel,
        out_shape=jax.ShapeDtypeStruct((ny, nc, nz, capacity, window, head), cache.dtype),
        grid=(ny,),
        in_specs=[pl.BlockSpec((1, nz, nc, capacity, window, head), lambda i: (i, 0, 0, 0, 0, 0))],
        out_specs=pl.BlockSpec((1, nc, nz, capacity, window, head), lambda i: (i, 0, 0, 0, 0, 0)),
        cost_estimate=COST,
        name="by_target",
    )(cache)


def copies_kernel(half, twin, out):
    out[0, 0], out[0, 1] = half[...], twin[...]


def copies(half, twin):
    depth, columns = half.shape
    whole = pl.BlockSpec((depth, columns), lambda i: (0, 0))
    return pl.pallas_call(
        copies_kernel,
        out_shape=jax.ShapeDtypeStruct((4, 2, depth, columns), half.dtype),
        grid=(4,),
        in_specs=[whole, whole],
        out_specs=pl.BlockSpec((1, 2, depth, columns), lambda i: (i, 0, 0, 0)),
        cost_estimate=COST,
        name="copies",
    )(half, twin)


def output_kernel(places, heads, mine, other, out, joined):
    count, depth = mine.shape[:2]

    @pl.when(pl.program_id(0) == 0)
    def _():
        for j in range(count):
            for h in range(2):
                first = pl.multiple_of((places[count] + h) % 2 * depth, depth)
                columns = slice((2 * j + h) * depth, (2 * j + h + 1) * depth)
                joined[:, columns] = heads[places[j], :, pl.ds(first, depth)]

    total = jnp.zeros(out.shape, jnp.float32)
    for j in range(count):
        weight = jnp.concatenate([mine[j], other[j]], axis=0)
        part = joined[:, 2 * j * depth : 2 * (j + 1) * depth]
        total = total + jnp.dot(part, weight, preferred_element_type=jnp.float32)
    out[...] = total.astype(jnp.bfloat16)


def project_out(places, heads, mine, other):
    blocks, rows, width = heads.shape
    depth, columns = mine.shape[1:]
    tile = 512
    half = pl.BlockSpec((blocks, depth, tile), lambda i, _: (0, 0, i))
    return pl.pallas_call(
        output_kernel,
        out_shape=jax.ShapeDtypeStruct((rows, columns), jnp.bfloat16),
        grid_spec=pltpu.PrefetchScalarGridSpec(
            num_scalar_prefetch=1,
            grid=(columns // tile,),
            in_specs=[pl.BlockSpec(heads.shape, lambda i, _: (0, 0, 0)), half, half],
            out_specs=pl.BlockSpec((rows, tile), lambda i, _: (0, i)),
            scratch_shapes=[pltpu.VMEM((rows, blocks * width), jnp.bfloat16)],
        ),
        cost_estimate=COST,
        name="project_out",
    )(places, heads, mine, other)


def across_y(slots):
    ny, nc, nz, capacity, window, head = slots.shape
    flat = slots.reshape(ny * nc, nz * capacity * window, head)
    flat = lax.all_to_all(flat, ("y", "c"), 0, 0, tiled=True)
    return flat.reshape(ny * nc, nz, capacity, window, head)


def across_z(parts):
    return [parts[0]] + [shift(parts[k], "zh", k) for k in range(1, 4)]


def local(
    span_rows,
    norm_gain,
    q_weight,
    gate_weight,
    k_weight,
    v_weight,
    q_norm_gain,
    k_norm_gain,
    o_weight,
    key_cache,
    value_cache,
    holders,
    prefix_lengths,
):
    groups = lax.axis_size(GROUP)
    group_id = lax.axis_index(GROUP)
    requests = prefix_lengths.shape[0] // groups
    rows = span_rows.shape[0]
    span_len = rows // requests
    head_dim = q_norm_gain.shape[0]
    capacity = key_cache.shape[1] // groups
    window = key_cache.shape[2]
    blocks = lax.axis_size(TENSOR)

    y, zh, core = lax.axis_index("y"), lax.axis_index("zh"), lax.axis_index("c")
    all_holders = holders.reshape(groups, requests)
    all_lengths = prefix_lengths.reshape(groups, requests)
    order = jnp.arange(requests)
    earlier = order[None, :] < order[:, None]
    same = all_holders[:, :, None] == all_holders[:, None, :]
    all_ranks = jnp.sum(same & earlier[None], axis=2)
    all_units = (all_lengths + UNIT - 1) // UNIT
    plane = all_holders // 2 % 4
    per_plane = jnp.sum(
        jnp.where(plane[:, :, None] == jnp.arange(4), all_units[:, :, None], 0), axis=1
    )
    fits = jnp.max(per_plane) * UNIT <= PACKED

    slot_y = jnp.arange(4)[:, None, None]
    slot_c = jnp.arange(2)[None, :, None]
    slot_rank = jnp.arange(capacity)[None, None, :]
    z_ids = (zh + jnp.arange(4)) % 4
    served = (y * 4 + z_ids) * 2 + core
    slot_holder = (slot_y * 4 + zh) * 2 + slot_c
    slot_key = (slot_holder * capacity + slot_rank).reshape(-1)
    served_key = (all_holders * capacity + all_ranks)[served]
    hit = served_key[:, :, None] == slot_key[None, None, :]
    slot_units = jnp.sum(jnp.where(hit, all_units[served][:, :, None], 0), axis=1)
    offsets = (jnp.cumsum(slot_units, axis=1) - slot_units) * UNIT

    mine = lambda a: lax.dynamic_index_in_dim(a, group_id, 0, keepdims=False)
    my_holders, my_ranks, my_lengths, my_units = map(
        mine, (all_holders, all_ranks, all_lengths, all_units)
    )
    from_z = (zh - my_holders // 2 % 4) % 4
    my_order = (my_holders // 8 * 2 + my_holders % 2) * capacity + my_ranks
    ahead = (from_z[:, None] == from_z[None, :]) & (my_order[None, :] < my_order[:, None])
    my_start = jnp.sum(jnp.where(ahead, my_units[None, :], 0), axis=1) * UNIT

    def packing(size):
        limit = jnp.minimum(offsets, size).reshape(-1)
        places = jnp.concatenate([z_ids, limit]).astype(jnp.int32)
        starts = jnp.minimum(from_z * size + my_start, 4 * size)
        return places, starts.astype(jnp.int32)

    positions = my_lengths[:, None] + jnp.arange(span_len, dtype=jnp.int32)[None, :]
    channel = jnp.arange(head_dim)
    half = head_dim // 2
    frequency = ROPE_BASE ** (-(channel % half).astype(jnp.float32) * 2.0 / head_dim)
    angles = positions.reshape(-1).astype(jnp.float32)[:, None] * frequency
    cosine = jnp.cos(angles)
    sine = jnp.sin(angles) * jnp.where(channel < half, -1.0, 1.0)

    ids = block_ids()
    sides = (4, 4, 2, capacity, window, head_dim)
    places, starts = packing(PACKED)
    pieces = spread(span_rows)
    depth = o_weight.shape[0] // 2
    half = lax.dynamic_slice_in_dim(o_weight, core * depth, depth, 0)
    half, pieces[1] = lax.optimization_barrier((half, pieces[1]))
    twin_half = shift(half, "zl", 1)

    key_part = across_y(by_target(key_cache.reshape(sides)))
    value_slots, key_part, pieces[1:6], twin_half = lax.optimization_barrier(
        (by_target(value_cache.reshape(sides)), key_part, pieces[1:6], twin_half)
    )
    value_part = across_y(value_slots)
    keys = across_z(pack(places, key_part, PACKED))
    q, g, k, v = project(
        ids, pieces, norm_gain, q_weight, gate_weight, k_weight, v_weight,
        q_norm_gain, k_norm_gain, cosine, sine,
    )
    repeated, value_part, q = lax.optimization_barrier(
        (copies(half, twin_half), value_part, q)
    )
    packed_values = pack(places, value_part, PACKED)
    repeated, packed_values, keys[1], keys[3] = lax.optimization_barrier(
        (repeated, packed_values, keys[1], keys[3])
    )
    values = across_z(packed_values)
    halves = lax.all_to_all(repeated, "x", 0, 0, tiled=True)
    halves = halves.reshape((blocks,) + half.shape)
    other_halves = shift(halves, "c", 1)

    def packed(keys, values, key_part, value_part, q, g, k, v):
        return attend(starts, my_lengths, q, g, k, v, keys, values, window)

    def full(keys, values, key_part, value_part, q, g, k, v):
        size = 8 * capacity * window
        places, starts = packing(size)
        keys, values = (across_z(pack(places, a, size)) for a in (key_part, value_part))
        return attend(starts, my_lengths, q, g, k, v, keys, values, window)

    attended = lax.cond(fits, packed, full, keys, values, key_part, value_part, q, g, k, v)
    heads = lax.all_to_all(
        attended.reshape(blocks, rows // blocks, attended.shape[1]), TENSOR, 0, 0, tiled=True
    )
    x_ids, zl_ids = jnp.arange(blocks) // 2, (lax.axis_index("zl") + jnp.arange(blocks)) % 2
    out_places = jnp.concatenate([zl_ids * 4 + x_ids, core[None]]).astype(jnp.int32)
    return project_out(out_places, heads, halves, other_halves)


def solution(mesh):
    mesh = Mesh(mesh.devices.reshape(4, 4, 2, 2, 4), GROUP + TENSOR)
    placed = (
        P(GROUP, TENSOR),
        P(),
        P(None, TENSOR),
        P(None, TENSOR),
        P(None, TENSOR),
        P(None, TENSOR),
        P(),
        P(),
        P(TENSOR, None),
        P(GROUP, None, None, TENSOR),
        P(GROUP, None, None, TENSOR),
        P(),
        P(),
    )
    return jax.shard_map(
        local, mesh=mesh, in_specs=placed, out_specs=P(GROUP + TENSOR, None), check_vma=False
    )
```

```python
import functools
import math

import jax
import jax.numpy as jnp
from jax import lax
from jax.experimental import pallas as pl
from jax.experimental.pallas import tpu as pltpu
from jax.sharding import Mesh
from jax.sharding import PartitionSpec as P

EPSILON = 1e-06
ROPE_BASE = 1000000.0
GROUP = ("y", "zh", "c")
TENSOR = ("zl", "x")
ROW_TILE = 256
BATCH = 4
UNIT = 16
PACKED = 68 * UNIT
LONG = pl.CostEstimate(flops=1 << 20, bytes_accessed=64 << 20, transcendentals=0)
COST = pl.CostEstimate(flops=1 << 20, bytes_accessed=1 << 20, transcendentals=0)


def ring(size, step):
    return [(i, (i + step) % size) for i in range(size)]


def shift(value, axis, step):
    return lax.ppermute(value, axis, ring(lax.axis_size(axis), step))


def spread(block):
    twin = shift(block, "zl", 1)
    below, above = shift(block, "x", 1), shift(block, "x", -1)
    twin_below, twin_above = shift(twin, "x", 1), shift(twin, "x", -1)
    far = shift(below, "x", 1)
    twin_far = shift(twin_above, "x", -1)
    return [block, twin, below, above, twin_below, twin_above, far, twin_far]


def block_ids():
    zl, x = lax.axis_index("zl"), lax.axis_index("x")
    pairs = [(0, 0), (1, 0), (0, 3), (0, 1), (1, 3), (1, 1), (0, 2), (1, 2)]
    return jnp.stack([((zl + dz) % 2) * 4 + (x + dx) % 4 for dz, dx in pairs]).astype(jnp.int32)


def head_norm_rotate(values, gain, cosine, sine):
    scale = lax.rsqrt(jnp.mean(values * values, axis=-1, keepdims=True) + EPSILON)
    scaled = values * scale * gain
    half = values.shape[-1] // 2
    return scaled * cosine + pltpu.roll(scaled, half, 1) * sine


def project_kernel(ids, *refs):
    pieces, rest = refs[:8], refs[8:]
    (gain, wq, wg, wk, wv, q_gain, k_gain, cosine, sine, q_out, g_out, k_out, v_out, scaled) = rest
    rows, width = pieces[0].shape
    head = wk.shape[1]
    edges = [0]
    for w in (wq, wg, wk, wv):
        edges.append(edges[-1] + w.shape[1])

    @pl.when(pl.program_id(0) == 0)
    def _():
        for j in range(8):
            block = pl.multiple_of(ids[j] * width, width)
            here = pl.ds(block, width)
            for w, first, last in zip((wq, wg, wk, wv), edges, edges[1:]):
                part = w[here, :].astype(jnp.float32) * gain[here, :]
                scaled[j * width : (j + 1) * width, first:last] = part.astype(jnp.bfloat16)

    total = jnp.zeros((rows, 128), jnp.float32)
    product = jnp.zeros((rows, edges[-1]), jnp.float32)
    for j, piece in enumerate(pieces):
        value = piece[...]
        product = product + jnp.dot(
            value, scaled[j * width : (j + 1) * width, :], preferred_element_type=jnp.float32
        )
        value = value.astype(jnp.float32)
        square = value * value
        for first in range(0, width, 128):
            total = total + square[:, first : first + 128]
    total = jnp.sum(total, axis=-1, keepdims=True)
    product = product * lax.rsqrt(total / (8 * width) + EPSILON)
    cos, sin = cosine[...], sine[...]
    for h in range(edges[1] // head):
        here = slice(h * head, (h + 1) * head)
        part = head_norm_rotate(product[:, here], q_gain[...], cos, sin)
        q_out[:, here] = part.astype(jnp.bfloat16)
    g_out[...] = jax.nn.sigmoid(product[:, edges[1] : edges[2]])
    k = head_norm_rotate(product[:, edges[2] : edges[3]], k_gain[...], cos, sin)
    k_out[...] = k.astype(jnp.bfloat16)
    v_out[...] = product[:, edges[3] : edges[4]].astype(jnp.bfloat16)


def project(ids, pieces, gain, wq, wg, wk, wv, q_gain, k_gain, cosine, sine):
    rows, width = pieces[0].shape
    depth = gain.shape[0]
    head = q_gain.shape[0]
    tile = lambda columns: pl.BlockSpec((ROW_TILE, columns), lambda i, _: (i, 0))
    whole = lambda a: pl.BlockSpec(a.shape, lambda i, _: (0, 0))
    q_gain, k_gain = q_gain.reshape(1, head), k_gain.reshape(1, head)
    constants = (gain.reshape(depth, 1), wq, wg, wk, wv, q_gain, k_gain)
    columns = sum(w.shape[1] for w in (wq, wg, wk, wv))
    return pl.pallas_call(
        project_kernel,
        out_shape=(
            jax.ShapeDtypeStruct((rows, wq.shape[1]), jnp.bfloat16),
            jax.ShapeDtypeStruct((rows, wg.shape[1]), jnp.float32),
            jax.ShapeDtypeStruct((rows, head), jnp.bfloat16),
            jax.ShapeDtypeStruct((rows, head), jnp.bfloat16),
        ),
        grid_spec=pltpu.PrefetchScalarGridSpec(
            num_scalar_prefetch=1,
            grid=(rows // ROW_TILE,),
            in_specs=[tile(width)] * 8 + [whole(a) for a in constants] + [tile(head)] * 2,
            out_specs=[tile(wq.shape[1]), tile(wg.shape[1]), tile(head), tile(head)],
            scratch_shapes=[pltpu.VMEM((depth, columns), jnp.bfloat16)],
        ),
        cost_estimate=COST,
        name="project",
    )(ids, *pieces, *constants, cosine, sine)


def attend_kernel(starts, lengths, q, g, k, v, *refs):
    key_parts, value_parts = refs[:4], refs[4:8]
    out, keys, values = refs[8:]
    head = k.shape[1]
    span = q.shape[0] // BATCH
    shares = q.shape[1] // head
    size = key_parts[0].shape[0]
    window = keys.shape[0] - 4 * size
    score_scale = 1.0 / math.sqrt(head)
    contract = (((1,), (1,)), ((), ()))

    @pl.when(pl.program_id(0) == 0)
    def _():
        for j in range(4):
            keys[j * size : (j + 1) * size, :] = key_parts[j][...]
            values[j * size : (j + 1) * size, :] = value_parts[j][...]
        keys[4 * size :, :] = jnp.zeros((window, head), keys.dtype)
        values[4 * size :, :] = jnp.zeros((window, head), values.dtype)

    column = lax.broadcasted_iota(jnp.int32, (shares * span, window), 1)
    old_row = lax.broadcasted_iota(jnp.int32, (window, head), 0)
    token = lax.broadcasted_iota(jnp.int32, (shares, span, window), 1)
    token = token.reshape(shares * span, window)
    together = window // span
    for b in range(BATCH):
        r = pl.program_id(0) * BATCH + b
        length = lengths[r]
        rows = slice(b * span, (b + 1) * span)
        first = b // together * together
        both = slice(first * span, (first + together) * span)
        own = column - (b - first) * span
        query = jnp.concatenate([q[rows, s * head : (s + 1) * head] for s in range(shares)], axis=0)
        place = pl.ds(pl.multiple_of(starts[r], UNIT), window)
        old_keys, old_values = keys[place, :], values[place, :]
        old_values = jnp.where(old_row < length, old_values, jnp.zeros_like(old_values))
        old = lax.dot_general(query, old_keys, contract, preferred_element_type=jnp.float32)
        new = lax.dot_general(query, k[both, :], contract, preferred_element_type=jnp.float32)
        old = jnp.where(column < length, old * score_scale, -jnp.inf)
        new = jnp.where((own >= 0) & (own <= token), new * score_scale, -jnp.inf)
        row_max = jnp.max(jnp.maximum(old, new), axis=-1, keepdims=True)
        old, new = jnp.exp(old - row_max), jnp.exp(new - row_max)
        row_total = jnp.sum(old + new, axis=-1, keepdims=True)
        mixed = jnp.dot(old.astype(jnp.bfloat16), old_values, preferred_element_type=jnp.float32)
        mixed += jnp.dot(new.astype(jnp.bfloat16), v[both, :], preferred_element_type=jnp.float32)
        mixed = mixed / row_total
        for s in range(shares):
            columns = slice(s * head, (s + 1) * head)
            part = mixed[s * span : (s + 1) * span] * g[rows, columns]
            out[rows, columns] = part.astype(jnp.bfloat16)


def attend(starts, lengths, q, g, k, v, keys, values, window):
    rows, columns = q.shape
    head = k.shape[1]
    step = rows // lengths.shape[0] * BATCH
    tile = lambda width: pl.BlockSpec((step, width), lambda i, *_: (i, 0))
    whole = lambda a: pl.BlockSpec(a.shape, lambda i, *_: (0, 0))
    store = pltpu.VMEM((4 * keys[0].shape[0] + window, head), keys[0].dtype)
    return pl.pallas_call(
        attend_kernel,
        out_shape=jax.ShapeDtypeStruct((rows, columns), jnp.bfloat16),
        grid_spec=pltpu.PrefetchScalarGridSpec(
            num_scalar_prefetch=2,
            grid=(rows // step,),
            in_specs=[tile(columns)] * 2 + [tile(head)] * 2 + [whole(a) for a in keys + values],
            out_specs=tile(columns),
            scratch_shapes=[store, store],
        ),
        compiler_params=pltpu.CompilerParams(vmem_limit_bytes=30 << 20),
        cost_estimate=COST,
        name="attend",
    )(starts, lengths, q, g, k, v, *keys, *values)


def pack_kernel(offsets, cache, *refs):
    outs, store = refs[:4], refs[4]
    sources, _, slots, window, head = cache.shape
    size = outs[0].shape[0]
    for k, out in enumerate(outs):
        for j in range(sources * slots):
            place = pl.multiple_of(offsets[4 + k * sources * slots + j], UNIT)
            store[pl.ds(place, window), :] = cache[j // slots, offsets[k], j % slots]
        out[...] = store[:size, :]


def pack(offsets, cache, size):
    window, head = cache.shape[3:]
    return pl.pallas_call(
        pack_kernel,
        out_shape=[jax.ShapeDtypeStruct((size, head), cache.dtype)] * 4,
        grid_spec=pltpu.PrefetchScalarGridSpec(
            num_scalar_prefetch=1,
            grid=(1,),
            in_specs=[pl.BlockSpec(cache.shape, lambda i, _: (0,) * 5)],
            out_specs=[pl.BlockSpec((size, head), lambda i, _: (0, 0))] * 4,
            scratch_shapes=[pltpu.VMEM((size + window, head), cache.dtype)],
        ),
        compiler_params=pltpu.CompilerParams(vmem_limit_bytes=16 << 20),
        cost_estimate=COST,
        name="pack",
    )(offsets, cache)


def by_target_kernel(source, target):
    for c in range(2):
        target[0, c] = source[0, :, c]


def by_target(cache):
    ny, nz, nc, capacity, window, head = cache.shape
    return pl.pallas_call(
        by_target_kernel,
        out_shape=jax.ShapeDtypeStruct((ny, nc, nz, capacity, window, head), cache.dtype),
        grid=(ny,),
        in_specs=[pl.BlockSpec((1, nz, nc, capacity, window, head), lambda i: (i, 0, 0, 0, 0, 0))],
        out_specs=pl.BlockSpec((1, nc, nz, capacity, window, head), lambda i: (i, 0, 0, 0, 0, 0)),
        compiler_params=pltpu.CompilerParams(vmem_limit_bytes=12 << 20),
        cost_estimate=LONG,
        name="by_target",
    )(cache)


def copies_kernel(half, twin, out):
    out[0, 0], out[0, 1] = half[...], twin[...]


def copies(half, twin):
    depth, columns = half.shape
    whole = pl.BlockSpec((depth, columns), lambda i: (0, 0))
    return pl.pallas_call(
        copies_kernel,
        out_shape=jax.ShapeDtypeStruct((4, 2, depth, columns), half.dtype),
        grid=(4,),
        in_specs=[whole, whole],
        out_specs=pl.BlockSpec((1, 2, depth, columns), lambda i: (i, 0, 0, 0)),
        compiler_params=pltpu.CompilerParams(vmem_limit_bytes=12 << 20),
        cost_estimate=COST,
        name="copies",
    )(half, twin)


def output_kernel(places, heads, mine, other, out, joined):
    count, depth = mine.shape[:2]

    @pl.when(pl.program_id(0) == 0)
    def _():
        for j in range(count):
            for h in range(2):
                first = pl.multiple_of((places[count] + h) % 2 * depth, depth)
                columns = slice((2 * j + h) * depth, (2 * j + h + 1) * depth)
                joined[:, columns] = heads[places[j], :, pl.ds(first, depth)]

    total = jnp.zeros(out.shape, jnp.float32)
    for j in range(count):
        weight = jnp.concatenate([mine[j], other[j]], axis=0)
        part = joined[:, 2 * j * depth : 2 * (j + 1) * depth]
        total = total + jnp.dot(part, weight, preferred_element_type=jnp.float32)
    out[...] = total.astype(jnp.bfloat16)


def project_out(places, heads, mine, other):
    blocks, rows, width = heads.shape
    depth, columns = mine.shape[1:]
    tile = 512
    half = pl.BlockSpec((blocks, depth, tile), lambda i, _: (0, 0, i))
    return pl.pallas_call(
        output_kernel,
        out_shape=jax.ShapeDtypeStruct((rows, columns), jnp.bfloat16),
        grid_spec=pltpu.PrefetchScalarGridSpec(
            num_scalar_prefetch=1,
            grid=(columns // tile,),
            in_specs=[pl.BlockSpec(heads.shape, lambda i, _: (0, 0, 0)), half, half],
            out_specs=pl.BlockSpec((rows, tile), lambda i, _: (0, i)),
            scratch_shapes=[pltpu.VMEM((rows, blocks * width), jnp.bfloat16)],
        ),
        compiler_params=pltpu.CompilerParams(vmem_limit_bytes=30 << 20),
        cost_estimate=COST,
        name="project_out",
    )(places, heads, mine, other)


def across_y(slots):
    ny, nc, nz, capacity, window, head = slots.shape
    flat = slots.reshape(ny * nc, nz * capacity * window, head)
    flat = lax.all_to_all(flat, ("y", "c"), 0, 0, tiled=True)
    return flat.reshape(ny * nc, nz, capacity, window, head)


def across_z(parts):
    return [parts[0]] + [shift(parts[k], "zh", k) for k in range(1, 4)]


def local(
    span_rows,
    norm_gain,
    q_weight,
    gate_weight,
    k_weight,
    v_weight,
    q_norm_gain,
    k_norm_gain,
    o_weight,
    key_cache,
    value_cache,
    holders,
    prefix_lengths,
):
    groups = lax.axis_size(GROUP)
    group_id = lax.axis_index(GROUP)
    requests = prefix_lengths.shape[0] // groups
    rows = span_rows.shape[0]
    span_len = rows // requests
    head_dim = q_norm_gain.shape[0]
    capacity = key_cache.shape[1] // groups
    window = key_cache.shape[2]
    blocks = lax.axis_size(TENSOR)

    y, zh, core = lax.axis_index("y"), lax.axis_index("zh"), lax.axis_index("c")
    all_holders = holders.reshape(groups, requests)
    all_lengths = prefix_lengths.reshape(groups, requests)
    order = jnp.arange(requests)
    earlier = order[None, :] < order[:, None]
    same = all_holders[:, :, None] == all_holders[:, None, :]
    all_ranks = jnp.sum(same & earlier[None], axis=2)
    all_units = (all_lengths + UNIT - 1) // UNIT
    plane = all_holders // 2 % 4
    per_plane = jnp.sum(
        jnp.where(plane[:, :, None] == jnp.arange(4), all_units[:, :, None], 0), axis=1
    )
    fits = jnp.max(per_plane) * UNIT <= PACKED

    slot_y = jnp.arange(4)[:, None, None]
    slot_c = jnp.arange(2)[None, :, None]
    slot_rank = jnp.arange(capacity)[None, None, :]
    z_ids = (zh + jnp.arange(4)) % 4
    served = (y * 4 + z_ids) * 2 + core
    slot_holder = (slot_y * 4 + zh) * 2 + slot_c
    slot_key = (slot_holder * capacity + slot_rank).reshape(-1)
    served_key = (all_holders * capacity + all_ranks)[served]
    hit = served_key[:, :, None] == slot_key[None, None, :]
    slot_units = jnp.sum(jnp.where(hit, all_units[served][:, :, None], 0), axis=1)
    offsets = (jnp.cumsum(slot_units, axis=1) - slot_units) * UNIT

    mine = lambda a: lax.dynamic_index_in_dim(a, group_id, 0, keepdims=False)
    my_holders, my_ranks, my_lengths, my_units = map(
        mine, (all_holders, all_ranks, all_lengths, all_units)
    )
    from_z = (zh - my_holders // 2 % 4) % 4
    my_order = (my_holders // 8 * 2 + my_holders % 2) * capacity + my_ranks
    ahead = (from_z[:, None] == from_z[None, :]) & (my_order[None, :] < my_order[:, None])
    my_start = jnp.sum(jnp.where(ahead, my_units[None, :], 0), axis=1) * UNIT

    def packing(size):
        limit = jnp.minimum(offsets, size).reshape(-1)
        places = jnp.concatenate([z_ids, limit]).astype(jnp.int32)
        starts = jnp.minimum(from_z * size + my_start, 4 * size)
        return places, starts.astype(jnp.int32)

    positions = my_lengths[:, None] + jnp.arange(span_len, dtype=jnp.int32)[None, :]
    channel = jnp.arange(head_dim)
    half = head_dim // 2
    frequency = ROPE_BASE ** (-(channel % half).astype(jnp.float32) * 2.0 / head_dim)
    angles = positions.reshape(-1).astype(jnp.float32)[:, None] * frequency
    cosine = jnp.cos(angles)
    sine = jnp.sin(angles) * jnp.where(channel < half, -1.0, 1.0)

    ids = block_ids()
    sides = (4, 4, 2, capacity, window, head_dim)
    places, starts = packing(PACKED)
    pieces = spread(span_rows)
    depth = o_weight.shape[0] // 2
    half = lax.dynamic_slice_in_dim(o_weight, core * depth, depth, 0)
    half, pieces[1] = lax.optimization_barrier((half, pieces[1]))
    twin_half = shift(half, "zl", 1)

    key_part = across_y(by_target(key_cache.reshape(sides)))
    value_slots, key_part, pieces[1:6], twin_half, places, starts, fits = lax.optimization_barrier(
        (by_target(value_cache.reshape(sides)), key_part, pieces[1:6], twin_half, places, starts, fits)
    )
    value_part = across_y(value_slots)
    keys = across_z(pack(places, key_part, PACKED))
    q, g, k, v = project(
        ids, pieces, norm_gain, q_weight, gate_weight, k_weight, v_weight,
        q_norm_gain, k_norm_gain, cosine, sine,
    )
    repeated, value_part, q = lax.optimization_barrier(
        (copies(half, twin_half), value_part, q)
    )
    packed_values = pack(places, value_part, PACKED)
    repeated, packed_values, keys = lax.optimization_barrier((repeated, packed_values, keys))
    values = across_z(packed_values)
    halves = lax.all_to_all(repeated, "x", 0, 0, tiled=True)
    halves = halves.reshape((blocks,) + half.shape)
    other_halves = shift(halves, "c", 1)

    def packed(keys, values, key_part, value_part, q, g, k, v):
        return attend(starts, my_lengths, q, g, k, v, keys, values, window)

    def full(keys, values, key_part, value_part, q, g, k, v):
        size = 8 * capacity * window
        places, starts = packing(size)
        keys, values = (across_z(pack(places, a, size)) for a in (key_part, value_part))
        return attend(starts, my_lengths, q, g, k, v, keys, values, window)

    attended = lax.cond(fits, packed, full, keys, values, key_part, value_part, q, g, k, v)
    heads = lax.all_to_all(
        attended.reshape(blocks, rows // blocks, attended.shape[1]), TENSOR, 0, 0, tiled=True
    )
    x_ids, zl_ids = jnp.arange(blocks) // 2, (lax.axis_index("zl") + jnp.arange(blocks)) % 2
    out_places = jnp.concatenate([zl_ids * 4 + x_ids, core[None]]).astype(jnp.int32)
    return project_out(out_places, heads, halves, other_halves)


def solution(mesh):
    mesh = Mesh(mesh.devices.reshape(4, 4, 2, 2, 4), GROUP + TENSOR)
    placed = (
        P(GROUP, TENSOR),
        P(),
        P(None, TENSOR),
        P(None, TENSOR),
        P(None, TENSOR),
        P(None, TENSOR),
        P(),
        P(),
        P(TENSOR, None),
        P(GROUP, None, None, TENSOR),
        P(GROUP, None, None, TENSOR),
        P(),
        P(),
    )
    return jax.shard_map(
        local, mesh=mesh, in_specs=placed, out_specs=P(GROUP + TENSOR, None), check_vma=False
    )
```

```python
import functools
import math

import jax
import jax.numpy as jnp
from jax import lax
from jax.experimental import pallas as pl
from jax.experimental.pallas import tpu as pltpu
from jax.sharding import Mesh
from jax.sharding import PartitionSpec as P

EPSILON = 1e-06
ROPE_BASE = 1000000.0
GROUP = ("y", "zh", "c")
TENSOR = ("zl", "x")
ROW_TILE = 256
BATCH = 4
UNIT = 16
PACKED = 68 * UNIT
LONG = pl.CostEstimate(flops=1 << 20, bytes_accessed=64 << 20, transcendentals=0)
COST = pl.CostEstimate(flops=1 << 20, bytes_accessed=1 << 20, transcendentals=0)


def ring(size, step):
    return [(i, (i + step) % size) for i in range(size)]


def shift(value, axis, step):
    return lax.ppermute(value, axis, ring(lax.axis_size(axis), step))


def spread(block):
    twin = shift(block, "zl", 1)
    below, above = shift(block, "x", 1), shift(block, "x", -1)
    twin_below, twin_above = shift(twin, "x", 1), shift(twin, "x", -1)
    far = shift(below, "x", 1)
    twin_far = shift(twin_above, "x", -1)
    return [block, twin, below, above, twin_below, twin_above, far, twin_far]


def block_ids():
    zl, x = lax.axis_index("zl"), lax.axis_index("x")
    pairs = [(0, 0), (1, 0), (0, 3), (0, 1), (1, 3), (1, 1), (0, 2), (1, 2)]
    return jnp.stack([((zl + dz) % 2) * 4 + (x + dx) % 4 for dz, dx in pairs]).astype(jnp.int32)


def head_norm_rotate(values, gain, cosine, sine):
    scale = lax.rsqrt(jnp.mean(values * values, axis=-1, keepdims=True) + EPSILON)
    scaled = values * scale * gain
    half = values.shape[-1] // 2
    return scaled * cosine + pltpu.roll(scaled, half, 1) * sine


def project_kernel(ids, *refs):
    pieces, rest = refs[:8], refs[8:]
    (gain, wq, wg, wk, wv, q_gain, k_gain, cosine, sine, q_out, g_out, k_out, v_out, scaled) = rest
    rows, width = pieces[0].shape
    head = wk.shape[1]
    edges = [0]
    for w in (wq, wg, wk, wv):
        edges.append(edges[-1] + w.shape[1])

    @pl.when(pl.program_id(0) == 0)
    def _():
        for j in range(8):
            block = pl.multiple_of(ids[j] * width, width)
            here = pl.ds(block, width)
            for w, first, last in zip((wq, wg, wk, wv), edges, edges[1:]):
                part = w[here, :].astype(jnp.float32) * gain[here, :]
                scaled[j * width : (j + 1) * width, first:last] = part.astype(jnp.bfloat16)

    total = jnp.zeros((rows, 128), jnp.float32)
    product = jnp.zeros((rows, edges[-1]), jnp.float32)
    for j, piece in enumerate(pieces):
        value = piece[...]
        product = product + jnp.dot(
            value, scaled[j * width : (j + 1) * width, :], preferred_element_type=jnp.float32
        )
        value = value.astype(jnp.float32)
        square = value * value
        for first in range(0, width, 128):
            total = total + square[:, first : first + 128]
    total = jnp.sum(total, axis=-1, keepdims=True)
    product = product * lax.rsqrt(total / (8 * width) + EPSILON)
    cos, sin = cosine[...], sine[...]
    for h in range(edges[1] // head):
        here = slice(h * head, (h + 1) * head)
        part = head_norm_rotate(product[:, here], q_gain[...], cos, sin)
        q_out[:, here] = part.astype(jnp.bfloat16)
    g_out[...] = jax.nn.sigmoid(product[:, edges[1] : edges[2]])
    k = head_norm_rotate(product[:, edges[2] : edges[3]], k_gain[...], cos, sin)
    k_out[...] = k.astype(jnp.bfloat16)
    v_out[...] = product[:, edges[3] : edges[4]].astype(jnp.bfloat16)


def project(ids, pieces, gain, wq, wg, wk, wv, q_gain, k_gain, cosine, sine):
    rows, width = pieces[0].shape
    depth = gain.shape[0]
    head = q_gain.shape[0]
    tile = lambda columns: pl.BlockSpec((ROW_TILE, columns), lambda i, _: (i, 0))
    whole = lambda a: pl.BlockSpec(a.shape, lambda i, _: (0, 0))
    q_gain, k_gain = q_gain.reshape(1, head), k_gain.reshape(1, head)
    constants = (gain, wq, wg, wk, wv, q_gain, k_gain)
    columns = sum(w.shape[1] for w in (wq, wg, wk, wv))
    return pl.pallas_call(
        project_kernel,
        out_shape=(
            jax.ShapeDtypeStruct((rows, wq.shape[1]), jnp.bfloat16),
            jax.ShapeDtypeStruct((rows, wg.shape[1]), jnp.float32),
            jax.ShapeDtypeStruct((rows, head), jnp.bfloat16),
            jax.ShapeDtypeStruct((rows, head), jnp.bfloat16),
        ),
        grid_spec=pltpu.PrefetchScalarGridSpec(
            num_scalar_prefetch=1,
            grid=(rows // ROW_TILE,),
            in_specs=[tile(width)] * 8 + [whole(a) for a in constants] + [tile(head)] * 2,
            out_specs=[tile(wq.shape[1]), tile(wg.shape[1]), tile(head), tile(head)],
            scratch_shapes=[pltpu.VMEM((depth, columns), jnp.bfloat16)],
        ),
        cost_estimate=COST,
        name="project",
    )(ids, *pieces, *constants, cosine, sine)


def gather_parts(parts, store):
    size = parts[0].shape[0]
    for j, part in enumerate(parts):
        store[j * size : (j + 1) * size, :] = part[...]
    slack = slice(len(parts) * size, store.shape[0])
    store[slack, :] = jnp.zeros((store.shape[0] - len(parts) * size, store.shape[1]), store.dtype)


def weigh_kernel(starts, lengths, q, g, k, v, *refs):
    parts, (weights, mixed_new, factor, keys) = refs[:4], refs[4:]
    head = k.shape[1]
    span = q.shape[0] // BATCH
    shares = q.shape[1] // head
    window = keys.shape[0] - 4 * parts[0].shape[0]
    score_scale = 1.0 / math.sqrt(head)
    contract = (((1,), (1,)), ((), ()))

    @pl.when(pl.program_id(0) == 0)
    def _():
        gather_parts(parts, keys)

    column = lax.broadcasted_iota(jnp.int32, (shares * span, window), 1)
    token = lax.broadcasted_iota(jnp.int32, (shares, span, window), 1)
    token = token.reshape(shares * span, window)
    together = window // span
    for b in range(BATCH):
        r = pl.program_id(0) * BATCH + b
        length = lengths[r]
        rows = slice(b * span, (b + 1) * span)
        first = b // together * together
        both = slice(first * span, (first + together) * span)
        own = column - (b - first) * span
        query = jnp.concatenate([q[rows, s * head : (s + 1) * head] for s in range(shares)], axis=0)
        old_keys = keys[pl.ds(pl.multiple_of(starts[r], UNIT), window), :]
        old = lax.dot_general(query, old_keys, contract, preferred_element_type=jnp.float32)
        new = lax.dot_general(query, k[both, :], contract, preferred_element_type=jnp.float32)
        old = jnp.where(column < length, old * score_scale, -jnp.inf)
        new = jnp.where((own >= 0) & (own <= token), new * score_scale, -jnp.inf)
        row_max = jnp.max(jnp.maximum(old, new), axis=-1, keepdims=True)
        old, new = jnp.exp(old - row_max), jnp.exp(new - row_max)
        row_total = jnp.sum(old + new, axis=-1, keepdims=True)
        weights[b * shares * span : (b + 1) * shares * span, :] = old.astype(jnp.bfloat16)
        mixed = jnp.dot(new.astype(jnp.bfloat16), v[both, :], preferred_element_type=jnp.float32)
        for s in range(shares):
            columns, here = slice(s * head, (s + 1) * head), slice(s * span, (s + 1) * span)
            mixed_new[rows, columns] = mixed[here]
            factor[rows, columns] = g[rows, columns] / row_total[here]


def weigh(starts, lengths, q, g, k, v, keys, window):
    rows, columns = q.shape
    head = k.shape[1]
    shares = columns // head
    step = rows // lengths.shape[0] * BATCH
    tile = lambda width: pl.BlockSpec((step, width), lambda i, *_: (i, 0))
    whole = lambda a: pl.BlockSpec(a.shape, lambda i, *_: (0, 0))
    return pl.pallas_call(
        weigh_kernel,
        out_shape=(
            jax.ShapeDtypeStruct((shares * rows, window), jnp.bfloat16),
            jax.ShapeDtypeStruct((rows, columns), jnp.float32),
            jax.ShapeDtypeStruct((rows, columns), jnp.float32),
        ),
        grid_spec=pltpu.PrefetchScalarGridSpec(
            num_scalar_prefetch=2,
            grid=(rows // step,),
            in_specs=[tile(columns)] * 2 + [tile(head)] * 2 + [whole(a) for a in keys],
            out_specs=(
                pl.BlockSpec((shares * step, window), lambda i, *_: (i, 0)),
                tile(columns),
                tile(columns),
            ),
            scratch_shapes=[pltpu.VMEM((4 * keys[0].shape[0] + window, head), keys[0].dtype)],
        ),
        compiler_params=pltpu.CompilerParams(vmem_limit_bytes=30 << 20),
        cost_estimate=COST,
        name="weigh",
    )(starts, lengths, q, g, k, v, *keys)


def mix_kernel(starts, lengths, weights, mixed_new, factor, *refs):
    parts, (out, values) = refs[:4], refs[4:]
    window, head = weights.shape[1], values.shape[1]
    span = out.shape[0] // BATCH
    shares = out.shape[1] // head

    @pl.when(pl.program_id(0) == 0)
    def _():
        gather_parts(parts, values)

    old_row = lax.broadcasted_iota(jnp.int32, (window, head), 0)
    for b in range(BATCH):
        r = pl.program_id(0) * BATCH + b
        rows = slice(b * span, (b + 1) * span)
        old_values = values[pl.ds(pl.multiple_of(starts[r], UNIT), window), :]
        old_values = jnp.where(old_row < lengths[r], old_values, jnp.zeros_like(old_values))
        old = weights[b * shares * span : (b + 1) * shares * span, :]
        mixed = jnp.dot(old, old_values, preferred_element_type=jnp.float32)
        for s in range(shares):
            columns, here = slice(s * head, (s + 1) * head), slice(s * span, (s + 1) * span)
            part = (mixed[here] + mixed_new[rows, columns]) * factor[rows, columns]
            out[rows, columns] = part.astype(jnp.bfloat16)


def mix(starts, lengths, weights, mixed_new, factor, values):
    rows, columns = factor.shape
    window, head = weights.shape[1], values[0].shape[1]
    step = rows // lengths.shape[0] * BATCH
    tile = lambda width: pl.BlockSpec((step, width), lambda i, *_: (i, 0))
    whole = lambda a: pl.BlockSpec(a.shape, lambda i, *_: (0, 0))
    return pl.pallas_call(
        mix_kernel,
        out_shape=jax.ShapeDtypeStruct((rows, columns), jnp.bfloat16),
        grid_spec=pltpu.PrefetchScalarGridSpec(
            num_scalar_prefetch=2,
            grid=(rows // step,),
            in_specs=[
                pl.BlockSpec((columns // head * step, window), lambda i, *_: (i, 0)),
                tile(columns),
                tile(columns),
            ]
            + [whole(a) for a in values],
            out_specs=tile(columns),
            scratch_shapes=[pltpu.VMEM((4 * values[0].shape[0] + window, head), values[0].dtype)],
        ),
        compiler_params=pltpu.CompilerParams(vmem_limit_bytes=30 << 20),
        cost_estimate=COST,
        name="mix",
    )(starts, lengths, weights, mixed_new, factor, *values)


def pack_kernel(offsets, cache, *refs):
    outs, store = refs[:4], refs[4]
    sources, _, slots, window, head = cache.shape
    size = outs[0].shape[0]
    for k, out in enumerate(outs):
        for j in range(sources * slots):
            place = pl.multiple_of(offsets[4 + k * sources * slots + j], UNIT)
            store[pl.ds(place, window), :] = cache[j // slots, offsets[k], j % slots]
        out[...] = store[:size, :]


def pack(offsets, cache, size):
    window, head = cache.shape[3:]
    return pl.pallas_call(
        pack_kernel,
        out_shape=[jax.ShapeDtypeStruct((size, head), cache.dtype)] * 4,
        grid_spec=pltpu.PrefetchScalarGridSpec(
            num_scalar_prefetch=1,
            grid=(1,),
            in_specs=[pl.BlockSpec(cache.shape, lambda i, _: (0,) * 5)],
            out_specs=[pl.BlockSpec((size, head), lambda i, _: (0, 0))] * 4,
            scratch_shapes=[pltpu.VMEM((size + window, head), cache.dtype)],
        ),
        compiler_params=pltpu.CompilerParams(vmem_limit_bytes=16 << 20),
        cost_estimate=COST,
        name="pack",
    )(offsets, cache)


def by_target_kernel(source, target):
    for c in range(2):
        target[0, c] = source[0, :, c]


def by_target(cache):
    ny, nz, nc, capacity, window, head = cache.shape
    return pl.pallas_call(
        by_target_kernel,
        out_shape=jax.ShapeDtypeStruct((ny, nc, nz, capacity, window, head), cache.dtype),
        grid=(ny,),
        in_specs=[pl.BlockSpec((1, nz, nc, capacity, window, head), lambda i: (i, 0, 0, 0, 0, 0))],
        out_specs=pl.BlockSpec((1, nc, nz, capacity, window, head), lambda i: (i, 0, 0, 0, 0, 0)),
        compiler_params=pltpu.CompilerParams(vmem_limit_bytes=12 << 20),
        cost_estimate=LONG,
        name="by_target",
    )(cache)


def pair_kernel(half, twin, out):
    out[0], out[1] = half[...], twin[...]


def pair(half, twin):
    depth, columns = half.shape
    tile = 512
    part = pl.BlockSpec((depth, tile), lambda i: (0, i))
    return pl.pallas_call(
        pair_kernel,
        out_shape=jax.ShapeDtypeStruct((2, depth, columns), half.dtype),
        grid=(columns // tile,),
        in_specs=[part, part],
        out_specs=pl.BlockSpec((2, depth, tile), lambda i: (0, 0, i)),
        compiler_params=pltpu.CompilerParams(vmem_limit_bytes=12 << 20),
        cost_estimate=COST,
        name="pair",
    )(half, twin)


def output_kernel(places, heads, mine, other, out, joined):
    count, depth = mine.shape[:2]

    @pl.when(pl.program_id(0) == 0)
    def _():
        for j in range(count):
            for h in range(2):
                first = pl.multiple_of((places[count] + h) % 2 * depth, depth)
                columns = slice((2 * j + h) * depth, (2 * j + h + 1) * depth)
                joined[:, columns] = heads[places[j], :, pl.ds(first, depth)]

    total = jnp.zeros(out.shape, jnp.float32)
    for j in range(count):
        weight = jnp.concatenate([mine[j], other[j]], axis=0)
        part = joined[:, 2 * j * depth : 2 * (j + 1) * depth]
        total = total + jnp.dot(part, weight, preferred_element_type=jnp.float32)
    out[...] = total.astype(jnp.bfloat16)


def project_out(places, heads, mine, other):
    blocks, rows, width = heads.shape
    depth, columns = mine.shape[1:]
    tile = 512
    half = pl.BlockSpec((blocks, depth, tile), lambda i, _: (0, 0, i))
    return pl.pallas_call(
        output_kernel,
        out_shape=jax.ShapeDtypeStruct((rows, columns), jnp.bfloat16),
        grid_spec=pltpu.PrefetchScalarGridSpec(
            num_scalar_prefetch=1,
            grid=(columns // tile,),
            in_specs=[pl.BlockSpec(heads.shape, lambda i, _: (0, 0, 0)), half, half],
            out_specs=pl.BlockSpec((rows, tile), lambda i, _: (0, i)),
            scratch_shapes=[pltpu.VMEM((rows, blocks * width), jnp.bfloat16)],
        ),
        compiler_params=pltpu.CompilerParams(vmem_limit_bytes=30 << 20),
        cost_estimate=COST,
        name="project_out",
    )(places, heads, mine, other)


def across_y(slots):
    ny, nc, nz, capacity, window, head = slots.shape
    flat = slots.reshape(ny * nc, nz * capacity * window, head)
    flat = lax.all_to_all(flat, ("y", "c"), 0, 0, tiled=True)
    return flat.reshape(ny * nc, nz, capacity, window, head)


def across_z(parts):
    return [parts[0]] + [shift(parts[k], "zh", k) for k in range(1, 4)]


def local(
    span_rows,
    norm_gain,
    q_weight,
    gate_weight,
    k_weight,
    v_weight,
    q_norm_gain,
    k_norm_gain,
    o_weight,
    key_cache,
    value_cache,
    holders,
    prefix_lengths,
):
    groups = lax.axis_size(GROUP)
    group_id = lax.axis_index(GROUP)
    requests = prefix_lengths.shape[0] // groups
    rows = span_rows.shape[0]
    span_len = rows // requests
    head_dim = q_norm_gain.shape[0]
    capacity = key_cache.shape[1] // groups
    window = key_cache.shape[2]
    blocks = lax.axis_size(TENSOR)

    y, zh, core = lax.axis_index("y"), lax.axis_index("zh"), lax.axis_index("c")
    all_holders = holders.reshape(groups, requests)
    all_lengths = prefix_lengths.reshape(groups, requests)
    order = jnp.arange(requests)
    earlier = order[None, :] < order[:, None]
    same = all_holders[:, :, None] == all_holders[:, None, :]
    all_ranks = jnp.sum(same & earlier[None], axis=2)
    all_units = (all_lengths + UNIT - 1) // UNIT
    plane = all_holders // 2 % 4
    per_plane = jnp.sum(
        jnp.where(plane[:, :, None] == jnp.arange(4), all_units[:, :, None], 0), axis=1
    )
    fits = jnp.max(per_plane) * UNIT <= PACKED

    slot_y = jnp.arange(4)[:, None, None]
    slot_c = jnp.arange(2)[None, :, None]
    slot_rank = jnp.arange(capacity)[None, None, :]
    z_ids = (zh + jnp.arange(4)) % 4
    served = (y * 4 + z_ids) * 2 + core
    slot_holder = (slot_y * 4 + zh) * 2 + slot_c
    slot_key = (slot_holder * capacity + slot_rank).reshape(-1)
    served_key = (all_holders * capacity + all_ranks)[served]
    hit = served_key[:, :, None] == slot_key[None, None, :]
    slot_units = jnp.sum(jnp.where(hit, all_units[served][:, :, None], 0), axis=1)
    offsets = (jnp.cumsum(slot_units, axis=1) - slot_units) * UNIT

    mine = lambda a: lax.dynamic_index_in_dim(a, group_id, 0, keepdims=False)
    my_holders, my_ranks, my_lengths, my_units = map(
        mine, (all_holders, all_ranks, all_lengths, all_units)
    )
    from_z = (zh - my_holders // 2 % 4) % 4
    my_order = (my_holders // 8 * 2 + my_holders % 2) * capacity + my_ranks
    ahead = (from_z[:, None] == from_z[None, :]) & (my_order[None, :] < my_order[:, None])
    my_start = jnp.sum(jnp.where(ahead, my_units[None, :], 0), axis=1) * UNIT

    def packing(size):
        limit = jnp.minimum(offsets, size).reshape(-1)
        places = jnp.concatenate([z_ids, limit]).astype(jnp.int32)
        starts = jnp.minimum(from_z * size + my_start, 4 * size)
        return places, starts.astype(jnp.int32)

    positions = my_lengths[:, None] + jnp.arange(span_len, dtype=jnp.int32)[None, :]
    channel = jnp.arange(head_dim)
    half = head_dim // 2
    frequency = ROPE_BASE ** (-(channel % half).astype(jnp.float32) * 2.0 / head_dim)
    angles = positions.reshape(-1).astype(jnp.float32)[:, None] * frequency
    cosine = jnp.cos(angles)
    sine = jnp.sin(angles) * jnp.where(channel < half, -1.0, 1.0)

    ids = block_ids()
    sides = (4, 4, 2, capacity, window, head_dim)
    places, starts = packing(PACKED)
    pieces = spread(span_rows)
    depth = o_weight.shape[0] // 2
    half = lax.dynamic_slice_in_dim(o_weight, core * depth, depth, 0)
    half, pieces[1] = lax.optimization_barrier((half, pieces[1]))
    twin_half = shift(half, "zl", 1)

    key_part = across_y(by_target(key_cache.reshape(sides)))
    gain = norm_gain.reshape(-1, 1)
    tables = (ids, places, starts, fits, gain, cosine, sine)
    value_slots, key_part, pieces[1:6], twin_half, tables = lax.optimization_barrier(
        (by_target(value_cache.reshape(sides)), key_part, pieces[1:6], twin_half, tables)
    )
    ids, places, starts, fits, gain, cosine, sine = tables
    value_part = across_y(value_slots)
    halves = lax.all_gather(pair(half, twin_half), "x").reshape((blocks,) + half.shape)
    keys = across_z(pack(places, key_part, PACKED))
    value_part, keys[1] = lax.optimization_barrier((value_part, keys[1]))
    packed_values, keys, pieces[6:] = lax.optimization_barrier(
        (pack(places, value_part, PACKED), keys, pieces[6:])
    )
    values = across_z(packed_values)
    q, g, k, v = project(
        ids, pieces, gain, q_weight, gate_weight, k_weight, v_weight,
        q_norm_gain, k_norm_gain, cosine, sine,
    )

    size = 8 * capacity * window

    def packed(values, key_part, value_part, q, g, k, v, *weighed):
        return mix(starts, my_lengths, *weighed, values)

    def full(values, key_part, value_part, q, g, k, v, *weighed):
        places, starts = packing(size)
        keys, values = (across_z(pack(places, a, size)) for a in (key_part, value_part))
        weighed = weigh(starts, my_lengths, q, g, k, v, keys, window)
        return mix(starts, my_lengths, *weighed, values)

    weighed = weigh(starts, my_lengths, q, g, k, v, keys, window)
    halves, weighed = lax.optimization_barrier((halves, weighed))
    other_halves = shift(halves, "c", 1)
    attended = lax.cond(fits, packed, full, values, key_part, value_part, q, g, k, v, *weighed)
    heads = lax.all_to_all(
        attended.reshape(blocks, rows // blocks, attended.shape[1]), TENSOR, 0, 0, tiled=True
    )
    x_ids, zl_ids = jnp.arange(blocks) // 2, (lax.axis_index("zl") + jnp.arange(blocks)) % 2
    out_places = jnp.concatenate([zl_ids * 4 + x_ids, core[None]]).astype(jnp.int32)
    return project_out(out_places, heads, halves, other_halves)


def solution(mesh):
    mesh = Mesh(mesh.devices.reshape(4, 4, 2, 2, 4), GROUP + TENSOR)
    placed = (
        P(GROUP, TENSOR),
        P(),
        P(None, TENSOR),
        P(None, TENSOR),
        P(None, TENSOR),
        P(None, TENSOR),
        P(),
        P(),
        P(TENSOR, None),
        P(GROUP, None, None, TENSOR),
        P(GROUP, None, None, TENSOR),
        P(),
        P(),
    )
    return jax.shard_map(
        local, mesh=mesh, in_specs=placed, out_specs=P(GROUP + TENSOR, None), check_vma=False
    )
```

```python
import functools
import math

import jax
import jax.numpy as jnp
from jax import lax
from jax.experimental import pallas as pl
from jax.experimental.pallas import tpu as pltpu
from jax.sharding import Mesh
from jax.sharding import PartitionSpec as P

EPSILON = 1e-06
ROPE_BASE = 1000000.0
GROUP = ("y", "zh", "c")
TENSOR = ("zl", "x")
ROW_TILE = 256
BATCH = 4
UNIT = 16
PACKED = 68 * UNIT
LONG = pl.CostEstimate(flops=1 << 20, bytes_accessed=64 << 20, transcendentals=0)
COST = pl.CostEstimate(flops=1 << 20, bytes_accessed=1 << 20, transcendentals=0)


def ring(size, step):
    return [(i, (i + step) % size) for i in range(size)]


def shift(value, axis, step):
    return lax.ppermute(value, axis, ring(lax.axis_size(axis), step))


def spread(block):
    twin = shift(block, "zl", 1)
    below, above = shift(block, "x", 1), shift(block, "x", -1)
    twin_below, twin_above = shift(twin, "x", 1), shift(twin, "x", -1)
    far = shift(below, "x", 1)
    twin_far = shift(twin_above, "x", -1)
    return [block, twin, below, above, twin_below, twin_above, far, twin_far]


def block_ids():
    zl, x = lax.axis_index("zl"), lax.axis_index("x")
    pairs = [(0, 0), (1, 0), (0, 3), (0, 1), (1, 3), (1, 1), (0, 2), (1, 2)]
    return jnp.stack([((zl + dz) % 2) * 4 + (x + dx) % 4 for dz, dx in pairs]).astype(jnp.int32)


def head_norm_rotate(values, gain, cosine, sine):
    scale = lax.rsqrt(jnp.mean(values * values, axis=-1, keepdims=True) + EPSILON)
    scaled = values * scale * gain
    half = values.shape[-1] // 2
    return scaled * cosine + pltpu.roll(scaled, half, 1) * sine


def project_kernel(ids, *refs):
    pieces, rest = refs[:8], refs[8:]
    (gain, wq, wg, wk, wv, q_gain, k_gain, cosine, sine, q_out, g_out, k_out, v_out, scaled) = rest
    rows, width = pieces[0].shape
    head = wk.shape[1]
    edges = [0]
    for w in (wq, wg, wk, wv):
        edges.append(edges[-1] + w.shape[1])

    @pl.when(pl.program_id(0) == 0)
    def _():
        for j in range(8):
            block = pl.multiple_of(ids[j] * width, width)
            here = pl.ds(block, width)
            for w, first, last in zip((wq, wg, wk, wv), edges, edges[1:]):
                lanes = jnp.concatenate([gain[here, :]] * ((last - first) // head), axis=1)
                part = w[here, :].astype(jnp.float32) * lanes
                scaled[j * width : (j + 1) * width, first:last] = part.astype(jnp.bfloat16)

    total = jnp.zeros((rows, 128), jnp.float32)
    product = jnp.zeros((rows, edges[-1]), jnp.float32)
    for j, piece in enumerate(pieces):
        value = piece[...]
        product = product + jnp.dot(
            value, scaled[j * width : (j + 1) * width, :], preferred_element_type=jnp.float32
        )
        value = value.astype(jnp.float32)
        square = value * value
        for first in range(0, width, 128):
            total = total + square[:, first : first + 128]
    total = jnp.sum(total, axis=-1, keepdims=True)
    product = product * lax.rsqrt(total / (8 * width) + EPSILON)
    cos, sin = cosine[...], sine[...]
    for h in range(edges[1] // head):
        here = slice(h * head, (h + 1) * head)
        part = head_norm_rotate(product[:, here], q_gain[...], cos, sin)
        q_out[:, here] = part.astype(jnp.bfloat16)
    g_out[...] = jax.nn.sigmoid(product[:, edges[1] : edges[2]])
    k = head_norm_rotate(product[:, edges[2] : edges[3]], k_gain[...], cos, sin)
    k_out[...] = k.astype(jnp.bfloat16)
    v_out[...] = product[:, edges[3] : edges[4]].astype(jnp.bfloat16)


def project(ids, pieces, gain, wq, wg, wk, wv, q_gain, k_gain, cosine, sine):
    rows, width = pieces[0].shape
    depth = gain.shape[0]
    head = q_gain.shape[0]
    tile = lambda columns: pl.BlockSpec((ROW_TILE, columns), lambda i, _: (i, 0))
    whole = lambda a: pl.BlockSpec(a.shape, lambda i, _: (0, 0))
    q_gain, k_gain = q_gain.reshape(1, head), k_gain.reshape(1, head)
    constants = (gain, wq, wg, wk, wv, q_gain, k_gain)
    columns = sum(w.shape[1] for w in (wq, wg, wk, wv))
    return pl.pallas_call(
        project_kernel,
        out_shape=(
            jax.ShapeDtypeStruct((rows, wq.shape[1]), jnp.bfloat16),
            jax.ShapeDtypeStruct((rows, wg.shape[1]), jnp.float32),
            jax.ShapeDtypeStruct((rows, head), jnp.bfloat16),
            jax.ShapeDtypeStruct((rows, head), jnp.bfloat16),
        ),
        grid_spec=pltpu.PrefetchScalarGridSpec(
            num_scalar_prefetch=1,
            grid=(rows // ROW_TILE,),
            in_specs=[tile(width)] * 8 + [whole(a) for a in constants] + [tile(head)] * 2,
            out_specs=[tile(wq.shape[1]), tile(wg.shape[1]), tile(head), tile(head)],
            scratch_shapes=[pltpu.VMEM((depth, columns), jnp.bfloat16)],
        ),
        cost_estimate=COST,
        name="project",
    )(ids, *pieces, *constants, cosine, sine)


def gather_parts(parts, store):
    size = parts[0].shape[0]
    for j, part in enumerate(parts):
        store[j * size : (j + 1) * size, :] = part[...]
    slack = slice(len(parts) * size, store.shape[0])
    store[slack, :] = jnp.zeros((store.shape[0] - len(parts) * size, store.shape[1]), store.dtype)


def weigh_kernel(starts, lengths, q, g, k, v, *refs):
    parts, (weights, mixed_new, factor, keys) = refs[:4], refs[4:]
    head = k.shape[1]
    span = q.shape[0] // BATCH
    shares = q.shape[1] // head
    window = keys.shape[0] - 4 * parts[0].shape[0]
    score_scale = 1.0 / math.sqrt(head)
    contract = (((1,), (1,)), ((), ()))

    @pl.when(pl.program_id(0) == 0)
    def _():
        gather_parts(parts, keys)

    column = lax.broadcasted_iota(jnp.int32, (shares * span, window), 1)
    token = lax.broadcasted_iota(jnp.int32, (shares, span, window), 1)
    token = token.reshape(shares * span, window)
    together = window // span
    for b in range(BATCH):
        r = pl.program_id(0) * BATCH + b
        length = lengths[r]
        rows = slice(b * span, (b + 1) * span)
        first = b // together * together
        both = slice(first * span, (first + together) * span)
        own = column - (b - first) * span
        query = jnp.concatenate([q[rows, s * head : (s + 1) * head] for s in range(shares)], axis=0)
        old_keys = keys[pl.ds(pl.multiple_of(starts[r], UNIT), window), :]
        old = lax.dot_general(query, old_keys, contract, preferred_element_type=jnp.float32)
        new = lax.dot_general(query, k[both, :], contract, preferred_element_type=jnp.float32)
        old = jnp.where(column < length, old * score_scale, -jnp.inf)
        new = jnp.where((own >= 0) & (own <= token), new * score_scale, -jnp.inf)
        row_max = jnp.max(jnp.maximum(old, new), axis=-1, keepdims=True)
        old, new = jnp.exp(old - row_max), jnp.exp(new - row_max)
        row_total = jnp.sum(old + new, axis=-1, keepdims=True)
        weights[b * shares * span : (b + 1) * shares * span, :] = old.astype(jnp.bfloat16)
        mixed = jnp.dot(new.astype(jnp.bfloat16), v[both, :], preferred_element_type=jnp.float32)
        for s in range(shares):
            columns, here = slice(s * head, (s + 1) * head), slice(s * span, (s + 1) * span)
            mixed_new[rows, columns] = mixed[here]
            factor[rows, columns] = g[rows, columns] / row_total[here]


def weigh(starts, lengths, q, g, k, v, keys, window):
    rows, columns = q.shape
    head = k.shape[1]
    shares = columns // head
    step = rows // lengths.shape[0] * BATCH
    tile = lambda width: pl.BlockSpec((step, width), lambda i, *_: (i, 0))
    whole = lambda a: pl.BlockSpec(a.shape, lambda i, *_: (0, 0))
    return pl.pallas_call(
        weigh_kernel,
        out_shape=(
            jax.ShapeDtypeStruct((shares * rows, window), jnp.bfloat16),
            jax.ShapeDtypeStruct((rows, columns), jnp.float32),
            jax.ShapeDtypeStruct((rows, columns), jnp.float32),
        ),
        grid_spec=pltpu.PrefetchScalarGridSpec(
            num_scalar_prefetch=2,
            grid=(rows // step,),
            in_specs=[tile(columns)] * 2 + [tile(head)] * 2 + [whole(a) for a in keys],
            out_specs=(
                pl.BlockSpec((shares * step, window), lambda i, *_: (i, 0)),
                tile(columns),
                tile(columns),
            ),
            scratch_shapes=[pltpu.VMEM((4 * keys[0].shape[0] + window, head), keys[0].dtype)],
        ),
        compiler_params=pltpu.CompilerParams(vmem_limit_bytes=30 << 20),
        cost_estimate=COST,
        name="weigh",
    )(starts, lengths, q, g, k, v, *keys)


def mix_kernel(starts, lengths, weights, mixed_new, factor, *refs):
    parts, (out, values) = refs[:4], refs[4:]
    window, head = weights.shape[1], values.shape[1]
    span = out.shape[0] // BATCH
    shares = out.shape[1] // head

    @pl.when(pl.program_id(0) == 0)
    def _():
        gather_parts(parts, values)

    old_row = lax.broadcasted_iota(jnp.int32, (window, head), 0)
    for b in range(BATCH):
        r = pl.program_id(0) * BATCH + b
        rows = slice(b * span, (b + 1) * span)
        old_values = values[pl.ds(pl.multiple_of(starts[r], UNIT), window), :]
        old_values = jnp.where(old_row < lengths[r], old_values, jnp.zeros_like(old_values))
        old = weights[b * shares * span : (b + 1) * shares * span, :]
        mixed = jnp.dot(old, old_values, preferred_element_type=jnp.float32)
        for s in range(shares):
            columns, here = slice(s * head, (s + 1) * head), slice(s * span, (s + 1) * span)
            part = (mixed[here] + mixed_new[rows, columns]) * factor[rows, columns]
            out[rows, columns] = part.astype(jnp.bfloat16)


def mix(starts, lengths, weights, mixed_new, factor, values):
    rows, columns = factor.shape
    window, head = weights.shape[1], values[0].shape[1]
    step = rows // lengths.shape[0] * BATCH
    tile = lambda width: pl.BlockSpec((step, width), lambda i, *_: (i, 0))
    whole = lambda a: pl.BlockSpec(a.shape, lambda i, *_: (0, 0))
    return pl.pallas_call(
        mix_kernel,
        out_shape=jax.ShapeDtypeStruct((rows, columns), jnp.bfloat16),
        grid_spec=pltpu.PrefetchScalarGridSpec(
            num_scalar_prefetch=2,
            grid=(rows // step,),
            in_specs=[
                pl.BlockSpec((columns // head * step, window), lambda i, *_: (i, 0)),
                tile(columns),
                tile(columns),
            ]
            + [whole(a) for a in values],
            out_specs=tile(columns),
            scratch_shapes=[pltpu.VMEM((4 * values[0].shape[0] + window, head), values[0].dtype)],
        ),
        compiler_params=pltpu.CompilerParams(vmem_limit_bytes=30 << 20),
        cost_estimate=COST,
        name="mix",
    )(starts, lengths, weights, mixed_new, factor, *values)


def pack_kernel(offsets, cache, *refs):
    outs, store = refs[:4], refs[4]
    sources, _, slots, window, head = cache.shape
    size = outs[0].shape[0]
    for k, out in enumerate(outs):
        for j in range(sources * slots):
            place = pl.multiple_of(offsets[4 + k * sources * slots + j], UNIT)
            store[pl.ds(place, window), :] = cache[j // slots, offsets[k], j % slots]
        out[...] = store[:size, :]


def pack(offsets, cache, size):
    window, head = cache.shape[3:]
    return pl.pallas_call(
        pack_kernel,
        out_shape=[jax.ShapeDtypeStruct((size, head), cache.dtype)] * 4,
        grid_spec=pltpu.PrefetchScalarGridSpec(
            num_scalar_prefetch=1,
            grid=(1,),
            in_specs=[pl.BlockSpec(cache.shape, lambda i, _: (0,) * 5)],
            out_specs=[pl.BlockSpec((size, head), lambda i, _: (0, 0))] * 4,
            scratch_shapes=[pltpu.VMEM((size + window, head), cache.dtype)],
        ),
        compiler_params=pltpu.CompilerParams(vmem_limit_bytes=16 << 20),
        cost_estimate=COST,
        name="pack",
    )(offsets, cache)


def by_target_kernel(source, target):
    for c in range(2):
        target[0, c] = source[0, :, c]


def by_target(cache):
    ny, nz, nc, capacity, window, head = cache.shape
    return pl.pallas_call(
        by_target_kernel,
        out_shape=jax.ShapeDtypeStruct((ny, nc, nz, capacity, window, head), cache.dtype),
        grid=(ny,),
        in_specs=[pl.BlockSpec((1, nz, nc, capacity, window, head), lambda i: (i, 0, 0, 0, 0, 0))],
        out_specs=pl.BlockSpec((1, nc, nz, capacity, window, head), lambda i: (i, 0, 0, 0, 0, 0)),
        compiler_params=pltpu.CompilerParams(vmem_limit_bytes=12 << 20),
        cost_estimate=LONG,
        name="by_target",
    )(cache)


def pair_kernel(half, twin, out):
    out[0], out[1] = half[...], twin[...]


def pair(half, twin):
    depth, columns = half.shape
    tile = 512
    part = pl.BlockSpec((depth, tile), lambda i: (0, i))
    return pl.pallas_call(
        pair_kernel,
        out_shape=jax.ShapeDtypeStruct((2, depth, columns), half.dtype),
        grid=(columns // tile,),
        in_specs=[part, part],
        out_specs=pl.BlockSpec((2, depth, tile), lambda i: (0, 0, i)),
        compiler_params=pltpu.CompilerParams(vmem_limit_bytes=12 << 20),
        cost_estimate=COST,
        name="pair",
    )(half, twin)


def output_kernel(places, heads, mine, other, out, joined):
    count, depth = mine.shape[:2]

    @pl.when(pl.program_id(0) == 0)
    def _():
        for j in range(count):
            for h in range(2):
                first = pl.multiple_of((places[count] + h) % 2 * depth, depth)
                columns = slice((2 * j + h) * depth, (2 * j + h + 1) * depth)
                joined[:, columns] = heads[places[j], :, pl.ds(first, depth)]

    total = jnp.zeros(out.shape, jnp.float32)
    for j in range(count):
        weight = jnp.concatenate([mine[j], other[j]], axis=0)
        part = joined[:, 2 * j * depth : 2 * (j + 1) * depth]
        total = total + jnp.dot(part, weight, preferred_element_type=jnp.float32)
    out[...] = total.astype(jnp.bfloat16)


def project_out(places, heads, mine, other):
    blocks, rows, width = heads.shape
    depth, columns = mine.shape[1:]
    tile = 512
    half = pl.BlockSpec((blocks, depth, tile), lambda i, _: (0, 0, i))
    return pl.pallas_call(
        output_kernel,
        out_shape=jax.ShapeDtypeStruct((rows, columns), jnp.bfloat16),
        grid_spec=pltpu.PrefetchScalarGridSpec(
            num_scalar_prefetch=1,
            grid=(columns // tile,),
            in_specs=[pl.BlockSpec(heads.shape, lambda i, _: (0, 0, 0)), half, half],
            out_specs=pl.BlockSpec((rows, tile), lambda i, _: (0, i)),
            scratch_shapes=[pltpu.VMEM((rows, blocks * width), jnp.bfloat16)],
        ),
        compiler_params=pltpu.CompilerParams(vmem_limit_bytes=30 << 20),
        cost_estimate=COST,
        name="project_out",
    )(places, heads, mine, other)


def across_y(slots):
    ny, nc, nz, capacity, window, head = slots.shape
    flat = slots.reshape(ny * nc, nz * capacity * window, head)
    flat = lax.all_to_all(flat, ("y", "c"), 0, 0, tiled=True)
    return flat.reshape(ny * nc, nz, capacity, window, head)


def across_z(parts):
    return [parts[0]] + [shift(parts[k], "zh", k) for k in range(1, 4)]


def local(
    span_rows,
    norm_gain,
    q_weight,
    gate_weight,
    k_weight,
    v_weight,
    q_norm_gain,
    k_norm_gain,
    o_weight,
    key_cache,
    value_cache,
    holders,
    prefix_lengths,
):
    groups = lax.axis_size(GROUP)
    group_id = lax.axis_index(GROUP)
    requests = prefix_lengths.shape[0] // groups
    rows = span_rows.shape[0]
    span_len = rows // requests
    head_dim = q_norm_gain.shape[0]
    capacity = key_cache.shape[1] // groups
    window = key_cache.shape[2]
    blocks = lax.axis_size(TENSOR)

    y, zh, core = lax.axis_index("y"), lax.axis_index("zh"), lax.axis_index("c")
    all_holders = holders.reshape(groups, requests)
    all_lengths = prefix_lengths.reshape(groups, requests)
    order = jnp.arange(requests)
    earlier = order[None, :] < order[:, None]
    same = all_holders[:, :, None] == all_holders[:, None, :]
    all_ranks = jnp.sum(same & earlier[None], axis=2)
    all_units = (all_lengths + UNIT - 1) // UNIT
    plane = all_holders // 2 % 4
    per_plane = jnp.sum(
        jnp.where(plane[:, :, None] == jnp.arange(4), all_units[:, :, None], 0), axis=1
    )
    fits = jnp.max(per_plane) * UNIT <= PACKED

    slot_y = jnp.arange(4)[:, None, None]
    slot_c = jnp.arange(2)[None, :, None]
    slot_rank = jnp.arange(capacity)[None, None, :]
    z_ids = (zh + jnp.arange(4)) % 4
    served = (y * 4 + z_ids) * 2 + core
    slot_holder = (slot_y * 4 + zh) * 2 + slot_c
    slot_key = (slot_holder * capacity + slot_rank).reshape(-1)
    served_key = (all_holders * capacity + all_ranks)[served]
    hit = served_key[:, :, None] == slot_key[None, None, :]
    slot_units = jnp.sum(jnp.where(hit, all_units[served][:, :, None], 0), axis=1)
    offsets = (jnp.cumsum(slot_units, axis=1) - slot_units) * UNIT

    mine = lambda a: lax.dynamic_index_in_dim(a, group_id, 0, keepdims=False)
    my_holders, my_ranks, my_lengths, my_units = map(
        mine, (all_holders, all_ranks, all_lengths, all_units)
    )
    from_z = (zh - my_holders // 2 % 4) % 4
    my_order = (my_holders // 8 * 2 + my_holders % 2) * capacity + my_ranks
    ahead = (from_z[:, None] == from_z[None, :]) & (my_order[None, :] < my_order[:, None])
    my_start = jnp.sum(jnp.where(ahead, my_units[None, :], 0), axis=1) * UNIT

    def packing(size):
        limit = jnp.minimum(offsets, size).reshape(-1)
        places = jnp.concatenate([z_ids, limit]).astype(jnp.int32)
        starts = jnp.minimum(from_z * size + my_start, 4 * size)
        return places, starts.astype(jnp.int32)

    positions = my_lengths[:, None] + jnp.arange(span_len, dtype=jnp.int32)[None, :]
    channel = jnp.arange(head_dim)
    half = head_dim // 2
    frequency = ROPE_BASE ** (-(channel % half).astype(jnp.float32) * 2.0 / head_dim)
    angles = positions.reshape(-1).astype(jnp.float32)[:, None] * frequency
    cosine = jnp.cos(angles)
    sine = jnp.sin(angles) * jnp.where(channel < half, -1.0, 1.0)

    ids = block_ids()
    sides = (4, 4, 2, capacity, window, head_dim)
    places, starts = packing(PACKED)
    pieces = spread(span_rows)
    depth = o_weight.shape[0] // 2
    half = lax.dynamic_slice_in_dim(o_weight, core * depth, depth, 0)
    half, pieces[1] = lax.optimization_barrier((half, pieces[1]))
    twin_half = shift(half, "zl", 1)

    key_part = across_y(by_target(key_cache.reshape(sides)))
    gain = jnp.broadcast_to(norm_gain[:, None], (norm_gain.shape[0], head_dim))
    tables = (ids, places, starts, fits, gain, cosine, sine)
    value_slots, key_part, pieces[1:6], both_halves, tables = lax.optimization_barrier(
        (by_target(value_cache.reshape(sides)), key_part, pieces[1:6], pair(half, twin_half), tables)
    )
    ids, places, starts, fits, gain, cosine, sine = tables
    value_part = across_y(value_slots)
    halves = lax.all_gather(both_halves, "x").reshape((blocks,) + half.shape)
    keys = across_z(pack(places, key_part, PACKED))
    q, g, k, v = project(
        ids, pieces, gain, q_weight, gate_weight, k_weight, v_weight,
        q_norm_gain, k_norm_gain, cosine, sine,
    )
    value_part, keys[1], q = lax.optimization_barrier((value_part, keys[1], q))
    packed_values, keys = lax.optimization_barrier((pack(places, value_part, PACKED), keys))
    values = across_z(packed_values)

    size = 8 * capacity * window

    def packed(values, key_part, value_part, q, g, k, v, *weighed):
        return mix(starts, my_lengths, *weighed, values)

    def full(values, key_part, value_part, q, g, k, v, *weighed):
        places, starts = packing(size)
        keys, values = (across_z(pack(places, a, size)) for a in (key_part, value_part))
        weighed = weigh(starts, my_lengths, q, g, k, v, keys, window)
        return mix(starts, my_lengths, *weighed, values)

    weighed = weigh(starts, my_lengths, q, g, k, v, keys, window)
    halves, weighed = lax.optimization_barrier((halves, weighed))
    other_halves = shift(halves, "c", 1)
    attended = lax.cond(fits, packed, full, values, key_part, value_part, q, g, k, v, *weighed)
    heads = lax.all_to_all(
        attended.reshape(blocks, rows // blocks, attended.shape[1]), TENSOR, 0, 0, tiled=True
    )
    x_ids, zl_ids = jnp.arange(blocks) // 2, (lax.axis_index("zl") + jnp.arange(blocks)) % 2
    out_places = jnp.concatenate([zl_ids * 4 + x_ids, core[None]]).astype(jnp.int32)
    return project_out(out_places, heads, halves, other_halves)


def solution(mesh):
    mesh = Mesh(mesh.devices.reshape(4, 4, 2, 2, 4), GROUP + TENSOR)
    placed = (
        P(GROUP, TENSOR),
        P(),
        P(None, TENSOR),
        P(None, TENSOR),
        P(None, TENSOR),
        P(None, TENSOR),
        P(),
        P(),
        P(TENSOR, None),
        P(GROUP, None, None, TENSOR),
        P(GROUP, None, None, TENSOR),
        P(),
        P(),
    )
    return jax.shard_map(
        local, mesh=mesh, in_specs=placed, out_specs=P(GROUP + TENSOR, None), check_vma=False
    )
```

```python
import functools
import math

import jax
import jax.numpy as jnp
from jax import lax
from jax.experimental import pallas as pl
from jax.experimental.pallas import tpu as pltpu
from jax.sharding import Mesh
from jax.sharding import PartitionSpec as P

EPSILON = 1e-06
ROPE_BASE = 1000000.0
GROUP = ("y", "zh", "c")
TENSOR = ("zl", "x")
ROW_TILE = 256
BATCH = 4
UNIT = 16
PACKED = 68 * UNIT
LONG = pl.CostEstimate(flops=1 << 20, bytes_accessed=64 << 20, transcendentals=0)
COST = pl.CostEstimate(flops=1 << 20, bytes_accessed=1 << 20, transcendentals=0)


def ring(size, step):
    return [(i, (i + step) % size) for i in range(size)]


def shift(value, axis, step):
    return lax.ppermute(value, axis, ring(lax.axis_size(axis), step))


def spread(block):
    twin = shift(block, "zl", 1)
    below, above = shift(block, "x", 1), shift(block, "x", -1)
    twin_below, twin_above = shift(twin, "x", 1), shift(twin, "x", -1)
    far = shift(below, "x", 1)
    twin_far = shift(twin_above, "x", -1)
    return [block, twin, below, above, twin_below, twin_above, far, twin_far]


def block_ids():
    zl, x = lax.axis_index("zl"), lax.axis_index("x")
    pairs = [(0, 0), (1, 0), (0, 3), (0, 1), (1, 3), (1, 1), (0, 2), (1, 2)]
    return jnp.stack([((zl + dz) % 2) * 4 + (x + dx) % 4 for dz, dx in pairs]).astype(jnp.int32)


def head_norm_rotate(values, gain, cosine, sine):
    scale = lax.rsqrt(jnp.mean(values * values, axis=-1, keepdims=True) + EPSILON)
    scaled = values * scale * gain
    half = values.shape[-1] // 2
    return scaled * cosine + pltpu.roll(scaled, half, 1) * sine


def project_kernel(ids, *refs):
    pieces, rest = refs[:8], refs[8:]
    (gain, wq, wg, wk, wv, q_gain, k_gain, cosine, sine, q_out, g_out, k_out, v_out, scaled) = rest
    rows, width = pieces[0].shape
    head = wk.shape[1]
    edges = [0]
    for w in (wq, wg, wk, wv):
        edges.append(edges[-1] + w.shape[1])

    @pl.when(pl.program_id(0) == 0)
    def _():
        for j in range(8):
            block = pl.multiple_of(ids[j] * width, width)
            here = pl.ds(block, width)
            for w, first, last in zip((wq, wg, wk, wv), edges, edges[1:]):
                lanes = jnp.concatenate([gain[here, :]] * ((last - first) // head), axis=1)
                part = w[here, :].astype(jnp.float32) * lanes
                scaled[j * width : (j + 1) * width, first:last] = part.astype(jnp.bfloat16)

    total = jnp.zeros((rows, 128), jnp.float32)
    product = jnp.zeros((rows, edges[-1]), jnp.float32)
    for j, piece in enumerate(pieces):
        value = piece[...]
        product = product + jnp.dot(
            value, scaled[j * width : (j + 1) * width, :], preferred_element_type=jnp.float32
        )
        value = value.astype(jnp.float32)
        square = value * value
        for first in range(0, width, 128):
            total = total + square[:, first : first + 128]
    total = jnp.sum(total, axis=-1, keepdims=True)
    product = product * lax.rsqrt(total / (8 * width) + EPSILON)
    cos, sin = cosine[...], sine[...]
    for h in range(edges[1] // head):
        here = slice(h * head, (h + 1) * head)
        part = head_norm_rotate(product[:, here], q_gain[...], cos, sin)
        q_out[:, here] = part.astype(jnp.bfloat16)
    g_out[...] = jax.nn.sigmoid(product[:, edges[1] : edges[2]])
    k = head_norm_rotate(product[:, edges[2] : edges[3]], k_gain[...], cos, sin)
    k_out[...] = k.astype(jnp.bfloat16)
    v_out[...] = product[:, edges[3] : edges[4]].astype(jnp.bfloat16)


def project(ids, pieces, gain, wq, wg, wk, wv, q_gain, k_gain, cosine, sine):
    rows, width = pieces[0].shape
    depth = gain.shape[0]
    head = q_gain.shape[0]
    tile = lambda columns: pl.BlockSpec((ROW_TILE, columns), lambda i, _: (i, 0))
    whole = lambda a: pl.BlockSpec(a.shape, lambda i, _: (0, 0))
    q_gain, k_gain = q_gain.reshape(1, head), k_gain.reshape(1, head)
    constants = (gain, wq, wg, wk, wv, q_gain, k_gain)
    columns = sum(w.shape[1] for w in (wq, wg, wk, wv))
    return pl.pallas_call(
        project_kernel,
        out_shape=(
            jax.ShapeDtypeStruct((rows, wq.shape[1]), jnp.bfloat16),
            jax.ShapeDtypeStruct((rows, wg.shape[1]), jnp.float32),
            jax.ShapeDtypeStruct((rows, head), jnp.bfloat16),
            jax.ShapeDtypeStruct((rows, head), jnp.bfloat16),
        ),
        grid_spec=pltpu.PrefetchScalarGridSpec(
            num_scalar_prefetch=1,
            grid=(rows // ROW_TILE,),
            in_specs=[tile(width)] * 8 + [whole(a) for a in constants] + [tile(head)] * 2,
            out_specs=[tile(wq.shape[1]), tile(wg.shape[1]), tile(head), tile(head)],
            scratch_shapes=[pltpu.VMEM((depth, columns), jnp.bfloat16)],
        ),
        cost_estimate=COST,
        name="project",
    )(ids, *pieces, *constants, cosine, sine)


def gather_parts(parts, store):
    size = parts[0].shape[0]
    for j, part in enumerate(parts):
        store[j * size : (j + 1) * size, :] = part[...]
    slack = slice(len(parts) * size, store.shape[0])
    store[slack, :] = jnp.zeros((store.shape[0] - len(parts) * size, store.shape[1]), store.dtype)


def weigh_kernel(starts, lengths, q, g, k, v, *refs):
    parts, (weights, mixed_new, factor, keys) = refs[:4], refs[4:]
    head = k.shape[1]
    span = q.shape[0] // BATCH
    shares = q.shape[1] // head
    window = keys.shape[0] - 4 * parts[0].shape[0]
    score_scale = 1.0 / math.sqrt(head)
    contract = (((1,), (1,)), ((), ()))

    @pl.when(pl.program_id(0) == 0)
    def _():
        gather_parts(parts, keys)

    column = lax.broadcasted_iota(jnp.int32, (shares * span, window), 1)
    token = lax.broadcasted_iota(jnp.int32, (shares, span, window), 1)
    token = token.reshape(shares * span, window)
    together = window // span
    for b in range(BATCH):
        r = pl.program_id(0) * BATCH + b
        length = lengths[r]
        rows = slice(b * span, (b + 1) * span)
        first = b // together * together
        both = slice(first * span, (first + together) * span)
        own = column - (b - first) * span
        query = jnp.concatenate([q[rows, s * head : (s + 1) * head] for s in range(shares)], axis=0)
        old_keys = keys[pl.ds(pl.multiple_of(starts[r], UNIT), window), :]
        old = lax.dot_general(query, old_keys, contract, preferred_element_type=jnp.float32)
        new = lax.dot_general(query, k[both, :], contract, preferred_element_type=jnp.float32)
        old = jnp.where(column < length, old * score_scale, -jnp.inf)
        new = jnp.where((own >= 0) & (own <= token), new * score_scale, -jnp.inf)
        row_max = jnp.max(jnp.maximum(old, new), axis=-1, keepdims=True)
        old, new = jnp.exp(old - row_max), jnp.exp(new - row_max)
        row_total = jnp.sum(old + new, axis=-1, keepdims=True)
        weights[b * shares * span : (b + 1) * shares * span, :] = old.astype(jnp.bfloat16)
        mixed = jnp.dot(new.astype(jnp.bfloat16), v[both, :], preferred_element_type=jnp.float32)
        for s in range(shares):
            columns, here = slice(s * head, (s + 1) * head), slice(s * span, (s + 1) * span)
            mixed_new[rows, columns] = mixed[here]
            factor[rows, columns] = g[rows, columns] / row_total[here]


def weigh(starts, lengths, q, g, k, v, keys, window):
    rows, columns = q.shape
    head = k.shape[1]
    shares = columns // head
    step = rows // lengths.shape[0] * BATCH
    tile = lambda width: pl.BlockSpec((step, width), lambda i, *_: (i, 0))
    whole = lambda a: pl.BlockSpec(a.shape, lambda i, *_: (0, 0))
    return pl.pallas_call(
        weigh_kernel,
        out_shape=(
            jax.ShapeDtypeStruct((shares * rows, window), jnp.bfloat16),
            jax.ShapeDtypeStruct((rows, columns), jnp.float32),
            jax.ShapeDtypeStruct((rows, columns), jnp.float32),
        ),
        grid_spec=pltpu.PrefetchScalarGridSpec(
            num_scalar_prefetch=2,
            grid=(rows // step,),
            in_specs=[tile(columns)] * 2 + [tile(head)] * 2 + [whole(a) for a in keys],
            out_specs=(
                pl.BlockSpec((shares * step, window), lambda i, *_: (i, 0)),
                tile(columns),
                tile(columns),
            ),
            scratch_shapes=[pltpu.VMEM((4 * keys[0].shape[0] + window, head), keys[0].dtype)],
        ),
        compiler_params=pltpu.CompilerParams(vmem_limit_bytes=30 << 20),
        cost_estimate=COST,
        name="weigh",
    )(starts, lengths, q, g, k, v, *keys)


def mix_kernel(starts, lengths, weights, mixed_new, factor, *refs):
    parts, (out, values) = refs[:4], refs[4:]
    window, head = weights.shape[1], values.shape[1]
    span = out.shape[0] // BATCH
    shares = out.shape[1] // head

    @pl.when(pl.program_id(0) == 0)
    def _():
        gather_parts(parts, values)

    old_row = lax.broadcasted_iota(jnp.int32, (window, head), 0)
    for b in range(BATCH):
        r = pl.program_id(0) * BATCH + b
        rows = slice(b * span, (b + 1) * span)
        old_values = values[pl.ds(pl.multiple_of(starts[r], UNIT), window), :]
        old_values = jnp.where(old_row < lengths[r], old_values, jnp.zeros_like(old_values))
        old = weights[b * shares * span : (b + 1) * shares * span, :]
        mixed = jnp.dot(old, old_values, preferred_element_type=jnp.float32)
        for s in range(shares):
            columns, here = slice(s * head, (s + 1) * head), slice(s * span, (s + 1) * span)
            part = (mixed[here] + mixed_new[rows, columns]) * factor[rows, columns]
            out[rows, columns] = part.astype(jnp.bfloat16)


def mix(starts, lengths, weights, mixed_new, factor, values):
    rows, columns = factor.shape
    window, head = weights.shape[1], values[0].shape[1]
    step = rows // lengths.shape[0] * BATCH
    tile = lambda width: pl.BlockSpec((step, width), lambda i, *_: (i, 0))
    whole = lambda a: pl.BlockSpec(a.shape, lambda i, *_: (0, 0))
    return pl.pallas_call(
        mix_kernel,
        out_shape=jax.ShapeDtypeStruct((rows, columns), jnp.bfloat16),
        grid_spec=pltpu.PrefetchScalarGridSpec(
            num_scalar_prefetch=2,
            grid=(rows // step,),
            in_specs=[
                pl.BlockSpec((columns // head * step, window), lambda i, *_: (i, 0)),
                tile(columns),
                tile(columns),
            ]
            + [whole(a) for a in values],
            out_specs=tile(columns),
            scratch_shapes=[pltpu.VMEM((4 * values[0].shape[0] + window, head), values[0].dtype)],
        ),
        compiler_params=pltpu.CompilerParams(vmem_limit_bytes=30 << 20),
        cost_estimate=COST,
        name="mix",
    )(starts, lengths, weights, mixed_new, factor, *values)


def pack_kernel(offsets, cache, *refs):
    outs, store = refs[:4], refs[4]
    sources, _, slots, window, head = cache.shape
    size = outs[0].shape[0]
    for k, out in enumerate(outs):
        for j in range(sources * slots):
            place = pl.multiple_of(offsets[4 + k * sources * slots + j], UNIT)
            store[pl.ds(place, window), :] = cache[j // slots, offsets[k], j % slots]
        out[...] = store[:size, :]


def pack(offsets, cache, size):
    window, head = cache.shape[3:]
    return pl.pallas_call(
        pack_kernel,
        out_shape=[jax.ShapeDtypeStruct((size, head), cache.dtype)] * 4,
        grid_spec=pltpu.PrefetchScalarGridSpec(
            num_scalar_prefetch=1,
            grid=(1,),
            in_specs=[pl.BlockSpec(cache.shape, lambda i, _: (0,) * 5)],
            out_specs=[pl.BlockSpec((size, head), lambda i, _: (0, 0))] * 4,
            scratch_shapes=[pltpu.VMEM((size + window, head), cache.dtype)],
        ),
        compiler_params=pltpu.CompilerParams(vmem_limit_bytes=16 << 20),
        cost_estimate=COST,
        name="pack",
    )(offsets, cache)


def by_target_kernel(source, target):
    for c in range(2):
        target[0, c] = source[0, :, c]


def by_target(cache):
    ny, nz, nc, capacity, window, head = cache.shape
    return pl.pallas_call(
        by_target_kernel,
        out_shape=jax.ShapeDtypeStruct((ny, nc, nz, capacity, window, head), cache.dtype),
        grid=(ny,),
        in_specs=[pl.BlockSpec((1, nz, nc, capacity, window, head), lambda i: (i, 0, 0, 0, 0, 0))],
        out_specs=pl.BlockSpec((1, nc, nz, capacity, window, head), lambda i: (i, 0, 0, 0, 0, 0)),
        compiler_params=pltpu.CompilerParams(vmem_limit_bytes=12 << 20),
        cost_estimate=LONG,
        name="by_target",
    )(cache)


def copies_kernel(half, twin, out):
    out[0, 0], out[0, 1] = half[...], twin[...]


def copies(half, twin):
    depth, columns = half.shape
    whole = pl.BlockSpec((depth, columns), lambda i: (0, 0))
    return pl.pallas_call(
        copies_kernel,
        out_shape=jax.ShapeDtypeStruct((4, 2, depth, columns), half.dtype),
        grid=(4,),
        in_specs=[whole, whole],
        out_specs=pl.BlockSpec((1, 2, depth, columns), lambda i: (i, 0, 0, 0)),
        compiler_params=pltpu.CompilerParams(vmem_limit_bytes=12 << 20),
        cost_estimate=COST,
        name="copies",
    )(half, twin)


def output_kernel(places, heads, mine, other, out, joined):
    count, depth = mine.shape[:2]

    @pl.when(pl.program_id(0) == 0)
    def _():
        for j in range(count):
            for h in range(2):
                first = pl.multiple_of((places[count] + h) % 2 * depth, depth)
                columns = slice((2 * j + h) * depth, (2 * j + h + 1) * depth)
                joined[:, columns] = heads[places[j], :, pl.ds(first, depth)]

    total = jnp.zeros(out.shape, jnp.float32)
    for j in range(count):
        weight = jnp.concatenate([mine[j], other[j]], axis=0)
        part = joined[:, 2 * j * depth : 2 * (j + 1) * depth]
        total = total + jnp.dot(part, weight, preferred_element_type=jnp.float32)
    out[...] = total.astype(jnp.bfloat16)


def project_out(places, heads, mine, other):
    blocks, rows, width = heads.shape
    depth, columns = mine.shape[1:]
    tile = 512
    half = pl.BlockSpec((blocks, depth, tile), lambda i, _: (0, 0, i))
    return pl.pallas_call(
        output_kernel,
        out_shape=jax.ShapeDtypeStruct((rows, columns), jnp.bfloat16),
        grid_spec=pltpu.PrefetchScalarGridSpec(
            num_scalar_prefetch=1,
            grid=(columns // tile,),
            in_specs=[pl.BlockSpec(heads.shape, lambda i, _: (0, 0, 0)), half, half],
            out_specs=pl.BlockSpec((rows, tile), lambda i, _: (0, i)),
            scratch_shapes=[pltpu.VMEM((rows, blocks * width), jnp.bfloat16)],
        ),
        compiler_params=pltpu.CompilerParams(vmem_limit_bytes=30 << 20),
        cost_estimate=COST,
        name="project_out",
    )(places, heads, mine, other)


def across_y(slots):
    ny, nc, nz, capacity, window, head = slots.shape
    flat = slots.reshape(ny * nc, nz * capacity * window, head)
    flat = lax.all_to_all(flat, ("y", "c"), 0, 0, tiled=True)
    return flat.reshape(ny * nc, nz, capacity, window, head)


def across_z(parts):
    return [parts[0]] + [shift(parts[k], "zh", k) for k in range(1, 4)]


def local(
    span_rows,
    norm_gain,
    q_weight,
    gate_weight,
    k_weight,
    v_weight,
    q_norm_gain,
    k_norm_gain,
    o_weight,
    key_cache,
    value_cache,
    holders,
    prefix_lengths,
):
    groups = lax.axis_size(GROUP)
    group_id = lax.axis_index(GROUP)
    requests = prefix_lengths.shape[0] // groups
    rows = span_rows.shape[0]
    span_len = rows // requests
    head_dim = q_norm_gain.shape[0]
    capacity = key_cache.shape[1] // groups
    window = key_cache.shape[2]
    blocks = lax.axis_size(TENSOR)

    y, zh, core = lax.axis_index("y"), lax.axis_index("zh"), lax.axis_index("c")
    all_holders = holders.reshape(groups, requests)
    all_lengths = prefix_lengths.reshape(groups, requests)
    order = jnp.arange(requests)
    earlier = order[None, :] < order[:, None]
    same = all_holders[:, :, None] == all_holders[:, None, :]
    all_ranks = jnp.sum(same & earlier[None], axis=2)
    all_units = (all_lengths + UNIT - 1) // UNIT
    plane = all_holders // 2 % 4
    per_plane = jnp.sum(
        jnp.where(plane[:, :, None] == jnp.arange(4), all_units[:, :, None], 0), axis=1
    )
    fits = jnp.max(per_plane) * UNIT <= PACKED

    slot_y = jnp.arange(4)[:, None, None]
    slot_c = jnp.arange(2)[None, :, None]
    slot_rank = jnp.arange(capacity)[None, None, :]
    z_ids = (zh + jnp.arange(4)) % 4
    served = (y * 4 + z_ids) * 2 + core
    slot_holder = (slot_y * 4 + zh) * 2 + slot_c
    slot_key = (slot_holder * capacity + slot_rank).reshape(-1)
    served_key = (all_holders * capacity + all_ranks)[served]
    hit = served_key[:, :, None] == slot_key[None, None, :]
    slot_units = jnp.sum(jnp.where(hit, all_units[served][:, :, None], 0), axis=1)
    offsets = (jnp.cumsum(slot_units, axis=1) - slot_units) * UNIT

    mine = lambda a: lax.dynamic_index_in_dim(a, group_id, 0, keepdims=False)
    my_holders, my_ranks, my_lengths, my_units = map(
        mine, (all_holders, all_ranks, all_lengths, all_units)
    )
    from_z = (zh - my_holders // 2 % 4) % 4
    my_order = (my_holders // 8 * 2 + my_holders % 2) * capacity + my_ranks
    ahead = (from_z[:, None] == from_z[None, :]) & (my_order[None, :] < my_order[:, None])
    my_start = jnp.sum(jnp.where(ahead, my_units[None, :], 0), axis=1) * UNIT

    def packing(size):
        limit = jnp.minimum(offsets, size).reshape(-1)
        places = jnp.concatenate([z_ids, limit]).astype(jnp.int32)
        starts = jnp.minimum(from_z * size + my_start, 4 * size)
        return places, starts.astype(jnp.int32)

    positions = my_lengths[:, None] + jnp.arange(span_len, dtype=jnp.int32)[None, :]
    channel = jnp.arange(head_dim)
    half = head_dim // 2
    frequency = ROPE_BASE ** (-(channel % half).astype(jnp.float32) * 2.0 / head_dim)
    angles = positions.reshape(-1).astype(jnp.float32)[:, None] * frequency
    cosine = jnp.cos(angles)
    sine = jnp.sin(angles) * jnp.where(channel < half, -1.0, 1.0)

    ids = block_ids()
    sides = (4, 4, 2, capacity, window, head_dim)
    places, starts = packing(PACKED)
    pieces = spread(span_rows)
    depth = o_weight.shape[0] // 2
    half = lax.dynamic_slice_in_dim(o_weight, core * depth, depth, 0)
    half, pieces[1] = lax.optimization_barrier((half, pieces[1]))
    twin_half = shift(half, "zl", 1)

    key_part = across_y(by_target(key_cache.reshape(sides)))
    gain = jnp.broadcast_to(norm_gain[:, None], (norm_gain.shape[0], head_dim))
    tables = (ids, places, starts, fits, gain, cosine, sine)
    value_slots, key_part, pieces[1:6], repeated, tables = lax.optimization_barrier(
        (by_target(value_cache.reshape(sides)), key_part, pieces[1:6], copies(half, twin_half), tables)
    )
    ids, places, starts, fits, gain, cosine, sine = tables
    value_part = across_y(value_slots)
    keys = across_z(pack(places, key_part, PACKED))
    value_part, keys[1], keys[3], pieces[6:], repeated = lax.optimization_barrier(
        (value_part, keys[1], keys[3], pieces[6:], repeated)
    )
    halves = lax.all_to_all(repeated, "x", 0, 0, tiled=True).reshape((blocks,) + half.shape)
    packed_values, pieces[0] = lax.optimization_barrier(
        (pack(places, value_part, PACKED), pieces[0])
    )
    values = across_z(packed_values)
    q, g, k, v = project(
        ids, pieces, gain, q_weight, gate_weight, k_weight, v_weight,
        q_norm_gain, k_norm_gain, cosine, sine,
    )

    size = 8 * capacity * window

    def packed(values, key_part, value_part, q, g, k, v, *weighed):
        return mix(starts, my_lengths, *weighed, values)

    def full(values, key_part, value_part, q, g, k, v, *weighed):
        places, starts = packing(size)
        keys, values = (across_z(pack(places, a, size)) for a in (key_part, value_part))
        weighed = weigh(starts, my_lengths, q, g, k, v, keys, window)
        return mix(starts, my_lengths, *weighed, values)

    weighed = weigh(starts, my_lengths, q, g, k, v, keys, window)
    attended = lax.cond(fits, packed, full, values, key_part, value_part, q, g, k, v, *weighed)
    halves, attended = lax.optimization_barrier((halves, attended))
    other_halves = shift(halves, "c", 1)
    heads = lax.all_to_all(
        attended.reshape(blocks, rows // blocks, attended.shape[1]), TENSOR, 0, 0, tiled=True
    )
    x_ids, zl_ids = jnp.arange(blocks) // 2, (lax.axis_index("zl") + jnp.arange(blocks)) % 2
    out_places = jnp.concatenate([zl_ids * 4 + x_ids, core[None]]).astype(jnp.int32)
    return project_out(out_places, heads, halves, other_halves)


def solution(mesh):
    mesh = Mesh(mesh.devices.reshape(4, 4, 2, 2, 4), GROUP + TENSOR)
    placed = (
        P(GROUP, TENSOR),
        P(),
        P(None, TENSOR),
        P(None, TENSOR),
        P(None, TENSOR),
        P(None, TENSOR),
        P(),
        P(),
        P(TENSOR, None),
        P(GROUP, None, None, TENSOR),
        P(GROUP, None, None, TENSOR),
        P(),
        P(),
    )
    return jax.shard_map(
        local, mesh=mesh, in_specs=placed, out_specs=P(GROUP + TENSOR, None), check_vma=False
    )
```

```python
import functools
import math

import jax
import jax.numpy as jnp
from jax import lax
from jax.experimental import pallas as pl
from jax.experimental.pallas import tpu as pltpu
from jax.sharding import Mesh
from jax.sharding import PartitionSpec as P

EPSILON = 1e-06
ROPE_BASE = 1000000.0
GROUP = ("y", "zh", "c")
TENSOR = ("zl", "x")
ROW_TILE = 256
BATCH = 4
MIX_BATCH = 8
UNIT = 16
PACKED = 66 * UNIT
LONG = pl.CostEstimate(flops=1 << 20, bytes_accessed=64 << 20, transcendentals=0)
COST = pl.CostEstimate(flops=1 << 20, bytes_accessed=1 << 20, transcendentals=0)


def ring(size, step):
    return [(i, (i + step) % size) for i in range(size)]


def shift(value, axis, step):
    return lax.ppermute(value, axis, ring(lax.axis_size(axis), step))


def spread(block):
    twin = shift(block, "zl", 1)
    below, above = shift(block, "x", 1), shift(block, "x", -1)
    twin_below, twin_above = shift(twin, "x", 1), shift(twin, "x", -1)
    far = shift(below, "x", 1)
    twin_far = shift(twin_above, "x", -1)
    return [block, twin, below, above, twin_below, twin_above, far, twin_far]


def block_ids():
    zl, x = lax.axis_index("zl"), lax.axis_index("x")
    pairs = [(0, 0), (1, 0), (0, 3), (0, 1), (1, 3), (1, 1), (0, 2), (1, 2)]
    return jnp.stack([((zl + dz) % 2) * 4 + (x + dx) % 4 for dz, dx in pairs]).astype(jnp.int32)


def head_norm_rotate(values, gain, cosine, sine):
    scale = lax.rsqrt(jnp.mean(values * values, axis=-1, keepdims=True) + EPSILON)
    scaled = values * scale * gain
    half = values.shape[-1] // 2
    return scaled * cosine + pltpu.roll(scaled, half, 1) * sine


def project_kernel(ids, *refs):
    pieces, rest = refs[:8], refs[8:]
    (gain, wq, wg, wk, wv, q_gain, k_gain, cosine, sine, q_out, g_out, k_out, v_out, scaled) = rest
    rows, width = pieces[0].shape
    head = wk.shape[1]
    edges = [0]
    for w in (wq, wg, wk, wv):
        edges.append(edges[-1] + w.shape[1])

    @pl.when(pl.program_id(0) == 0)
    def _():
        for j in range(8):
            block = pl.multiple_of(ids[j] * width, width)
            here = pl.ds(block, width)
            for w, first, last in zip((wq, wg, wk, wv), edges, edges[1:]):
                lanes = jnp.concatenate([gain[here, :]] * ((last - first) // head), axis=1)
                part = w[here, :].astype(jnp.float32) * lanes
                scaled[j * width : (j + 1) * width, first:last] = part.astype(jnp.bfloat16)

    total = jnp.zeros((rows, 128), jnp.float32)
    product = jnp.zeros((rows, edges[-1]), jnp.float32)
    for j, piece in enumerate(pieces):
        value = piece[...]
        product = product + jnp.dot(
            value, scaled[j * width : (j + 1) * width, :], preferred_element_type=jnp.float32
        )
        value = value.astype(jnp.float32)
        square = value * value
        for first in range(0, width, 128):
            total = total + square[:, first : first + 128]
    total = jnp.sum(total, axis=-1, keepdims=True)
    product = product * lax.rsqrt(total / (8 * width) + EPSILON)
    cos, sin = cosine[...], sine[...]
    for h in range(edges[1] // head):
        here = slice(h * head, (h + 1) * head)
        part = head_norm_rotate(product[:, here], q_gain[...], cos, sin)
        q_out[:, here] = part.astype(jnp.bfloat16)
    g_out[...] = jax.nn.sigmoid(product[:, edges[1] : edges[2]])
    k = head_norm_rotate(product[:, edges[2] : edges[3]], k_gain[...], cos, sin)
    k_out[...] = k.astype(jnp.bfloat16)
    v_out[...] = product[:, edges[3] : edges[4]].astype(jnp.bfloat16)


def project(ids, pieces, gain, wq, wg, wk, wv, q_gain, k_gain, cosine, sine):
    rows, width = pieces[0].shape
    depth = gain.shape[0]
    head = q_gain.shape[0]
    tile = lambda columns: pl.BlockSpec((ROW_TILE, columns), lambda i, _: (i, 0))
    whole = lambda a: pl.BlockSpec(a.shape, lambda i, _: (0, 0))
    q_gain, k_gain = q_gain.reshape(1, head), k_gain.reshape(1, head)
    constants = (gain, wq, wg, wk, wv, q_gain, k_gain)
    columns = sum(w.shape[1] for w in (wq, wg, wk, wv))
    return pl.pallas_call(
        project_kernel,
        out_shape=(
            jax.ShapeDtypeStruct((rows, wq.shape[1]), jnp.bfloat16),
            jax.ShapeDtypeStruct((rows, wg.shape[1]), jnp.float32),
            jax.ShapeDtypeStruct((rows, head), jnp.bfloat16),
            jax.ShapeDtypeStruct((rows, head), jnp.bfloat16),
        ),
        grid_spec=pltpu.PrefetchScalarGridSpec(
            num_scalar_prefetch=1,
            grid=(rows // ROW_TILE,),
            in_specs=[tile(width)] * 8 + [whole(a) for a in constants] + [tile(head)] * 2,
            out_specs=[tile(wq.shape[1]), tile(wg.shape[1]), tile(head), tile(head)],
            scratch_shapes=[pltpu.VMEM((depth, columns), jnp.bfloat16)],
        ),
        cost_estimate=COST,
        name="project",
    )(ids, *pieces, *constants, cosine, sine)


def gather_parts(parts, store):
    size = parts[0].shape[0]
    for j, part in enumerate(parts):
        store[j * size : (j + 1) * size, :] = part[...]
    slack = slice(len(parts) * size, store.shape[0])
    store[slack, :] = jnp.zeros((store.shape[0] - len(parts) * size, store.shape[1]), store.dtype)


def weigh_kernel(starts, lengths, q, g, k, v, *refs):
    parts, (weights, mixed_new, factor, keys) = refs[:4], refs[4:]
    head = k.shape[1]
    span = q.shape[0] // BATCH
    shares = q.shape[1] // head
    window = keys.shape[0] - 4 * parts[0].shape[0]
    score_scale = 1.0 / math.sqrt(head)
    contract = (((1,), (1,)), ((), ()))

    @pl.when(pl.program_id(0) == 0)
    def _():
        gather_parts(parts, keys)

    column = lax.broadcasted_iota(jnp.int32, (shares * span, window), 1)
    token = lax.broadcasted_iota(jnp.int32, (shares, span, window), 1)
    token = token.reshape(shares * span, window)
    together = window // span
    for b in range(BATCH):
        r = pl.program_id(0) * BATCH + b
        length = lengths[r]
        rows = slice(b * span, (b + 1) * span)
        first = b // together * together
        both = slice(first * span, (first + together) * span)
        own = column - (b - first) * span
        query = jnp.concatenate([q[rows, s * head : (s + 1) * head] for s in range(shares)], axis=0)
        old_keys = keys[pl.ds(pl.multiple_of(starts[r], UNIT), window), :]
        old = lax.dot_general(query, old_keys, contract, preferred_element_type=jnp.float32)
        new = lax.dot_general(query, k[both, :], contract, preferred_element_type=jnp.float32)
        old = jnp.where(column < length, old * score_scale, -jnp.inf)
        new = jnp.where((own >= 0) & (own <= token), new * score_scale, -jnp.inf)
        row_max = jnp.max(jnp.maximum(old, new), axis=-1, keepdims=True)
        old, new = jnp.exp(old - row_max), jnp.exp(new - row_max)
        row_total = jnp.sum(old + new, axis=-1, keepdims=True)
        weights[b * shares * span : (b + 1) * shares * span, :] = old.astype(jnp.bfloat16)
        mixed = jnp.dot(new.astype(jnp.bfloat16), v[both, :], preferred_element_type=jnp.float32)
        for s in range(shares):
            columns, here = slice(s * head, (s + 1) * head), slice(s * span, (s + 1) * span)
            mixed_new[rows, columns] = mixed[here]
            factor[rows, columns] = g[rows, columns] / row_total[here]


def weigh(starts, lengths, q, g, k, v, keys, window):
    rows, columns = q.shape
    head = k.shape[1]
    shares = columns // head
    step = rows // lengths.shape[0] * BATCH
    tile = lambda width: pl.BlockSpec((step, width), lambda i, *_: (i, 0))
    whole = lambda a: pl.BlockSpec(a.shape, lambda i, *_: (0, 0))
    return pl.pallas_call(
        weigh_kernel,
        out_shape=(
            jax.ShapeDtypeStruct((shares * rows, window), jnp.bfloat16),
            jax.ShapeDtypeStruct((rows, columns), jnp.float32),
            jax.ShapeDtypeStruct((rows, columns), jnp.float32),
        ),
        grid_spec=pltpu.PrefetchScalarGridSpec(
            num_scalar_prefetch=2,
            grid=(rows // step,),
            in_specs=[tile(columns)] * 2 + [tile(head)] * 2 + [whole(a) for a in keys],
            out_specs=(
                pl.BlockSpec((shares * step, window), lambda i, *_: (i, 0)),
                tile(columns),
                tile(columns),
            ),
            scratch_shapes=[pltpu.VMEM((4 * keys[0].shape[0] + window, head), keys[0].dtype)],
        ),
        compiler_params=pltpu.CompilerParams(vmem_limit_bytes=30 << 20),
        cost_estimate=COST,
        name="weigh",
    )(starts, lengths, q, g, k, v, *keys)


def mix_kernel(starts, lengths, weights, mixed_new, factor, *refs):
    parts, (out, values) = refs[:4], refs[4:]
    window, head = weights.shape[1], values.shape[1]
    span = out.shape[0] // MIX_BATCH
    shares = out.shape[1] // head

    @pl.when(pl.program_id(0) == 0)
    def _():
        gather_parts(parts, values)

    old_row = lax.broadcasted_iota(jnp.int32, (window, head), 0)
    for b in range(MIX_BATCH):
        r = pl.program_id(0) * MIX_BATCH + b
        rows = slice(b * span, (b + 1) * span)
        old_values = values[pl.ds(pl.multiple_of(starts[r], UNIT), window), :]
        old_values = jnp.where(old_row < lengths[r], old_values, jnp.zeros_like(old_values))
        old = weights[b * shares * span : (b + 1) * shares * span, :]
        mixed = jnp.dot(old, old_values, preferred_element_type=jnp.float32)
        for s in range(shares):
            columns, here = slice(s * head, (s + 1) * head), slice(s * span, (s + 1) * span)
            part = (mixed[here] + mixed_new[rows, columns]) * factor[rows, columns]
            out[rows, columns] = part.astype(jnp.bfloat16)


def mix(starts, lengths, weights, mixed_new, factor, values):
    rows, columns = factor.shape
    window, head = weights.shape[1], values[0].shape[1]
    step = rows // lengths.shape[0] * MIX_BATCH
    tile = lambda width: pl.BlockSpec((step, width), lambda i, *_: (i, 0))
    whole = lambda a: pl.BlockSpec(a.shape, lambda i, *_: (0, 0))
    return pl.pallas_call(
        mix_kernel,
        out_shape=jax.ShapeDtypeStruct((rows, columns), jnp.bfloat16),
        grid_spec=pltpu.PrefetchScalarGridSpec(
            num_scalar_prefetch=2,
            grid=(rows // step,),
            in_specs=[
                pl.BlockSpec((columns // head * step, window), lambda i, *_: (i, 0)),
                tile(columns),
                tile(columns),
            ]
            + [whole(a) for a in values],
            out_specs=tile(columns),
            scratch_shapes=[pltpu.VMEM((4 * values[0].shape[0] + window, head), values[0].dtype)],
        ),
        compiler_params=pltpu.CompilerParams(vmem_limit_bytes=30 << 20),
        cost_estimate=COST,
        name="mix",
    )(starts, lengths, weights, mixed_new, factor, *values)


def pack_kernel(offsets, cache, *refs):
    outs, store = refs[:4], refs[4]
    sources, _, slots, window, head = cache.shape
    size = outs[0].shape[0]
    for k, out in enumerate(outs):
        for j in range(sources * slots):
            place = pl.multiple_of(offsets[4 + k * sources * slots + j], UNIT)
            store[pl.ds(place, window), :] = cache[j // slots, offsets[k], j % slots]
        out[...] = store[:size, :]


def pack(offsets, cache, size):
    window, head = cache.shape[3:]
    return pl.pallas_call(
        pack_kernel,
        out_shape=[jax.ShapeDtypeStruct((size, head), cache.dtype)] * 4,
        grid_spec=pltpu.PrefetchScalarGridSpec(
            num_scalar_prefetch=1,
            grid=(1,),
            in_specs=[pl.BlockSpec(cache.shape, lambda i, _: (0,) * 5)],
            out_specs=[pl.BlockSpec((size, head), lambda i, _: (0, 0))] * 4,
            scratch_shapes=[pltpu.VMEM((size + window, head), cache.dtype)],
        ),
        compiler_params=pltpu.CompilerParams(vmem_limit_bytes=16 << 20),
        cost_estimate=COST,
        name="pack",
    )(offsets, cache)


def by_target_kernel(source, target):
    for c in range(2):
        target[0, c] = source[0, :, c]


def by_target(cache):
    ny, nz, nc, capacity, window, head = cache.shape
    return pl.pallas_call(
        by_target_kernel,
        out_shape=jax.ShapeDtypeStruct((ny, nc, nz, capacity, window, head), cache.dtype),
        grid=(ny,),
        in_specs=[pl.BlockSpec((1, nz, nc, capacity, window, head), lambda i: (i, 0, 0, 0, 0, 0))],
        out_specs=pl.BlockSpec((1, nc, nz, capacity, window, head), lambda i: (i, 0, 0, 0, 0, 0)),
        compiler_params=pltpu.CompilerParams(vmem_limit_bytes=12 << 20),
        cost_estimate=LONG,
        name="by_target",
    )(cache)


def copies_kernel(half, twin, out):
    out[0, 0], out[0, 1] = half[...], twin[...]


def copies(half, twin):
    depth, columns = half.shape
    whole = pl.BlockSpec((depth, columns), lambda i: (0, 0))
    return pl.pallas_call(
        copies_kernel,
        out_shape=jax.ShapeDtypeStruct((4, 2, depth, columns), half.dtype),
        grid=(4,),
        in_specs=[whole, whole],
        out_specs=pl.BlockSpec((1, 2, depth, columns), lambda i: (i, 0, 0, 0)),
        compiler_params=pltpu.CompilerParams(vmem_limit_bytes=12 << 20),
        cost_estimate=COST,
        name="copies",
    )(half, twin)


def output_kernel(places, heads, mine, other, out, joined):
    count, depth = mine.shape[:2]

    @pl.when(pl.program_id(0) == 0)
    def _():
        for j in range(count):
            for h in range(2):
                first = pl.multiple_of((places[count] + h) % 2 * depth, depth)
                columns = slice((2 * j + h) * depth, (2 * j + h + 1) * depth)
                joined[:, columns] = heads[places[j], :, pl.ds(first, depth)]

    total = jnp.zeros(out.shape, jnp.float32)
    for j in range(count):
        weight = jnp.concatenate([mine[j], other[j]], axis=0)
        part = joined[:, 2 * j * depth : 2 * (j + 1) * depth]
        total = total + jnp.dot(part, weight, preferred_element_type=jnp.float32)
    out[...] = total.astype(jnp.bfloat16)


def project_out(places, heads, mine, other):
    blocks, rows, width = heads.shape
    depth, columns = mine.shape[1:]
    tile = 512
    half = pl.BlockSpec((blocks, depth, tile), lambda i, _: (0, 0, i))
    return pl.pallas_call(
        output_kernel,
        out_shape=jax.ShapeDtypeStruct((rows, columns), jnp.bfloat16),
        grid_spec=pltpu.PrefetchScalarGridSpec(
            num_scalar_prefetch=1,
            grid=(columns // tile,),
            in_specs=[pl.BlockSpec(heads.shape, lambda i, _: (0, 0, 0)), half, half],
            out_specs=pl.BlockSpec((rows, tile), lambda i, _: (0, i)),
            scratch_shapes=[pltpu.VMEM((rows, blocks * width), jnp.bfloat16)],
        ),
        compiler_params=pltpu.CompilerParams(vmem_limit_bytes=30 << 20),
        cost_estimate=COST,
        name="project_out",
    )(places, heads, mine, other)


def across_y(slots):
    ny, nc, nz, capacity, window, head = slots.shape
    flat = slots.reshape(ny * nc, nz * capacity * window, head)
    flat = lax.all_to_all(flat, ("y", "c"), 0, 0, tiled=True)
    return flat.reshape(ny * nc, nz, capacity, window, head)


def across_z(parts):
    return [parts[0]] + [shift(parts[k], "zh", k) for k in range(1, 4)]


def local(
    span_rows,
    norm_gain,
    q_weight,
    gate_weight,
    k_weight,
    v_weight,
    q_norm_gain,
    k_norm_gain,
    o_weight,
    key_cache,
    value_cache,
    holders,
    prefix_lengths,
):
    groups = lax.axis_size(GROUP)
    group_id = lax.axis_index(GROUP)
    requests = prefix_lengths.shape[0] // groups
    rows = span_rows.shape[0]
    span_len = rows // requests
    head_dim = q_norm_gain.shape[0]
    capacity = key_cache.shape[1] // groups
    window = key_cache.shape[2]
    blocks = lax.axis_size(TENSOR)

    y, zh, core = lax.axis_index("y"), lax.axis_index("zh"), lax.axis_index("c")
    all_holders = holders.reshape(groups, requests)
    all_lengths = prefix_lengths.reshape(groups, requests)
    order = jnp.arange(requests)
    earlier = order[None, :] < order[:, None]
    same = all_holders[:, :, None] == all_holders[:, None, :]
    all_ranks = jnp.sum(same & earlier[None], axis=2)
    all_units = (all_lengths + UNIT - 1) // UNIT
    plane = all_holders // 2 % 4
    per_plane = jnp.sum(
        jnp.where(plane[:, :, None] == jnp.arange(4), all_units[:, :, None], 0), axis=1
    )
    fits = jnp.max(per_plane) * UNIT <= PACKED

    slot_y = jnp.arange(4)[:, None, None]
    slot_c = jnp.arange(2)[None, :, None]
    slot_rank = jnp.arange(capacity)[None, None, :]
    z_ids = (zh + jnp.arange(4)) % 4
    served = (y * 4 + z_ids) * 2 + core
    slot_holder = (slot_y * 4 + zh) * 2 + slot_c
    slot_key = (slot_holder * capacity + slot_rank).reshape(-1)
    served_key = (all_holders * capacity + all_ranks)[served]
    hit = served_key[:, :, None] == slot_key[None, None, :]
    slot_units = jnp.sum(jnp.where(hit, all_units[served][:, :, None], 0), axis=1)
    offsets = (jnp.cumsum(slot_units, axis=1) - slot_units) * UNIT

    mine = lambda a: lax.dynamic_index_in_dim(a, group_id, 0, keepdims=False)
    my_holders, my_ranks, my_lengths, my_units = map(
        mine, (all_holders, all_ranks, all_lengths, all_units)
    )
    from_z = (zh - my_holders // 2 % 4) % 4
    my_order = (my_holders // 8 * 2 + my_holders % 2) * capacity + my_ranks
    ahead = (from_z[:, None] == from_z[None, :]) & (my_order[None, :] < my_order[:, None])
    my_start = jnp.sum(jnp.where(ahead, my_units[None, :], 0), axis=1) * UNIT

    def packing(size):
        limit = jnp.minimum(offsets, size).reshape(-1)
        places = jnp.concatenate([z_ids, limit]).astype(jnp.int32)
        starts = jnp.minimum(from_z * size + my_start, 4 * size)
        return places, starts.astype(jnp.int32)

    positions = my_lengths[:, None] + jnp.arange(span_len, dtype=jnp.int32)[None, :]
    channel = jnp.arange(head_dim)
    half = head_dim // 2
    frequency = ROPE_BASE ** (-(channel % half).astype(jnp.float32) * 2.0 / head_dim)
    angles = positions.reshape(-1).astype(jnp.float32)[:, None] * frequency
    cosine = jnp.cos(angles)
    sine = jnp.sin(angles) * jnp.where(channel < half, -1.0, 1.0)

    ids = block_ids()
    sides = (4, 4, 2, capacity, window, head_dim)
    places, starts = packing(PACKED)
    pieces = spread(span_rows)
    depth = o_weight.shape[0] // 2
    half = lax.dynamic_slice_in_dim(o_weight, core * depth, depth, 0)
    gain = jnp.broadcast_to(norm_gain[:, None], (norm_gain.shape[0], head_dim))
    half, pieces[1], gain = lax.optimization_barrier((half, pieces[1], gain))
    twin_half = shift(half, "zl", 1)

    key_part = across_y(by_target(key_cache.reshape(sides)))
    tables = (ids, places, starts, fits, gain, cosine, sine)
    value_slots, key_part, pieces[1:6], repeated, tables = lax.optimization_barrier(
        (by_target(value_cache.reshape(sides)), key_part, pieces[1:6], copies(half, twin_half), tables)
    )
    ids, places, starts, fits, gain, cosine, sine = tables
    value_part = across_y(value_slots)
    keys = across_z(pack(places, key_part, PACKED))
    value_part, keys[1], keys[3], pieces[6:], repeated = lax.optimization_barrier(
        (value_part, keys[1], keys[3], pieces[6:], repeated)
    )
    halves = lax.all_to_all(repeated, "x", 0, 0, tiled=True).reshape((blocks,) + half.shape)
    packed_values, pieces[0] = lax.optimization_barrier(
        (pack(places, value_part, PACKED), pieces[0])
    )
    values = across_z(packed_values)
    q, g, k, v = project(
        ids, pieces, gain, q_weight, gate_weight, k_weight, v_weight,
        q_norm_gain, k_norm_gain, cosine, sine,
    )

    size = 8 * capacity * window

    def packed(values, key_part, value_part, q, g, k, v, *weighed):
        return mix(starts, my_lengths, *weighed, values)

    def full(values, key_part, value_part, q, g, k, v, *weighed):
        places, starts = packing(size)
        keys, values = (across_z(pack(places, a, size)) for a in (key_part, value_part))
        weighed = weigh(starts, my_lengths, q, g, k, v, keys, window)
        return mix(starts, my_lengths, *weighed, values)

    weighed = weigh(starts, my_lengths, q, g, k, v, keys, window)
    attended = lax.cond(fits, packed, full, values, key_part, value_part, q, g, k, v, *weighed)
    halves, attended = lax.optimization_barrier((halves, attended))
    other_halves = shift(halves, "c", 1)
    heads = lax.all_to_all(
        attended.reshape(blocks, rows // blocks, attended.shape[1]), TENSOR, 0, 0, tiled=True
    )
    x_ids, zl_ids = jnp.arange(blocks) // 2, (lax.axis_index("zl") + jnp.arange(blocks)) % 2
    out_places = jnp.concatenate([zl_ids * 4 + x_ids, core[None]]).astype(jnp.int32)
    return project_out(out_places, heads, halves, other_halves)


def solution(mesh):
    mesh = Mesh(mesh.devices.reshape(4, 4, 2, 2, 4), GROUP + TENSOR)
    placed = (
        P(GROUP, TENSOR),
        P(),
        P(None, TENSOR),
        P(None, TENSOR),
        P(None, TENSOR),
        P(None, TENSOR),
        P(),
        P(),
        P(TENSOR, None),
        P(GROUP, None, None, TENSOR),
        P(GROUP, None, None, TENSOR),
        P(),
        P(),
    )
    return jax.shard_map(
        local, mesh=mesh, in_specs=placed, out_specs=P(GROUP + TENSOR, None), check_vma=False
    )
```
